32 devices in a mesh: dp: 2 (over x), hst: 4 (over y, core), chip: 4 (over z).
Axes of the slice: x: 2, y: 2, z: 4, core: 2. Of those that a mesh axis runs over, the one named last changes fastest.
Arguments:
- tokens: bfloat16 [512, 8192], P('dp', ('hst', 'chip')), may hold values from -6 to 6
- out_grad: bfloat16 [512, 8192], P('dp', ('hst', 'chip')), may hold values from -6 to 6
- up_blocks: bfloat16 [112, 16, 128, 128], P(('hst', 'chip')), may hold values from -0.125 to 0.125
- up_cols: int32 [112, 16], P(('hst', 'chip')), may hold values from 0 to 63, all different within a row
- down_blocks: bfloat16 [112, 16, 128, 128], P(('hst', 'chip')), may hold values from -0.09375 to 0.09375
- down_cols: int32 [112, 16], P(('hst', 'chip')), may hold values from 0 to 63, all different within a row
Outputs:
- input_grad: bfloat16 [512, 8192], P('dp', ('hst', 'chip'))
- up_grad: float32 [112, 16, 128, 128], P(('hst', 'chip'), None, 'dp')
- down_grad: float32 [112, 16, 128, 128], P(('hst', 'chip'), None, 'dp')
The draws below stay inside these ranges and needn't reach their ends.
Inputs may be any that keep to these rules, and one draw needn't show every extreme that they name: `up_cols`: each block row names 16 different block columns; every block column is named by some row. `down_cols`: each block row names 16 different block columns; every block column is named by some row.
All inputs are finite; a program needn't handle non-finite values.
Results may differ from the reference program's by a relative error of at most 0.017.
Values may be sent and summed in bfloat16 or wider, within the bound.
A program may use at most 128 MiB of HBM per device.

```python
import jax
import jax.numpy as jnp
from jax import lax

D = 8192
FF = 14336
BLK = 128
K = 16
TOK_DEV = 256
TOKENS = 512
HB = 112
N_DP = 2
N_HST = 4
N_CHIP = 4


def level_of(rng, shape, cuts, smallest, largest):
    level, own = 1.0, jax.random.fold_in(rng, 6)
    for position, parts in cuts:
        heights = jnp.exp(jax.random.uniform(jax.random.fold_in(own, position), (parts,), jnp.float32, smallest / len(cuts), largest / len(cuts)))
        level = level * jnp.repeat(heights, shape[position] // parts).reshape([-1 if axis == position else 1 for axis in range(len(shape))])
    return level


def different_ones(own_key, rows, amount, top, lift):
    ranking = jax.random.permutation(jax.random.fold_in(own_key, 1), amount)
    boost = ranking
    for power in range(3):
        boost = boost * boost // amount
    boost = boost * lift // amount
    chance = jax.random.randint(jax.random.fold_in(own_key, 2), (rows, amount), 0, 4096) + boost
    fixed_rows = jax.random.permutation(jax.random.fold_in(own_key, 3), rows)[jnp.arange(amount) % rows]
    chance = jnp.where(jnp.arange(rows)[:, None] == fixed_rows[None, :], 1 << 14, chance)
    score = chance * amount + jnp.arange(amount)
    return lax.top_k(score.astype(jnp.int32), top)[1].astype(jnp.int32)


def bell_draw(own_key, shape, deviation, bound, pieces=(), kind=jnp.bfloat16):
    values = jax.random.normal(own_key, shape, jnp.float32) * deviation
    if len(pieces) > 0:
        values = level_of(own_key, shape, pieces, -0.22, 0.18) * values
    return jnp.clip(values, min=-bound, max=bound).astype(kind)


def setup_inputs(seed: int = 0) -> dict:
    seeds = jax.random.split(jax.random.key(seed), 7)
    return {
        "tokens": bell_draw(seeds[0], (TOKENS, D), 1.0, 6.0, ((0, 2), (1, 16))),
        "out_grad": bell_draw(seeds[1], (TOKENS, D), 1.0, 6.0, ((0, 2), (1, 16))),
        "up_blocks": bell_draw(seeds[2], (HB, K, BLK, BLK), (K * BLK) ** -0.5, 0.125, ((0, 16),)),
        "up_cols": different_ones(seeds[3], HB, D // BLK, K, 4096),
        "down_blocks": bell_draw(seeds[4], (HB, K, BLK, BLK), (FF // 4) ** -0.5, 0.09375, ((0, 16),)),
        "down_cols": different_ones(seeds[5], HB, D // BLK, K, 4096),
    }


def reference(tokens, out_grad, up_blocks, up_cols, down_blocks, down_cols):
    dblocks = D // BLK
    shards = N_HST * N_CHIP
    rows_each = HB // shards
    x_blocks = tokens.reshape(N_DP, TOK_DEV, dblocks, BLK)
    dy_blocks = out_grad.reshape(N_DP, TOK_DEV, dblocks, BLK)
    columns = jnp.arange(dblocks, dtype=jnp.int32)

    def row_step(carried, per_row):
        up_row, up_idx, down_row, down_idx = per_row
        x_sel = x_blocks[:, :, up_idx, :].astype(jnp.float32)
        dy_sel = dy_blocks[:, :, down_idx, :].astype(jnp.float32)
        up_f = up_row.astype(jnp.float32)
        down_f = down_row.astype(jnp.float32)
        pre_act = jnp.einsum('gtkc,khc->gth', x_sel, up_f)
        activated = jax.nn.silu(pre_act).astype(jnp.bfloat16)
        down_part = jnp.einsum('gth,gtkc->gkhc', activated.astype(jnp.float32), dy_sel).astype(jnp.bfloat16)
        down_part = lax.optimization_barrier(down_part)
        down_sum = jnp.sum(down_part.astype(jnp.float32), axis=0)
        hidden_grad = jnp.einsum('gtkc,khc->gth', dy_sel, down_f)
        sigmoid_pre = jax.nn.sigmoid(pre_act)
        pre_grad = (hidden_grad * sigmoid_pre * (1.0 + pre_act * (1.0 - sigmoid_pre))).astype(jnp.bfloat16)
        pre_float = pre_grad.astype(jnp.float32)
        up_part = jnp.einsum('gth,gtkc->gkhc', pre_float, x_sel).astype(jnp.bfloat16)
        up_part = lax.optimization_barrier(up_part)
        up_sum = jnp.sum(up_part.astype(jnp.float32), axis=0)
        contrib = jnp.einsum('gth,khc->gtkc', pre_float, up_f).reshape(TOKENS, K, BLK)
        onehot = (up_idx[:, None] == columns[None, :]).astype(jnp.float32)
        carried = carried + jnp.einsum('tkc,kb->tbc', contrib, onehot, precision=lax.Precision.HIGHEST)
        return carried, (up_sum, down_sum)

    def shard_step(total, per_shard):
        start = jnp.zeros((TOKENS, dblocks, BLK), jnp.float32)
        partial_value, grads = lax.scan(row_step, start, per_shard)
        rounded = lax.optimization_barrier(partial_value.astype(jnp.bfloat16))
        return total + rounded.astype(jnp.float32), grads

    grouped = (up_blocks.reshape(shards, rows_each, K, BLK, BLK),
               up_cols.astype(jnp.int32).reshape(shards, rows_each, K),
               down_blocks.reshape(shards, rows_each, K, BLK, BLK),
               down_cols.astype(jnp.int32).reshape(shards, rows_each, K))
    begin = jnp.zeros((TOKENS, dblocks, BLK), jnp.float32)
    total, grads = lax.scan(shard_step, begin, grouped)
    input_grad = total.reshape(TOKENS, D).astype(jnp.bfloat16)
    up_grad = grads[0].reshape(HB, K, BLK, BLK)
    down_grad = grads[1].reshape(HB, K, BLK, BLK)
    return input_grad, up_grad, down_grad
```

```python
import functools

import jax
import jax.numpy as jnp
from jax import lax
from jax.experimental import pallas as pl
from jax.experimental.pallas import tpu as pltpu
from jax.sharding import PartitionSpec as P

NT = (((1,), (1,)), ((), ()))


def rows_kernel(
    split,
    up_cols,
    down_cols,
    me,
    x_ref,
    dy_ref,
    up_ref,
    down_ref,
    in_ref,
    *rest,
):
    outs, (acc, xs, dys, us, ds) = rest[:-5], rest[-5:]
    row = pl.program_id(0)
    width = up_ref.shape[-1]
    per_shard = x_ref.shape[2] // width
    count = up_ref.shape[1]

    @pl.when(row == 0)
    def _():
        acc[...] = jnp.zeros_like(acc)

    def place(col):
        return col // per_shard, pl.ds(pl.multiple_of((col % per_shard) * width, width), width)

    for k in range(count):
        lanes = pl.ds(k * width, width)
        shard, at = place(up_cols[row, k])
        xs[:, lanes] = x_ref[shard, :, at]
        shard, at = place(down_cols[row, k])
        dys[:, lanes] = dy_ref[shard, :, at]
        us[:, lanes] = up_ref[0, k]
        ds[:, lanes] = down_ref[0, k]
    pre = lax.dot_general(us[...], xs[...], NT, preferred_element_type=jnp.float32)
    hid = lax.dot_general(ds[...], dys[...], NT, preferred_element_type=jnp.float32)
    sig = 1.0 / (1.0 + jnp.exp(-pre))
    act = (pre * sig).astype(jnp.bfloat16)
    pre_grad_f = hid * sig * (1.0 + pre * (1.0 - sig))
    pre_grad = pre_grad_f.astype(jnp.bfloat16)
    pre_grad_t = pre_grad_f.T.astype(jnp.bfloat16)

    step = 4
    for base in range(0, count, step):
        lanes = pl.ds(base * width, step * width)
        up_part = jnp.dot(pre_grad, xs[:, lanes], preferred_element_type=jnp.float32)
        down_part = jnp.dot(act, dys[:, lanes], preferred_element_type=jnp.float32)
        back = jnp.dot(pre_grad_t, us[:, lanes], preferred_element_type=jnp.float32)
        for i in range(step):
            k = base + i
            cut = slice(i * width, (i + 1) * width)
            for part, out in ((up_part, outs[: len(outs) // 2]), (down_part, outs[len(outs) // 2 :])):
                block = part[:, cut].astype(jnp.bfloat16)
                if split:
                    half = width // 2
                    first = me[0] == 0
                    out[0][0, k] = jnp.where(first, block[:half], block[half:])
                    out[1][0, k] = jnp.where(first, block[half:], block[:half])
                else:
                    out[0][0, k] = block
            shard, at = place(up_cols[row, k])
            acc[shard, :, at] += back[:, cut]

    @pl.when(row == pl.num_programs(0) - 1)
    def _():
        for s in range(acc.shape[0]):
            in_ref[s] = acc[s].astype(jnp.bfloat16)


def rows_call(split, whole_x, whole_dy, up_blocks, up_cols, down_blocks, down_cols):
    rows, count, width, _ = up_blocks.shape
    shards, tok, part = whole_x.shape
    out_h = width // 2 if split else width
    n_out = 4 if split else 2
    whole = pl.BlockSpec(memory_space=pltpu.VMEM)
    smem = pl.BlockSpec(memory_space=pltpu.SMEM)

    def block(h):
        return pl.BlockSpec((1, count, h, width), lambda r: (r, 0, 0, 0))

    me = lax.axis_index("dp").astype(jnp.int32).reshape(1)
    flops = 10 * tok * rows * count * width * width
    return pl.pallas_call(
        functools.partial(rows_kernel, split),
        grid=(rows,),
        in_specs=[smem, smem, smem, whole, whole, block(width), block(width)],
        out_specs=[whole] + [block(out_h)] * n_out,
        out_shape=[jax.ShapeDtypeStruct(whole_x.shape, jnp.bfloat16)]
        + [jax.ShapeDtypeStruct((rows, count, out_h, width), jnp.bfloat16)] * n_out,
        scratch_shapes=[
            pltpu.VMEM(whole_x.shape, jnp.float32),
            pltpu.VMEM((tok, count * width), jnp.bfloat16),
            pltpu.VMEM((tok, count * width), jnp.bfloat16),
            pltpu.VMEM((width, count * width), jnp.bfloat16),
            pltpu.VMEM((width, count * width), jnp.bfloat16),
        ],
        compiler_params=pltpu.CompilerParams(
            dimension_semantics=("arbitrary",), vmem_limit_bytes=56 * 2**20
        ),
        cost_estimate=pl.CostEstimate(
            flops=flops, bytes_accessed=30 * 2**20, transcendentals=rows * width * tok
        ),
    )(up_cols, down_cols, me, whole_x, whole_dy, up_blocks, down_blocks)


MESH = pl.DeviceIdType.MESH
ALONG_UP, ALONG_DOWN, ACROSS, SIDE = range(4)


def gather_kernel(n_chip, x_ref, dy_ref, x_out, dy_out, send_sem, recv_sem, own_sem):
    hst, z = lax.axis_index("hst"), lax.axis_index("chip")
    far, c = hst // 2, hst % 2
    own = hst * n_chip + z
    ins, outs = (x_ref, dy_ref), (x_out, dy_out)
    not_last, not_first = z < n_chip - 1, z > 0
    peers = {
        ALONG_UP: {"hst": hst, "chip": (z + 1) % n_chip},
        ALONG_DOWN: {"hst": hst, "chip": (z + n_chip - 1) % n_chip},
        ACROSS: {"hst": (1 - far) * 2 + c, "chip": z},
        SIDE: {"hst": far * 2 + 1 - c, "chip": z},
    }

    barrier = pltpu.get_barrier_semaphore()

    def greet(way):
        pl.semaphore_signal(barrier, inc=1, device_id=peers[way], device_id_type=MESH)

    greet(ACROSS)
    greet(SIDE)
    pl.when(not_last)(lambda: greet(ALONG_UP))
    pl.when(not_first)(lambda: greet(ALONG_DOWN))
    inner = jnp.logical_and(not_last, not_first)
    pl.when(inner)(lambda: pl.semaphore_wait(barrier, 4))
    pl.when(jnp.logical_not(inner))(lambda: pl.semaphore_wait(barrier, 3))

    def copy(a, way, shard, source=None):
        return pltpu.make_async_remote_copy(
            src_ref=outs[a].at[shard] if source is None else source,
            dst_ref=outs[a].at[shard],
            send_sem=send_sem.at[a, way, shard],
            recv_sem=recv_sem.at[a, shard],
            device_id=peers[way],
            device_id_type=MESH,
        )

    def each(act):
        for t in range(n_chip + 1):
            for a in range(2):
                if t == 0:
                    act(a, (), own, None, True)
                elif t < n_chip:
                    below = z - t
                    act(a, (ALONG_UP,), hst * n_chip + below, below >= 0, False)
                    above = z + t
                    act(a, (ALONG_DOWN,), hst * n_chip + above, above < n_chip, False)
            for a in range(2):
                if t >= 1:
                    base = ((1 - far) * 2 + c) * n_chip
                    if t == 1:
                        act(a, None, base + z, None, False)
                    else:
                        act(a, None, base + z - (t - 1), z - (t - 1) >= 0, False)
                        act(a, None, base + z + (t - 1), z + (t - 1) < n_chip, False)

    def guarded(condition, run):
        if condition is None:
            run()
        else:
            pl.when(condition)(run)

    def forward(a, ways, shard, condition, is_own):
        def run():
            if not is_own:
                copy(a, SIDE, shard).wait_recv()
            source = ins[a] if is_own else None
            if ways is not None:
                if is_own or ALONG_UP in ways:
                    pl.when(not_last)(lambda: copy(a, ALONG_UP, shard, source).start())
                if is_own or ALONG_DOWN in ways:
                    pl.when(not_first)(lambda: copy(a, ALONG_DOWN, shard, source).start())
                copy(a, ACROSS, shard, source).start()
            copy(a, SIDE, shard, source).start()

        guarded(condition, run)

    def finish(a, ways, shard, condition, is_own):
        def run():
            source = ins[a] if is_own else None
            if ways is not None:
                if is_own or ALONG_UP in ways:
                    pl.when(not_last)(lambda: copy(a, ALONG_UP, shard, source).wait_send())
                if is_own or ALONG_DOWN in ways:
                    pl.when(not_first)(lambda: copy(a, ALONG_DOWN, shard, source).wait_send())
                copy(a, ACROSS, shard, source).wait_send()
            copy(a, SIDE, shard, source).wait_send()

        guarded(condition, run)

    each(forward)
    mine = [pltpu.make_async_copy(ins[a], outs[a].at[own], own_sem.at[a]) for a in range(2)]
    for m in mine:
        m.start()
    for half in range(2):
        for place in range(n_chip):
            for a in range(2):
                copy(a, SIDE, (half * 2 + 1 - c) * n_chip + place).wait_recv()
    each(finish)
    for m in mine:
        m.wait()


def gather_call(n_hst, n_chip, tokens, out_grad):
    if n_hst != 4:
        return [
            lax.all_gather(v, ("hst", "chip"), axis=0, tiled=False) for v in (tokens, out_grad)
        ]
    shards = n_hst * n_chip
    return pl.pallas_call(
        functools.partial(gather_kernel, n_chip),
        in_specs=[pl.BlockSpec(memory_space=pltpu.VMEM)] * 2,
        out_specs=[pl.BlockSpec(memory_space=pl.ANY)] * 2,
        out_shape=[jax.ShapeDtypeStruct((shards, *v.shape), v.dtype) for v in (tokens, out_grad)],
        scratch_shapes=[
            pltpu.SemaphoreType.DMA((2, 4, shards)),
            pltpu.SemaphoreType.DMA((2, shards)),
            pltpu.SemaphoreType.DMA((2,)),
        ],
        compiler_params=pltpu.CompilerParams(collective_id=0, has_side_effects=True),
    )(tokens, out_grad)


def scatter_kernel(n_chip, part, out, side, cross, up, down, cross_out, line_out, send_sem, recv_sem):
    hst, z = lax.axis_index("hst"), lax.axis_index("chip")
    far, c = hst // 2, hst % 2
    not_last, not_first = z < n_chip - 1, z > 0
    peers = {
        ALONG_UP: {"hst": hst, "chip": (z + 1) % n_chip},
        ALONG_DOWN: {"hst": hst, "chip": (z + n_chip - 1) % n_chip},
        ACROSS: {"hst": (1 - far) * 2 + c, "chip": z},
        SIDE: {"hst": far * 2 + 1 - c, "chip": z},
    }
    barrier = pltpu.get_barrier_semaphore()

    def greet(way):
        pl.semaphore_signal(barrier, inc=1, device_id=peers[way], device_id_type=MESH)

    greet(ACROSS)
    greet(SIDE)
    pl.when(not_last)(lambda: greet(ALONG_UP))
    pl.when(not_first)(lambda: greet(ALONG_DOWN))
    inner = jnp.logical_and(not_last, not_first)
    pl.when(inner)(lambda: pl.semaphore_wait(barrier, 4))
    pl.when(jnp.logical_not(inner))(lambda: pl.semaphore_wait(barrier, 3))

    def copy(way, source, target, slot):
        return pltpu.make_async_remote_copy(
            src_ref=source,
            dst_ref=target,
            send_sem=send_sem.at[way, slot],
            recv_sem=recv_sem.at[way, slot],
            device_id=peers[way],
            device_id_type=MESH,
        )

    def side_copy(half, place):
        slot = half * n_chip + place
        return copy(SIDE, part.at[(half * 2 + 1 - c) * n_chip + place], side.at[slot], slot)

    def cross_copy(place):
        return copy(ACROSS, cross_out.at[place], cross.at[place], place)

    def up_copy(place):
        return copy(ALONG_UP, line_out.at[place], up.at[place], place)

    def down_copy(place):
        return copy(ALONG_DOWN, line_out.at[place], down.at[place], place)

    def each(act):
        for t in range(n_chip - 1, 0, -1):
            pl.when(z + t < n_chip)(lambda t=t: act(z + t, 1))
            pl.when(z - t >= 0)(lambda t=t: act(z - t, -1))
        act(z, 0)

    rows = part.shape[1]
    chunk = 32 if rows % 32 == 0 else rows

    def total(store, terms):
        def body(i, carry):
            at = pl.ds(pl.multiple_of(i * chunk, chunk), chunk)
            value = None
            for ref, slot in terms:
                term = ref[slot, at, :].astype(jnp.float32)
                value = term if value is None else value + term
            store(at, value.astype(jnp.bfloat16))
            return carry

        lax.fori_loop(0, rows // chunk, body, 0)

    def to(ref, slot):
        def store(at, value):
            ref[slot, at, :] = value

        return store

    def to_out(at, value):
        out[at, :] = value

    each(lambda place, _: side_copy(1 - far, place).start())
    each(lambda place, _: side_copy(far, place).start())

    def cross_step(place, _):
        slot = (1 - far) * n_chip + place
        side_copy(1 - far, place).wait_recv()
        total(to(cross_out, place), [(part, ((1 - far) * 2 + c) * n_chip + place), (side, slot)])
        cross_copy(place).start()

    each(cross_step)

    def line_step(place, sign):
        slot = far * n_chip + place
        side_copy(far, place).wait_recv()
        cross_copy(place).wait_recv()
        base = [(part, (far * 2 + c) * n_chip + place), (side, slot), (cross, place)]
        if sign > 0:

            @pl.when(not_first)
            def _():
                up_copy(place).wait_recv()
                total(to(line_out, place), base + [(up, place)])

            @pl.when(jnp.logical_not(not_first))
            def _():
                total(to(line_out, place), base)

            up_copy(place).start()
        elif sign < 0:

            @pl.when(not_last)
            def _():
                down_copy(place).wait_recv()
                total(to(line_out, place), base + [(down, place)])

            @pl.when(jnp.logical_not(not_last))
            def _():
                total(to(line_out, place), base)

            down_copy(place).start()
        else:

            @pl.when(inner)
            def _():
                up_copy(place).wait_recv()
                down_copy(place).wait_recv()
                total(to_out, base + [(up, place), (down, place)])

            @pl.when(jnp.logical_not(not_first))
            def _():
                down_copy(place).wait_recv()
                total(to_out, base + [(down, place)])

            @pl.when(jnp.logical_not(not_last))
            def _():
                up_copy(place).wait_recv()
                total(to_out, base + [(up, place)])

    each(line_step)

    def finish(place, sign):
        side_copy(1 - far, place).wait_send()
        side_copy(far, place).wait_send()
        cross_copy(place).wait_send()
        if sign > 0:
            up_copy(place).wait_send()
        elif sign < 0:
            down_copy(place).wait_send()

    each(finish)


def scatter_call(n_hst, n_chip, part):
    if n_hst != 4 or n_chip < 2:
        return lax.psum_scatter(part, ("hst", "chip"), scatter_dimension=0, tiled=False)
    shards, rows, width = part.shape
    whole = pl.BlockSpec(memory_space=pltpu.VMEM)

    def slots(count):
        return pltpu.VMEM((count, rows, width), jnp.bfloat16)

    return pl.pallas_call(
        functools.partial(scatter_kernel, n_chip),
        in_specs=[whole],
        out_specs=whole,
        out_shape=jax.ShapeDtypeStruct((rows, width), jnp.bfloat16),
        scratch_shapes=[slots(2 * n_chip)]
        + [slots(n_chip)] * 5
        + [pltpu.SemaphoreType.DMA((4, 2 * n_chip))] * 2,
        compiler_params=pltpu.CompilerParams(
            collective_id=1, has_side_effects=True, vmem_limit_bytes=24 * 2**20
        ),
        cost_estimate=pl.CostEstimate(
            flops=shards * rows * width, bytes_accessed=120 * 2**20, transcendentals=0
        ),
    )(part)

PAIR, MATE = 4, 5


def fused_kernel(
    n_chip,
    inv,
    up_cols,
    down_cols,
    tokens,
    out_grad,
    up_hbm,
    down_hbm,
    in_ref,
    up_ref,
    down_ref,
    own,
    oth_x,
    oth_dy,
    wts,
    dense,
    pre,
    lhs,
    lhs_o,
    back,
    part,
    side,
    cross,
    cross_out,
    up_in,
    down_in,
    line_out,
    g_send,
    g_recv,
    o_send,
    o_recv,
    l_send,
    l_recv,
    s_send,
    s_recv,
    own_sem,
    w_sem,
):
    dp, hst, z = lax.axis_index("dp"), lax.axis_index("hst"), lax.axis_index("chip")
    y, c = hst // 2, hst % 2
    _, rows, count_1, width, _ = wts.shape
    count = count_1 - 1
    tok = back.shape[0]
    per = dense.shape[1] // width
    half = width // 2
    events = 2 * n_chip
    not_last, not_first = z < n_chip - 1, z > 0
    inner = jnp.logical_and(not_last, not_first)
    toward = 1 - 2 * (z % 2)
    peers = {
        ALONG_UP: {"dp": dp, "hst": hst, "chip": (z + 1) % n_chip},
        ALONG_DOWN: {"dp": dp, "hst": hst, "chip": (z + n_chip - 1) % n_chip},
        ACROSS: {"dp": dp, "hst": (1 - y) * 2 + c, "chip": z},
        SIDE: {"dp": dp, "hst": y * 2 + 1 - c, "chip": z},
        PAIR: {"dp": 1 - dp, "hst": hst, "chip": z},
        MATE: {"dp": dp, "hst": hst, "chip": z + toward},
    }
    ins, oth = (tokens, out_grad), (oth_x, oth_dy)
    mine = hst * n_chip + z

    def blocks_of(shard):
        return pl.ds(shard * per, per)

    locals_ = [
        pltpu.make_async_copy(
            ins[a].at[:, pl.ds(b * width, width)], own.at[a, mine * per + b], own_sem.at[a, b]
        )
        for a in range(2)
        for b in range(per)
    ]
    weights = [
        pltpu.make_async_copy(w, wts.at[a, :, pl.ds(0, count)], w_sem.at[a])
        for a, w in enumerate((up_hbm, down_hbm))
    ]
    for m in locals_ + weights:
        m.start()

    barrier = pltpu.get_barrier_semaphore()

    def greet(way):
        pl.semaphore_signal(barrier, inc=1, device_id=peers[way], device_id_type=MESH)

    for way in (ACROSS, SIDE, PAIR):
        greet(way)
    pl.when(not_last)(lambda: greet(ALONG_UP))
    pl.when(not_first)(lambda: greet(ALONG_DOWN))
    pl.when(inner)(lambda: pl.semaphore_wait(barrier, 5))
    pl.when(jnp.logical_not(inner))(lambda: pl.semaphore_wait(barrier, 4))

    for m in locals_:
        m.wait()

    short = jnp.minimum(z, n_chip - 1 - z)

    def place_of(i):
        both = z + toward * (2 * (i % 2) - 1) * ((i + 1) // 2)
        return jnp.where(i <= 2 * short, both, jnp.where(2 * z < n_chip - 1, i, n_chip - 1 - i))

    def event(n):
        far = jnp.where(n == events - 1, 1, jnp.where(n == 0, 0, 1 - n % 2))
        i = jnp.where(n == events - 1, n_chip - 1, jnp.where(n == 0, 0, (n + 1) // 2 - (1 - n % 2)))
        return far, i

    def shard_of(far, i, core):
        column = far * (1 - y) + (1 - far) * y
        return (column * 2 + core) * n_chip + place_of(i)

    def g_copy(a, way, shard, slot):
        return pltpu.make_async_remote_copy(
            src_ref=own.at[a, blocks_of(shard)],
            dst_ref=oth[a].at[blocks_of(shard)] if way == PAIR else own.at[a, blocks_of(shard)],
            send_sem=g_send.at[a, way, slot],
            recv_sem=o_recv.at[a, shard] if way == PAIR else g_recv.at[a, shard],
            device_id=peers[way],
            device_id_type=MESH,
        )

    def o_copy(a, way, shard, slot):
        return pltpu.make_async_remote_copy(
            src_ref=oth[a].at[blocks_of(shard)],
            dst_ref=oth[a].at[blocks_of(shard)],
            send_sem=o_send.at[a, 0 if way == SIDE else 1, slot],
            recv_sem=o_recv.at[a, shard],
            device_id=peers[way],
            device_id_type=MESH,
        )

    def own_ways(n, far, i, shard, act, late):
        place = place_of(i)
        near = far == 0
        for a in range(2):
            c_ = lambda way, a=a: g_copy(a, way, shard, n)
            if not late:
                pl.when(near & (place <= z) & not_last)(lambda: act(c_(ALONG_UP)))
                pl.when(near & (place >= z) & not_first)(lambda: act(c_(ALONG_DOWN)))
                pl.when(near)(lambda: act(c_(ACROSS)))
                act(c_(SIDE))
            if a == 0:
                if not late:
                    pl.when(i != 1)(lambda: act(c_(PAIR)))
            else:
                pl.when(i > 1 if late else i == 0)(lambda: act(c_(PAIR)))

    def assemble(a, shard):
        for j in range(rows):
            for b in range(per):
                dense[j * width : (j + 1) * width, b * width : (b + 1) * width] = wts[
                    a, j, inv[a, j, shard * per + b]
                ]

    def gather_step(n, carry):
        @pl.when(n < events)
        def _():
            far, i = event(n)
            shard = shard_of(far, i, c)

            @pl.when(n > 0)
            def _():
                for a in range(2):
                    g_copy(a, SIDE, shard, n).wait_recv()

            own_ways(n, far, i, shard, lambda d: d.start(), False)

        @pl.when(n == 0)
        def _():
            for m in weights:
                m.wait()
            for a in range(2):
                wts[a, :, count] = jnp.zeros((rows, width, width), wts.dtype)
            pre[...] = jnp.zeros_like(pre)

        def unit(q, carry):
            sib, a = q // 2, q % 2
            now = n - sib

            @pl.when((now >= 0) & (now < events))
            def _():
                far, i = event(now)
                core = jnp.where(sib == 1, 1 - c, c)
                shard = shard_of(far, i, core)

                @pl.when(sib == 1)
                def _():
                    g_copy(a, SIDE, shard, now).wait_recv()

                assemble(a, shard)
                taken = [own[a, shard * per + b] for b in range(per)]
                pre[a] += lax.dot_general(
                    dense[...],
                    jnp.concatenate(taken, axis=1),
                    NT,
                    preferred_element_type=jnp.float32,
                )

            return carry

        lax.fori_loop(0, 4, unit, 0)
        return carry

    lax.fori_loop(0, events + 1, gather_step, 0)

    def gates(j, carry):
        at = pl.ds(pl.multiple_of(j * width, width), width)
        p, h = pre[0, at, :], pre[1, at, :]
        sig = 1.0 / (1.0 + jnp.exp(-p))
        act = (p * sig).astype(jnp.bfloat16)
        grad_f = h * sig * (1.0 + p * (1.0 - sig))
        grad = grad_f.astype(jnp.bfloat16)
        for f in range(2):
            lhs[0, f, j] = grad[f * half : (f + 1) * half]
            lhs[1, f, j] = act[f * half : (f + 1) * half]
        back[:, at] = grad_f.T.astype(jnp.bfloat16)
        return carry

    lax.fori_loop(0, rows, gates, 0)

    def l_copy(a):
        return pltpu.make_async_remote_copy(
            src_ref=lhs.at[a, 1 - dp],
            dst_ref=lhs_o.at[a],
            send_sem=l_send.at[a],
            recv_sem=l_recv.at[a],
            device_id=peers[PAIR],
            device_id_type=MESH,
        )

    def late_ways(act):
        def body(n, carry):
            far, i = event(n)
            own_ways(n, far, i, shard_of(far, i, c), act, True)
            return carry

        lax.fori_loop(0, events, body, 0)

    l_copy(0).start()
    late_ways(lambda d: d.start())
    l_copy(1).start()

    def service(far, i, a):
        shard = shard_of(far, i, c)
        slot = far * n_chip + i
        o_copy(a, SIDE, shard, slot).wait_recv()
        o_copy(a, SIDE, shard, slot).start()
        if i == 0:
            o_copy(a, MATE, shard, slot).start()

    for a in range(2):
        for far in range(2):
            service(far, 0, a)

    def copy(way, source, target, slot):
        return pltpu.make_async_remote_copy(
            src_ref=source,
            dst_ref=target,
            send_sem=s_send.at[way, slot],
            recv_sem=s_recv.at[way, slot],
            device_id=peers[way],
            device_id_type=MESH,
        )

    def side_copy(column, place):
        slot = column * n_chip + place
        return copy(SIDE, part.at[(column * 2 + 1 - c) * n_chip + place], side.at[slot], slot)

    def cross_copy(place):
        return copy(ACROSS, cross_out.at[place], cross.at[place], place)

    def up_copy(place):
        return copy(ALONG_UP, line_out.at[place], up_in.at[place], place)

    def down_copy(place):
        return copy(ALONG_DOWN, line_out.at[place], down_in.at[place], place)

    chunk = 32 if tok % 32 == 0 else tok

    def total(store, terms):
        def body(i, carry):
            at = pl.ds(pl.multiple_of(i * chunk, chunk), chunk)
            value = None
            for ref, slot in terms:
                term = ref[slot, at, :].astype(jnp.float32)
                value = term if value is None else value + term
            store(at, value.astype(jnp.bfloat16))
            return carry

        lax.fori_loop(0, tok // chunk, body, 0)

    def to(ref, slot):
        def store(at, value):
            ref[slot, at, :] = value

        return store

    def to_out(at, value):
        in_ref[at, :] = value

    def pieces(column, place):
        def body(q, carry):
            core = jnp.where(q == 0, 1 - c, c)
            shard = (column * 2 + core) * n_chip + place
            assemble(0, shard)
            part[shard] = jnp.dot(
                back[...], dense[...], preferred_element_type=jnp.float32
            ).astype(jnp.bfloat16)
            pl.when(q == 0)(lambda: side_copy(column, place).start())
            return carry

        lax.fori_loop(0, 2, body, 0)

    def piece_step(r, carry):
        @pl.when(r < events)
        def _():
            column = jnp.where(r < n_chip, 1 - y, y)
            pieces(column, place_of(n_chip - 1 - r % n_chip))

        @pl.when((r > 0) & (r <= n_chip))
        def _():
            place = place_of(n_chip - r)
            slot = (1 - y) * n_chip + place
            side_copy(1 - y, place).wait_recv()
            total(to(cross_out, place), [(part, ((1 - y) * 2 + c) * n_chip + place), (side, slot)])
            cross_copy(place).start()

        return carry

    lax.fori_loop(0, events, piece_step, 0)

    def line_step(place):
        slot = y * n_chip + place
        side_copy(y, place).wait_recv()
        cross_copy(place).wait_recv()
        base = [(part, (y * 2 + c) * n_chip + place), (side, slot), (cross, place)]

        @pl.when(place > z)
        def _():
            @pl.when(not_first)
            def _():
                up_copy(place).wait_recv()
                total(to(line_out, place), base + [(up_in, place)])

            @pl.when(jnp.logical_not(not_first))
            def _():
                total(to(line_out, place), base)

            up_copy(place).start()

        @pl.when(place < z)
        def _():
            @pl.when(not_last)
            def _():
                down_copy(place).wait_recv()
                total(to(line_out, place), base + [(down_in, place)])

            @pl.when(jnp.logical_not(not_last))
            def _():
                total(to(line_out, place), base)

            down_copy(place).start()

        @pl.when(place == z)
        def _():
            @pl.when(inner)
            def _():
                up_copy(place).wait_recv()
                down_copy(place).wait_recv()
                total(to_out, base + [(up_in, place), (down_in, place)])

            @pl.when(jnp.logical_not(not_first))
            def _():
                down_copy(place).wait_recv()
                total(to_out, base + [(down_in, place)])

            @pl.when(jnp.logical_not(not_last))
            def _():
                up_copy(place).wait_recv()
                total(to_out, base + [(up_in, place)])

    cols, outs = (up_cols, down_cols), (up_ref, down_ref)
    step = 4 if count % 4 == 0 else 1

    def grad_row(a, left, source, j, add):
        for first in range(0, count, step):
            picked = [source(cols[a][j, k]) for k in range(first, first + step)]
            value = jnp.dot(
                left, jnp.concatenate(picked, axis=1), preferred_element_type=jnp.float32
            )
            for i in range(step):
                block = value[:, i * width : (i + 1) * width]
                if add:
                    outs[a][j, first + i] += block
                else:
                    outs[a][j, first + i] = block

    share = -(-rows // n_chip)

    def line_loop(r, carry):
        def body(j, carry):
            for a in range(2):
                grad_row(a, lhs[a, dp, j], lambda col, a=a: own[a, col], j, False)
            return carry

        lax.fori_loop(r * share, jnp.minimum((r + 1) * share, rows), body, 0)
        line_step(place_of(n_chip - 1 - r))
        return carry

    for r in range(n_chip):
        line_loop(r, 0)
        if r == 0:
            for i in range(2, n_chip):
                for far in range(2):
                    service(far, i, 0)
        if r == 1:
            for far in range(2):
                service(far, 1, 0)

    for a in range(2):
        if a == 1:
            for i in [*range(2, n_chip), 1]:
                for far in range(2):
                    service(far, i, a)
        for far in range(2):
            for i in range(n_chip):
                shard = shard_of(far, i, 1 - c)
                o_copy(a, SIDE, shard, far * n_chip + i).wait_recv()
        l_copy(a).wait_recv()

        def body(j, carry, a=a):
            grad_row(a, lhs_o[a, j], lambda col: oth[a][col], j, True)
            return carry

        lax.fori_loop(0, rows, body, 0)

    def settle(n, carry):
        far, i = event(n)
        shard = shard_of(far, i, c)
        own_ways(n, far, i, shard, lambda d: d.wait_send(), False)
        for a in range(2):
            o_copy(a, SIDE, shard, far * n_chip + i).wait_send()
            pl.when(i == 0)(lambda a=a: o_copy(a, MATE, shard, far * n_chip + i).wait_send())
        return carry

    lax.fori_loop(0, events, settle, 0)
    late_ways(lambda d: d.wait_send())
    for a in range(2):
        l_copy(a).wait_send()

    def settle_sum(place, carry):
        side_copy(1 - y, place).wait_send()
        side_copy(y, place).wait_send()
        cross_copy(place).wait_send()
        pl.when(place > z)(lambda: up_copy(place).wait_send())
        pl.when(place < z)(lambda: down_copy(place).wait_send())
        return carry

    lax.fori_loop(0, n_chip, settle_sum, 0)


def fused_call(n_hst, n_chip, tokens, out_grad, up_blocks, up_cols, down_blocks, down_cols):
    rows, count, width, _ = up_blocks.shape
    tok, part = tokens.shape
    shards = n_hst * n_chip
    blocks = shards * part // width
    names = jnp.arange(blocks, dtype=jnp.int32)
    ranks = jnp.arange(count, dtype=jnp.int32)[None, None, :, None] - count
    cols = jnp.stack([up_cols, down_cols])
    hits = cols[:, :, :, None] == names
    inv = jnp.sum(jnp.where(hits, ranks, 0), axis=2, dtype=jnp.int32) + count
    hidden = rows * width
    bf, f32 = jnp.bfloat16, jnp.float32
    dma = pltpu.SemaphoreType.DMA
    whole = pl.BlockSpec(memory_space=pltpu.VMEM)
    smem = pl.BlockSpec(memory_space=pltpu.SMEM)
    anywhere = pl.BlockSpec(memory_space=pl.ANY)
    grads = jax.ShapeDtypeStruct((rows, count, width // 2, width), f32)

    def slots(amount):
        return pltpu.VMEM((amount, tok, part), bf)

    return pl.pallas_call(
        functools.partial(fused_kernel, n_chip),
        in_specs=[smem] * 3 + [anywhere] * 4,
        out_specs=[whole] * 3,
        out_shape=[jax.ShapeDtypeStruct((tok, part), bf), grads, grads],
        scratch_shapes=[
            pltpu.VMEM((2, blocks, tok, width), bf),
            pltpu.VMEM((blocks, tok, width), bf),
            pltpu.VMEM((blocks, tok, width), bf),
            pltpu.VMEM((2, rows, count + 1, width, width), bf),
            pltpu.VMEM((hidden, part), bf),
            pltpu.VMEM((2, hidden, tok), f32),
            pltpu.VMEM((2, 2, rows, width // 2, tok), bf),
            pltpu.VMEM((2, rows, width // 2, tok), bf),
            pltpu.VMEM((tok, hidden), bf),
            slots(shards),
            slots(2 * n_chip),
        ]
        + [slots(n_chip)] * 5
        + [
            dma((2, 5, 2 * n_chip)),
            dma((2, shards)),
            dma((2, 2, 2 * n_chip)),
            dma((2, shards)),
            dma((2,)),
            dma((2,)),
            dma((4, 2 * n_chip)),
            dma((4, 2 * n_chip)),
            dma((2, part // width)),
            dma((2,)),
        ],
        compiler_params=pltpu.CompilerParams(
            collective_id=2, has_side_effects=True, vmem_limit_bytes=58 * 2**20
        ),
        cost_estimate=pl.CostEstimate(
            flops=22 * tok * hidden * shards * part // 4,
            bytes_accessed=20 * 2**20,
            transcendentals=hidden * tok,
        ),
    )(inv, up_cols, down_cols, tokens, out_grad, up_blocks, down_blocks)


def local(n_dp, n_hst, n_chip, tokens, out_grad, up_blocks, up_cols, down_blocks, down_cols):
    if n_dp == 2 and n_hst == 4 and n_chip >= 2 and n_chip % 2 == 0:
        return tuple(
            fused_call(
                n_hst, n_chip, tokens, out_grad, up_blocks, up_cols, down_blocks, down_cols
            )
        )
    whole_x, whole_dy = gather_call(n_hst, n_chip, tokens, out_grad)
    split = n_dp == 2
    partial_value, *grads = rows_call(
        split, whole_x, whole_dy, up_blocks, up_cols, down_blocks, down_cols
    )
    if split:
        swap = [(0, 1), (1, 0)]
        sums = [
            grads[i].astype(jnp.float32)
            + lax.ppermute(grads[i + 1], "dp", swap).astype(jnp.float32)
            for i in (0, 2)
        ]
    else:
        sums = [
            lax.psum_scatter(g, "dp", scatter_dimension=2, tiled=True).astype(jnp.float32)
            for g in grads
        ]
    summed = scatter_call(n_hst, n_chip, partial_value)
    return (summed, *sums)


def solution(mesh):
    placed = (
        P("dp", ("hst", "chip")),
        P("dp", ("hst", "chip")),
        P(("hst", "chip"), None, None, None),
        P(("hst", "chip"), None),
        P(("hst", "chip"), None, None, None),
        P(("hst", "chip"), None),
    )
    return jax.shard_map(
        functools.partial(local, mesh.shape["dp"], mesh.shape["hst"], mesh.shape["chip"]),
        mesh=mesh,
        in_specs=placed,
        out_specs=(
            P("dp", ("hst", "chip")),
            P(("hst", "chip"), None, "dp", None),
            P(("hst", "chip"), None, "dp", None),
        ),
        check_vma=False,
    )
```

```python
import functools

import jax
import jax.numpy as jnp
from jax import lax
from jax.experimental import pallas as pl
from jax.experimental.pallas import tpu as pltpu
from jax.sharding import PartitionSpec as P

NT = (((1,), (1,)), ((), ()))


def rows_kernel(
    split,
    up_cols,
    down_cols,
    me,
    x_ref,
    dy_ref,
    up_ref,
    down_ref,
    in_ref,
    *rest,
):
    outs, (acc, xs, dys, us, ds) = rest[:-5], rest[-5:]
    row = pl.program_id(0)
    width = up_ref.shape[-1]
    per_shard = x_ref.shape[2] // width
    count = up_ref.shape[1]

    @pl.when(row == 0)
    def _():
        acc[...] = jnp.zeros_like(acc)

    def place(col):
        return col // per_shard, pl.ds(pl.multiple_of((col % per_shard) * width, width), width)

    for k in range(count):
        lanes = pl.ds(k * width, width)
        shard, at = place(up_cols[row, k])
        xs[:, lanes] = x_ref[shard, :, at]
        shard, at = place(down_cols[row, k])
        dys[:, lanes] = dy_ref[shard, :, at]
        us[:, lanes] = up_ref[0, k]
        ds[:, lanes] = down_ref[0, k]
    pre = lax.dot_general(us[...], xs[...], NT, preferred_element_type=jnp.float32)
    hid = lax.dot_general(ds[...], dys[...], NT, preferred_element_type=jnp.float32)
    sig = 1.0 / (1.0 + jnp.exp(-pre))
    act = (pre * sig).astype(jnp.bfloat16)
    pre_grad_f = hid * sig * (1.0 + pre * (1.0 - sig))
    pre_grad = pre_grad_f.astype(jnp.bfloat16)
    pre_grad_t = pre_grad_f.T.astype(jnp.bfloat16)

    step = 4
    for base in range(0, count, step):
        lanes = pl.ds(base * width, step * width)
        up_part = jnp.dot(pre_grad, xs[:, lanes], preferred_element_type=jnp.float32)
        down_part = jnp.dot(act, dys[:, lanes], preferred_element_type=jnp.float32)
        back = jnp.dot(pre_grad_t, us[:, lanes], preferred_element_type=jnp.float32)
        for i in range(step):
            k = base + i
            cut = slice(i * width, (i + 1) * width)
            for part, out in ((up_part, outs[: len(outs) // 2]), (down_part, outs[len(outs) // 2 :])):
                block = part[:, cut].astype(jnp.bfloat16)
                if split:
                    half = width // 2
                    first = me[0] == 0
                    out[0][0, k] = jnp.where(first, block[:half], block[half:])
                    out[1][0, k] = jnp.where(first, block[half:], block[:half])
                else:
                    out[0][0, k] = block
            shard, at = place(up_cols[row, k])
            acc[shard, :, at] += back[:, cut]

    @pl.when(row == pl.num_programs(0) - 1)
    def _():
        for s in range(acc.shape[0]):
            in_ref[s] = acc[s].astype(jnp.bfloat16)


def rows_call(split, whole_x, whole_dy, up_blocks, up_cols, down_blocks, down_cols):
    rows, count, width, _ = up_blocks.shape
    shards, tok, part = whole_x.shape
    out_h = width // 2 if split else width
    n_out = 4 if split else 2
    whole = pl.BlockSpec(memory_space=pltpu.VMEM)
    smem = pl.BlockSpec(memory_space=pltpu.SMEM)

    def block(h):
        return pl.BlockSpec((1, count, h, width), lambda r: (r, 0, 0, 0))

    me = lax.axis_index("dp").astype(jnp.int32).reshape(1)
    flops = 10 * tok * rows * count * width * width
    return pl.pallas_call(
        functools.partial(rows_kernel, split),
        grid=(rows,),
        in_specs=[smem, smem, smem, whole, whole, block(width), block(width)],
        out_specs=[whole] + [block(out_h)] * n_out,
        out_shape=[jax.ShapeDtypeStruct(whole_x.shape, jnp.bfloat16)]
        + [jax.ShapeDtypeStruct((rows, count, out_h, width), jnp.bfloat16)] * n_out,
        scratch_shapes=[
            pltpu.VMEM(whole_x.shape, jnp.float32),
            pltpu.VMEM((tok, count * width), jnp.bfloat16),
            pltpu.VMEM((tok, count * width), jnp.bfloat16),
            pltpu.VMEM((width, count * width), jnp.bfloat16),
            pltpu.VMEM((width, count * width), jnp.bfloat16),
        ],
        compiler_params=pltpu.CompilerParams(
            dimension_semantics=("arbitrary",), vmem_limit_bytes=56 * 2**20
        ),
        cost_estimate=pl.CostEstimate(
            flops=flops, bytes_accessed=30 * 2**20, transcendentals=rows * width * tok
        ),
    )(up_cols, down_cols, me, whole_x, whole_dy, up_blocks, down_blocks)


MESH = pl.DeviceIdType.MESH
ALONG_UP, ALONG_DOWN, ACROSS, SIDE = range(4)


def gather_kernel(n_chip, x_ref, dy_ref, x_out, dy_out, send_sem, recv_sem, own_sem):
    hst, z = lax.axis_index("hst"), lax.axis_index("chip")
    far, c = hst // 2, hst % 2
    own = hst * n_chip + z
    ins, outs = (x_ref, dy_ref), (x_out, dy_out)
    not_last, not_first = z < n_chip - 1, z > 0
    peers = {
        ALONG_UP: {"hst": hst, "chip": (z + 1) % n_chip},
        ALONG_DOWN: {"hst": hst, "chip": (z + n_chip - 1) % n_chip},
        ACROSS: {"hst": (1 - far) * 2 + c, "chip": z},
        SIDE: {"hst": far * 2 + 1 - c, "chip": z},
    }

    barrier = pltpu.get_barrier_semaphore()

    def greet(way):
        pl.semaphore_signal(barrier, inc=1, device_id=peers[way], device_id_type=MESH)

    greet(ACROSS)
    greet(SIDE)
    pl.when(not_last)(lambda: greet(ALONG_UP))
    pl.when(not_first)(lambda: greet(ALONG_DOWN))
    inner = jnp.logical_and(not_last, not_first)
    pl.when(inner)(lambda: pl.semaphore_wait(barrier, 4))
    pl.when(jnp.logical_not(inner))(lambda: pl.semaphore_wait(barrier, 3))

    def copy(a, way, shard, source=None):
        return pltpu.make_async_remote_copy(
            src_ref=outs[a].at[shard] if source is None else source,
            dst_ref=outs[a].at[shard],
            send_sem=send_sem.at[a, way, shard],
            recv_sem=recv_sem.at[a, shard],
            device_id=peers[way],
            device_id_type=MESH,
        )

    def each(act):
        for t in range(n_chip + 1):
            for a in range(2):
                if t == 0:
                    act(a, (), own, None, True)
                elif t < n_chip:
                    below = z - t
                    act(a, (ALONG_UP,), hst * n_chip + below, below >= 0, False)
                    above = z + t
                    act(a, (ALONG_DOWN,), hst * n_chip + above, above < n_chip, False)
            for a in range(2):
                if t >= 1:
                    base = ((1 - far) * 2 + c) * n_chip
                    if t == 1:
                        act(a, None, base + z, None, False)
                    else:
                        act(a, None, base + z - (t - 1), z - (t - 1) >= 0, False)
                        act(a, None, base + z + (t - 1), z + (t - 1) < n_chip, False)

    def guarded(condition, run):
        if condition is None:
            run()
        else:
            pl.when(condition)(run)

    def forward(a, ways, shard, condition, is_own):
        def run():
            if not is_own:
                copy(a, SIDE, shard).wait_recv()
            source = ins[a] if is_own else None
            if ways is not None:
                if is_own or ALONG_UP in ways:
                    pl.when(not_last)(lambda: copy(a, ALONG_UP, shard, source).start())
                if is_own or ALONG_DOWN in ways:
                    pl.when(not_first)(lambda: copy(a, ALONG_DOWN, shard, source).start())
                copy(a, ACROSS, shard, source).start()
            copy(a, SIDE, shard, source).start()

        guarded(condition, run)

    def finish(a, ways, shard, condition, is_own):
        def run():
            source = ins[a] if is_own else None
            if ways is not None:
                if is_own or ALONG_UP in ways:
                    pl.when(not_last)(lambda: copy(a, ALONG_UP, shard, source).wait_send())
                if is_own or ALONG_DOWN in ways:
                    pl.when(not_first)(lambda: copy(a, ALONG_DOWN, shard, source).wait_send())
                copy(a, ACROSS, shard, source).wait_send()
            copy(a, SIDE, shard, source).wait_send()

        guarded(condition, run)

    each(forward)
    mine = [pltpu.make_async_copy(ins[a], outs[a].at[own], own_sem.at[a]) for a in range(2)]
    for m in mine:
        m.start()
    for half in range(2):
        for place in range(n_chip):
            for a in range(2):
                copy(a, SIDE, (half * 2 + 1 - c) * n_chip + place).wait_recv()
    each(finish)
    for m in mine:
        m.wait()


def gather_call(n_hst, n_chip, tokens, out_grad):
    if n_hst != 4:
        return [
            lax.all_gather(v, ("hst", "chip"), axis=0, tiled=False) for v in (tokens, out_grad)
        ]
    shards = n_hst * n_chip
    return pl.pallas_call(
        functools.partial(gather_kernel, n_chip),
        in_specs=[pl.BlockSpec(memory_space=pltpu.VMEM)] * 2,
        out_specs=[pl.BlockSpec(memory_space=pl.ANY)] * 2,
        out_shape=[jax.ShapeDtypeStruct((shards, *v.shape), v.dtype) for v in (tokens, out_grad)],
        scratch_shapes=[
            pltpu.SemaphoreType.DMA((2, 4, shards)),
            pltpu.SemaphoreType.DMA((2, shards)),
            pltpu.SemaphoreType.DMA((2,)),
        ],
        compiler_params=pltpu.CompilerParams(collective_id=0, has_side_effects=True),
    )(tokens, out_grad)


def scatter_kernel(n_chip, part, out, side, cross, up, down, cross_out, line_out, send_sem, recv_sem):
    hst, z = lax.axis_index("hst"), lax.axis_index("chip")
    far, c = hst // 2, hst % 2
    not_last, not_first = z < n_chip - 1, z > 0
    peers = {
        ALONG_UP: {"hst": hst, "chip": (z + 1) % n_chip},
        ALONG_DOWN: {"hst": hst, "chip": (z + n_chip - 1) % n_chip},
        ACROSS: {"hst": (1 - far) * 2 + c, "chip": z},
        SIDE: {"hst": far * 2 + 1 - c, "chip": z},
    }
    barrier = pltpu.get_barrier_semaphore()

    def greet(way):
        pl.semaphore_signal(barrier, inc=1, device_id=peers[way], device_id_type=MESH)

    greet(ACROSS)
    greet(SIDE)
    pl.when(not_last)(lambda: greet(ALONG_UP))
    pl.when(not_first)(lambda: greet(ALONG_DOWN))
    inner = jnp.logical_and(not_last, not_first)
    pl.when(inner)(lambda: pl.semaphore_wait(barrier, 4))
    pl.when(jnp.logical_not(inner))(lambda: pl.semaphore_wait(barrier, 3))

    def copy(way, source, target, slot):
        return pltpu.make_async_remote_copy(
            src_ref=source,
            dst_ref=target,
            send_sem=send_sem.at[way, slot],
            recv_sem=recv_sem.at[way, slot],
            device_id=peers[way],
            device_id_type=MESH,
        )

    def side_copy(half, place):
        slot = half * n_chip + place
        return copy(SIDE, part.at[(half * 2 + 1 - c) * n_chip + place], side.at[slot], slot)

    def cross_copy(place):
        return copy(ACROSS, cross_out.at[place], cross.at[place], place)

    def up_copy(place):
        return copy(ALONG_UP, line_out.at[place], up.at[place], place)

    def down_copy(place):
        return copy(ALONG_DOWN, line_out.at[place], down.at[place], place)

    def each(act):
        for t in range(n_chip - 1, 0, -1):
            pl.when(z + t < n_chip)(lambda t=t: act(z + t, 1))
            pl.when(z - t >= 0)(lambda t=t: act(z - t, -1))
        act(z, 0)

    rows = part.shape[1]
    chunk = 32 if rows % 32 == 0 else rows

    def total(store, terms):
        def body(i, carry):
            at = pl.ds(pl.multiple_of(i * chunk, chunk), chunk)
            value = None
            for ref, slot in terms:
                term = ref[slot, at, :].astype(jnp.float32)
                value = term if value is None else value + term
            store(at, value.astype(jnp.bfloat16))
            return carry

        lax.fori_loop(0, rows // chunk, body, 0)

    def to(ref, slot):
        def store(at, value):
            ref[slot, at, :] = value

        return store

    def to_out(at, value):
        out[at, :] = value

    each(lambda place, _: side_copy(1 - far, place).start())
    each(lambda place, _: side_copy(far, place).start())

    def cross_step(place, _):
        slot = (1 - far) * n_chip + place
        side_copy(1 - far, place).wait_recv()
        total(to(cross_out, place), [(part, ((1 - far) * 2 + c) * n_chip + place), (side, slot)])
        cross_copy(place).start()

    each(cross_step)

    def line_step(place, sign):
        slot = far * n_chip + place
        side_copy(far, place).wait_recv()
        cross_copy(place).wait_recv()
        base = [(part, (far * 2 + c) * n_chip + place), (side, slot), (cross, place)]
        if sign > 0:

            @pl.when(not_first)
            def _():
                up_copy(place).wait_recv()
                total(to(line_out, place), base + [(up, place)])

            @pl.when(jnp.logical_not(not_first))
            def _():
                total(to(line_out, place), base)

            up_copy(place).start()
        elif sign < 0:

            @pl.when(not_last)
            def _():
                down_copy(place).wait_recv()
                total(to(line_out, place), base + [(down, place)])

            @pl.when(jnp.logical_not(not_last))
            def _():
                total(to(line_out, place), base)

            down_copy(place).start()
        else:

            @pl.when(inner)
            def _():
                up_copy(place).wait_recv()
                down_copy(place).wait_recv()
                total(to_out, base + [(up, place), (down, place)])

            @pl.when(jnp.logical_not(not_first))
            def _():
                down_copy(place).wait_recv()
                total(to_out, base + [(down, place)])

            @pl.when(jnp.logical_not(not_last))
            def _():
                up_copy(place).wait_recv()
                total(to_out, base + [(up, place)])

    each(line_step)

    def finish(place, sign):
        side_copy(1 - far, place).wait_send()
        side_copy(far, place).wait_send()
        cross_copy(place).wait_send()
        if sign > 0:
            up_copy(place).wait_send()
        elif sign < 0:
            down_copy(place).wait_send()

    each(finish)


def scatter_call(n_hst, n_chip, part):
    if n_hst != 4 or n_chip < 2:
        return lax.psum_scatter(part, ("hst", "chip"), scatter_dimension=0, tiled=False)
    shards, rows, width = part.shape
    whole = pl.BlockSpec(memory_space=pltpu.VMEM)

    def slots(count):
        return pltpu.VMEM((count, rows, width), jnp.bfloat16)

    return pl.pallas_call(
        functools.partial(scatter_kernel, n_chip),
        in_specs=[whole],
        out_specs=whole,
        out_shape=jax.ShapeDtypeStruct((rows, width), jnp.bfloat16),
        scratch_shapes=[slots(2 * n_chip)]
        + [slots(n_chip)] * 5
        + [pltpu.SemaphoreType.DMA((4, 2 * n_chip))] * 2,
        compiler_params=pltpu.CompilerParams(
            collective_id=1, has_side_effects=True, vmem_limit_bytes=24 * 2**20
        ),
        cost_estimate=pl.CostEstimate(
            flops=shards * rows * width, bytes_accessed=120 * 2**20, transcendentals=0
        ),
    )(part)

PAIR, MATE = 4, 5


def fused_kernel(
    n_chip,
    inv,
    up_cols,
    down_cols,
    tokens,
    out_grad,
    up_hbm,
    down_hbm,
    in_ref,
    up_ref,
    down_ref,
    own,
    oth_x,
    oth_dy,
    wts,
    dense,
    pre,
    lhs,
    lhs_o,
    back,
    part,
    side,
    cross,
    cross_out,
    up_in,
    down_in,
    line_out,
    g_send,
    g_recv,
    o_send,
    o_recv,
    l_send,
    l_recv,
    s_send,
    s_recv,
    own_sem,
    w_sem,
):
    dp, hst, z = lax.axis_index("dp"), lax.axis_index("hst"), lax.axis_index("chip")
    y, c = hst // 2, hst % 2
    _, rows, count_1, width, _ = wts.shape
    count = count_1 - 1
    tok = back.shape[0]
    per = dense.shape[1] // width
    half = width // 2
    events = 2 * n_chip
    not_last, not_first = z < n_chip - 1, z > 0
    inner = jnp.logical_and(not_last, not_first)
    toward = 1 - 2 * (z % 2)
    peers = {
        ALONG_UP: {"dp": dp, "hst": hst, "chip": (z + 1) % n_chip},
        ALONG_DOWN: {"dp": dp, "hst": hst, "chip": (z + n_chip - 1) % n_chip},
        ACROSS: {"dp": dp, "hst": (1 - y) * 2 + c, "chip": z},
        SIDE: {"dp": dp, "hst": y * 2 + 1 - c, "chip": z},
        PAIR: {"dp": 1 - dp, "hst": hst, "chip": z},
        MATE: {"dp": dp, "hst": hst, "chip": z + toward},
    }
    ins, oth = (tokens, out_grad), (oth_x, oth_dy)
    mine = hst * n_chip + z

    def blocks_of(shard):
        return pl.ds(shard * per, per)

    locals_ = [
        pltpu.make_async_copy(
            ins[a].at[:, pl.ds(b * width, width)], own.at[a, mine * per + b], own_sem.at[a, b]
        )
        for a in range(2)
        for b in range(per)
    ]
    weights = [
        pltpu.make_async_copy(w, wts.at[a, :, pl.ds(0, count)], w_sem.at[a])
        for a, w in enumerate((up_hbm, down_hbm))
    ]
    for m in locals_ + weights:
        m.start()

    barrier = pltpu.get_barrier_semaphore()

    def greet(way):
        pl.semaphore_signal(barrier, inc=1, device_id=peers[way], device_id_type=MESH)

    for way in (ACROSS, SIDE, PAIR):
        greet(way)
    pl.when(not_last)(lambda: greet(ALONG_UP))
    pl.when(not_first)(lambda: greet(ALONG_DOWN))
    pl.when(inner)(lambda: pl.semaphore_wait(barrier, 5))
    pl.when(jnp.logical_not(inner))(lambda: pl.semaphore_wait(barrier, 4))

    for m in locals_:
        m.wait()

    short = jnp.minimum(z, n_chip - 1 - z)

    def place_of(i):
        both = z + toward * (2 * (i % 2) - 1) * ((i + 1) // 2)
        return jnp.where(i <= 2 * short, both, jnp.where(2 * z < n_chip - 1, i, n_chip - 1 - i))

    last = n_chip - 1
    order = [(0, 0, 0), (0, 0, 1), (0, 1, 0), (1, 0, 0), (0, 1, 1), (1, 0, 1)]
    if n_chip > 2:
        order += [(0, 2, 0), (1, 1, 0), (0, 2, 1)]
    else:
        order += [(1, 1, 0)]
    for i in range(3, n_chip):
        order += [(1, i - 1, 0), (0, i, 0), (1, i - 1, 1), (0, i, 1)]
    if n_chip > 2:
        order += [(1, last, 0), (1, last, 1)]
    order += [(1, 1, 1)]
    units = len(order)
    lined = max(order.index((0, last, 1)), order.index((1, 0, 1)))

    def pick(n, values):
        found = values[0]
        for m in range(1, len(values)):
            found = jnp.where(n == m, values[m], found)
        return found

    def unit_of(n):
        return tuple(pick(n, [u[m] for u in order]) for m in range(3))

    def shard_of(far, i, core):
        column = far * (1 - y) + (1 - far) * y
        return (column * 2 + core) * n_chip + place_of(i)

    def g_copy(a, way, shard, slot):
        return pltpu.make_async_remote_copy(
            src_ref=own.at[a, blocks_of(shard)],
            dst_ref=own.at[a, blocks_of(shard)],
            send_sem=g_send.at[a, way, slot],
            recv_sem=g_recv.at[a, shard],
            device_id=peers[way],
            device_id_type=MESH,
        )

    def x_copy(a, shard, slot):
        return pltpu.make_async_remote_copy(
            src_ref=own.at[a, blocks_of(shard)],
            dst_ref=oth[a].at[blocks_of(shard)],
            send_sem=g_send.at[a, PAIR, slot],
            recv_sem=o_recv.at[a, shard],
            device_id=peers[PAIR],
            device_id_type=MESH,
        )

    def o_copy(a, way, shard, slot):
        return pltpu.make_async_remote_copy(
            src_ref=oth[a].at[blocks_of(shard)],
            dst_ref=oth[a].at[blocks_of(shard)],
            send_sem=o_send.at[a, 0 if way == SIDE else 1, slot],
            recv_sem=o_recv.at[a, shard],
            device_id=peers[way],
            device_id_type=MESH,
        )

    def own_ways(far, i, a, act):
        place, shard, slot = place_of(i), shard_of(far, i, c), far * n_chip + i
        near = far == 0
        act(g_copy(a, SIDE, shard, slot))
        pl.when(near & (place <= z) & not_last)(lambda: act(g_copy(a, ALONG_UP, shard, slot)))
        pl.when(near & (place >= z) & not_first)(lambda: act(g_copy(a, ALONG_DOWN, shard, slot)))
        pl.when(near & ((i != 1) | (a == 0)))(lambda: act(g_copy(a, ACROSS, shard, slot)))
        pl.when((a == 0) & (i != 1))(lambda: act(x_copy(0, shard, slot)))
        pl.when((a == 1) & (i == 0))(lambda: act(x_copy(1, shard, slot)))

    def mate_way(act):
        act(g_copy(1, MATE, shard_of(1, 0, c), n_chip))

    def assemble(a, shard):
        for j in range(rows):
            for b in range(per):
                dense[j * width : (j + 1) * width, b * width : (b + 1) * width] = wts[
                    a, j, inv[a, j, shard * per + b]
                ]

    def service(far, i, a):
        shard, slot = shard_of(far, i, c), far * n_chip + i
        o_copy(a, SIDE, shard, slot).wait_recv()
        o_copy(a, SIDE, shard, slot).start()

    def mate_service(far, a):
        o_copy(a, MATE, shard_of(far, 0, c), far * n_chip).start()

    def gather_step(n, carry):
        @pl.when(n < units)
        def _():
            far, i, a = unit_of(n)
            pl.when(n > 1)(lambda: g_copy(a, SIDE, shard_of(far, i, c), 0).wait_recv())
            own_ways(far, i, a, lambda d: d.start())
            pl.when(n == lined)(lambda: mate_way(lambda d: d.start()))

        for far, at in ((0, units // 2 - 1), (1, units - 5)):

            @pl.when(n == at)
            def _():
                for a in range(2):
                    service(far, 0, a)
                    pl.when(jnp.logical_not(inner))(lambda: mate_service(far, a))

        @pl.when(n == 0)
        def _():
            for m in weights:
                m.wait()
            for a in range(2):
                wts[a, :, count] = jnp.zeros((rows, width, width), wts.dtype)
            pre[...] = jnp.zeros_like(pre)

        def unit(sib, carry):
            now = n - sib

            @pl.when((now >= 0) & (now < units))
            def _():
                far, i, a = unit_of(now)
                shard = shard_of(far, i, jnp.where(sib == 1, 1 - c, c))
                pl.when(sib == 1)(lambda: g_copy(a, SIDE, shard, 0).wait_recv())
                assemble(a, shard)
                taken = [own[a, shard * per + b] for b in range(per)]
                pre[a] += lax.dot_general(
                    dense[...],
                    jnp.concatenate(taken, axis=1),
                    NT,
                    preferred_element_type=jnp.float32,
                )

            return carry

        lax.fori_loop(0, 2, unit, 0)
        return carry

    lax.fori_loop(0, units + 1, gather_step, 0)

    def gates(j, carry):
        at = pl.ds(pl.multiple_of(j * width, width), width)
        p, h = pre[0, at, :], pre[1, at, :]
        sig = 1.0 / (1.0 + jnp.exp(-p))
        act = (p * sig).astype(jnp.bfloat16)
        grad_f = h * sig * (1.0 + p * (1.0 - sig))
        grad = grad_f.astype(jnp.bfloat16)
        for f in range(2):
            lhs[0, f, j] = grad[f * half : (f + 1) * half]
            lhs[1, f, j] = act[f * half : (f + 1) * half]
        back[:, at] = grad_f.T.astype(jnp.bfloat16)
        return carry

    lax.fori_loop(0, rows, gates, 0)

    def l_copy(a):
        return pltpu.make_async_remote_copy(
            src_ref=lhs.at[a, 1 - dp],
            dst_ref=lhs_o.at[a],
            send_sem=l_send.at[a],
            recv_sem=l_recv.at[a],
            device_id=peers[PAIR],
            device_id_type=MESH,
        )

    def late_ways(act):
        for i in range(2, n_chip):
            for far in range(2):
                act(x_copy(1, shard_of(far, i, c), far * n_chip + i))

    l_copy(0).start()
    l_copy(1).start()
    late_ways(lambda d: d.start())

    @pl.when(inner)
    def _():
        for a in range(2):
            for far in range(2):
                mate_service(far, a)

    def copy(way, source, target, slot):
        return pltpu.make_async_remote_copy(
            src_ref=source,
            dst_ref=target,
            send_sem=s_send.at[way, slot],
            recv_sem=s_recv.at[way, slot],
            device_id=peers[way],
            device_id_type=MESH,
        )

    def side_copy(column, place):
        slot = column * n_chip + place
        return copy(SIDE, part.at[(column * 2 + 1 - c) * n_chip + place], side.at[slot], slot)

    def cross_copy(place):
        return copy(ACROSS, cross_out.at[place], cross.at[place], place)

    def up_copy(place):
        return copy(ALONG_UP, line_out.at[place], up_in.at[place], place)

    def down_copy(place):
        return copy(ALONG_DOWN, line_out.at[place], down_in.at[place], place)

    chunk = 32 if tok % 32 == 0 else tok

    def total(store, terms):
        def body(i, carry):
            at = pl.ds(pl.multiple_of(i * chunk, chunk), chunk)
            value = None
            for ref, slot in terms:
                term = ref[slot, at, :].astype(jnp.float32)
                value = term if value is None else value + term
            store(at, value.astype(jnp.bfloat16))
            return carry

        lax.fori_loop(0, tok // chunk, body, 0)

    def to(ref, slot):
        def store(at, value):
            ref[slot, at, :] = value

        return store

    def to_out(at, value):
        in_ref[at, :] = value

    def pieces(column, place):
        def body(q, carry):
            core = jnp.where(q == 0, 1 - c, c)
            shard = (column * 2 + core) * n_chip + place
            assemble(0, shard)
            part[shard] = jnp.dot(
                back[...], dense[...], preferred_element_type=jnp.float32
            ).astype(jnp.bfloat16)
            pl.when(q == 0)(lambda: side_copy(column, place).start())
            return carry

        lax.fori_loop(0, 2, body, 0)

    def piece_step(r, carry):
        @pl.when(r < events)
        def _():
            column = jnp.where(r < n_chip, 1 - y, y)
            pieces(column, place_of(n_chip - 1 - r % n_chip))

        @pl.when((r > 0) & (r <= n_chip))
        def _():
            place = place_of(n_chip - r)
            slot = (1 - y) * n_chip + place
            side_copy(1 - y, place).wait_recv()
            total(to(cross_out, place), [(part, ((1 - y) * 2 + c) * n_chip + place), (side, slot)])
            cross_copy(place).start()

        return carry

    lax.fori_loop(0, events, piece_step, 0)

    def line_step(place):
        slot = y * n_chip + place
        side_copy(y, place).wait_recv()
        cross_copy(place).wait_recv()
        base = [(part, (y * 2 + c) * n_chip + place), (side, slot), (cross, place)]

        @pl.when(place > z)
        def _():
            @pl.when(not_first)
            def _():
                up_copy(place).wait_recv()
                total(to(line_out, place), base + [(up_in, place)])

            @pl.when(jnp.logical_not(not_first))
            def _():
                total(to(line_out, place), base)

            up_copy(place).start()

        @pl.when(place < z)
        def _():
            @pl.when(not_last)
            def _():
                down_copy(place).wait_recv()
                total(to(line_out, place), base + [(down_in, place)])

            @pl.when(jnp.logical_not(not_last))
            def _():
                total(to(line_out, place), base)

            down_copy(place).start()

        @pl.when(place == z)
        def _():
            @pl.when(inner)
            def _():
                up_copy(place).wait_recv()
                down_copy(place).wait_recv()
                total(to_out, base + [(up_in, place), (down_in, place)])

            @pl.when(jnp.logical_not(not_first))
            def _():
                down_copy(place).wait_recv()
                total(to_out, base + [(down_in, place)])

            @pl.when(jnp.logical_not(not_last))
            def _():
                up_copy(place).wait_recv()
                total(to_out, base + [(up_in, place)])

    cols, outs = (up_cols, down_cols), (up_ref, down_ref)
    step = 4 if count % 4 == 0 else 1

    def grad_row(a, left, source, j, add):
        for first in range(0, count, step):
            picked = [source(cols[a][j, k]) for k in range(first, first + step)]
            value = jnp.dot(
                left, jnp.concatenate(picked, axis=1), preferred_element_type=jnp.float32
            )
            for i in range(step):
                block = value[:, i * width : (i + 1) * width]
                if add:
                    outs[a][j, first + i] += block
                else:
                    outs[a][j, first + i] = block

    share = -(-rows // n_chip)

    def line_rows(r):
        def body(j, carry):
            for a in range(2):
                grad_row(a, lhs[a, dp, j], lambda col, a=a: own[a, col], j, False)
            return carry

        lax.fori_loop(min(r * share, rows), min((r + 1) * share, rows), body, 0)

    far_near = [(far, i) for i in range(2, n_chip) for far in range(2)]
    early = {0: [(far, i, 0) for far, i in far_near], 1: [(0, 1, 0), (1, 1, 0)]}
    early[n_chip - 1] = early.get(n_chip - 1, []) + [(0, 1, 1), (1, 1, 1)]
    for r in range(n_chip):
        line_rows(r)
        for far, i, a in early.get(r, []):
            service(far, i, a)
        line_step(place_of(n_chip - 1 - r))

    for a in range(2):
        if a == 1:
            for far, i in far_near:
                service(far, i, a)
        for far in range(2):
            for i in range(n_chip):
                o_copy(a, SIDE, shard_of(far, i, 1 - c), far * n_chip + i).wait_recv()
        l_copy(a).wait_recv()

        def body(j, carry, a=a):
            grad_row(a, lhs_o[a, j], lambda col: oth[a][col], j, True)
            return carry

        lax.fori_loop(0, rows, body, 0)

    def settle(n, carry):
        far, i, a = unit_of(n)
        own_ways(far, i, a, lambda d: d.wait_send())
        return carry

    lax.fori_loop(0, units, settle, 0)
    mate_way(lambda d: d.wait_send())
    late_ways(lambda d: d.wait_send())
    for a in range(2):
        for far in range(2):
            for i in range(n_chip):
                o_copy(a, SIDE, shard_of(far, i, c), far * n_chip + i).wait_send()
            o_copy(a, MATE, shard_of(far, 0, c), far * n_chip).wait_send()
        l_copy(a).wait_send()

    def settle_sum(place, carry):
        side_copy(1 - y, place).wait_send()
        side_copy(y, place).wait_send()
        cross_copy(place).wait_send()
        pl.when(place > z)(lambda: up_copy(place).wait_send())
        pl.when(place < z)(lambda: down_copy(place).wait_send())
        return carry

    lax.fori_loop(0, n_chip, settle_sum, 0)


def fused_call(n_hst, n_chip, tokens, out_grad, up_blocks, up_cols, down_blocks, down_cols):
    rows, count, width, _ = up_blocks.shape
    tok, part = tokens.shape
    shards = n_hst * n_chip
    blocks = shards * part // width
    names = jnp.arange(blocks, dtype=jnp.int32)
    ranks = jnp.arange(count, dtype=jnp.int32)[None, None, :, None] - count
    cols = jnp.stack([up_cols, down_cols])
    hits = cols[:, :, :, None] == names
    inv = jnp.sum(jnp.where(hits, ranks, 0), axis=2, dtype=jnp.int32) + count
    hidden = rows * width
    bf, f32 = jnp.bfloat16, jnp.float32
    dma = pltpu.SemaphoreType.DMA
    whole = pl.BlockSpec(memory_space=pltpu.VMEM)
    smem = pl.BlockSpec(memory_space=pltpu.SMEM)
    anywhere = pl.BlockSpec(memory_space=pl.ANY)
    grads = jax.ShapeDtypeStruct((rows, count, width // 2, width), f32)

    def slots(amount):
        return pltpu.VMEM((amount, tok, part), bf)

    return pl.pallas_call(
        functools.partial(fused_kernel, n_chip),
        in_specs=[smem] * 3 + [anywhere] * 4,
        out_specs=[whole] * 3,
        out_shape=[jax.ShapeDtypeStruct((tok, part), bf), grads, grads],
        scratch_shapes=[
            pltpu.VMEM((2, blocks, tok, width), bf),
            pltpu.VMEM((blocks, tok, width), bf),
            pltpu.VMEM((blocks, tok, width), bf),
            pltpu.VMEM((2, rows, count + 1, width, width), bf),
            pltpu.VMEM((hidden, part), bf),
            pltpu.VMEM((2, hidden, tok), f32),
            pltpu.VMEM((2, 2, rows, width // 2, tok), bf),
            pltpu.VMEM((2, rows, width // 2, tok), bf),
            pltpu.VMEM((tok, hidden), bf),
            slots(shards),
            slots(2 * n_chip),
        ]
        + [slots(n_chip)] * 5
        + [
            dma((2, 6, 2 * n_chip)),
            dma((2, shards)),
            dma((2, 2, 2 * n_chip)),
            dma((2, shards)),
            dma((2,)),
            dma((2,)),
            dma((4, 2 * n_chip)),
            dma((4, 2 * n_chip)),
            dma((2, part // width)),
            dma((2,)),
        ],
        compiler_params=pltpu.CompilerParams(
            collective_id=2, has_side_effects=True, vmem_limit_bytes=58 * 2**20
        ),
        cost_estimate=pl.CostEstimate(
            flops=22 * tok * hidden * shards * part // 4,
            bytes_accessed=20 * 2**20,
            transcendentals=hidden * tok,
        ),
    )(inv, up_cols, down_cols, tokens, out_grad, up_blocks, down_blocks)


def local(n_dp, n_hst, n_chip, tokens, out_grad, up_blocks, up_cols, down_blocks, down_cols):
    if n_dp == 2 and n_hst == 4 and n_chip >= 2 and n_chip % 2 == 0:
        return tuple(
            fused_call(
                n_hst, n_chip, tokens, out_grad, up_blocks, up_cols, down_blocks, down_cols
            )
        )
    whole_x, whole_dy = gather_call(n_hst, n_chip, tokens, out_grad)
    split = n_dp == 2
    partial_value, *grads = rows_call(
        split, whole_x, whole_dy, up_blocks, up_cols, down_blocks, down_cols
    )
    if split:
        swap = [(0, 1), (1, 0)]
        sums = [
            grads[i].astype(jnp.float32)
            + lax.ppermute(grads[i + 1], "dp", swap).astype(jnp.float32)
            for i in (0, 2)
        ]
    else:
        sums = [
            lax.psum_scatter(g, "dp", scatter_dimension=2, tiled=True).astype(jnp.float32)
            for g in grads
        ]
    summed = scatter_call(n_hst, n_chip, partial_value)
    return (summed, *sums)


def solution(mesh):
    placed = (
        P("dp", ("hst", "chip")),
        P("dp", ("hst", "chip")),
        P(("hst", "chip"), None, None, None),
        P(("hst", "chip"), None),
        P(("hst", "chip"), None, None, None),
        P(("hst", "chip"), None),
    )
    return jax.shard_map(
        functools.partial(local, mesh.shape["dp"], mesh.shape["hst"], mesh.shape["chip"]),
        mesh=mesh,
        in_specs=placed,
        out_specs=(
            P("dp", ("hst", "chip")),
            P(("hst", "chip"), None, "dp", None),
            P(("hst", "chip"), None, "dp", None),
        ),
        check_vma=False,
    )
```

```python
import functools

import jax
import jax.numpy as jnp
from jax import lax
from jax.experimental import pallas as pl
from jax.experimental.pallas import tpu as pltpu
from jax.sharding import PartitionSpec as P

NT = (((1,), (1,)), ((), ()))


def rows_kernel(
    split,
    up_cols,
    down_cols,
    me,
    x_ref,
    dy_ref,
    up_ref,
    down_ref,
    in_ref,
    *rest,
):
    outs, (acc, xs, dys, us, ds) = rest[:-5], rest[-5:]
    row = pl.program_id(0)
    width = up_ref.shape[-1]
    per_shard = x_ref.shape[2] // width
    count = up_ref.shape[1]

    @pl.when(row == 0)
    def _():
        acc[...] = jnp.zeros_like(acc)

    def place(col):
        return col // per_shard, pl.ds(pl.multiple_of((col % per_shard) * width, width), width)

    for k in range(count):
        lanes = pl.ds(k * width, width)
        shard, at = place(up_cols[row, k])
        xs[:, lanes] = x_ref[shard, :, at]
        shard, at = place(down_cols[row, k])
        dys[:, lanes] = dy_ref[shard, :, at]
        us[:, lanes] = up_ref[0, k]
        ds[:, lanes] = down_ref[0, k]
    pre = lax.dot_general(us[...], xs[...], NT, preferred_element_type=jnp.float32)
    hid = lax.dot_general(ds[...], dys[...], NT, preferred_element_type=jnp.float32)
    sig = 1.0 / (1.0 + jnp.exp(-pre))
    act = (pre * sig).astype(jnp.bfloat16)
    pre_grad_f = hid * sig * (1.0 + pre * (1.0 - sig))
    pre_grad = pre_grad_f.astype(jnp.bfloat16)
    pre_grad_t = pre_grad_f.T.astype(jnp.bfloat16)

    step = 4
    for base in range(0, count, step):
        lanes = pl.ds(base * width, step * width)
        up_part = jnp.dot(pre_grad, xs[:, lanes], preferred_element_type=jnp.float32)
        down_part = jnp.dot(act, dys[:, lanes], preferred_element_type=jnp.float32)
        back = jnp.dot(pre_grad_t, us[:, lanes], preferred_element_type=jnp.float32)
        for i in range(step):
            k = base + i
            cut = slice(i * width, (i + 1) * width)
            for part, out in ((up_part, outs[: len(outs) // 2]), (down_part, outs[len(outs) // 2 :])):
                block = part[:, cut].astype(jnp.bfloat16)
                if split:
                    half = width // 2
                    first = me[0] == 0
                    out[0][0, k] = jnp.where(first, block[:half], block[half:])
                    out[1][0, k] = jnp.where(first, block[half:], block[:half])
                else:
                    out[0][0, k] = block
            shard, at = place(up_cols[row, k])
            acc[shard, :, at] += back[:, cut]

    @pl.when(row == pl.num_programs(0) - 1)
    def _():
        for s in range(acc.shape[0]):
            in_ref[s] = acc[s].astype(jnp.bfloat16)


def rows_call(split, whole_x, whole_dy, up_blocks, up_cols, down_blocks, down_cols):
    rows, count, width, _ = up_blocks.shape
    shards, tok, part = whole_x.shape
    out_h = width // 2 if split else width
    n_out = 4 if split else 2
    whole = pl.BlockSpec(memory_space=pltpu.VMEM)
    smem = pl.BlockSpec(memory_space=pltpu.SMEM)

    def block(h):
        return pl.BlockSpec((1, count, h, width), lambda r: (r, 0, 0, 0))

    me = lax.axis_index("dp").astype(jnp.int32).reshape(1)
    flops = 10 * tok * rows * count * width * width
    return pl.pallas_call(
        functools.partial(rows_kernel, split),
        grid=(rows,),
        in_specs=[smem, smem, smem, whole, whole, block(width), block(width)],
        out_specs=[whole] + [block(out_h)] * n_out,
        out_shape=[jax.ShapeDtypeStruct(whole_x.shape, jnp.bfloat16)]
        + [jax.ShapeDtypeStruct((rows, count, out_h, width), jnp.bfloat16)] * n_out,
        scratch_shapes=[
            pltpu.VMEM(whole_x.shape, jnp.float32),
            pltpu.VMEM((tok, count * width), jnp.bfloat16),
            pltpu.VMEM((tok, count * width), jnp.bfloat16),
            pltpu.VMEM((width, count * width), jnp.bfloat16),
            pltpu.VMEM((width, count * width), jnp.bfloat16),
        ],
        compiler_params=pltpu.CompilerParams(
            dimension_semantics=("arbitrary",), vmem_limit_bytes=56 * 2**20
        ),
        cost_estimate=pl.CostEstimate(
            flops=flops, bytes_accessed=30 * 2**20, transcendentals=rows * width * tok
        ),
    )(up_cols, down_cols, me, whole_x, whole_dy, up_blocks, down_blocks)


MESH = pl.DeviceIdType.MESH
ALONG_UP, ALONG_DOWN, ACROSS, SIDE = range(4)


def gather_kernel(n_chip, x_ref, dy_ref, x_out, dy_out, send_sem, recv_sem, own_sem):
    hst, z = lax.axis_index("hst"), lax.axis_index("chip")
    far, c = hst // 2, hst % 2
    own = hst * n_chip + z
    ins, outs = (x_ref, dy_ref), (x_out, dy_out)
    not_last, not_first = z < n_chip - 1, z > 0
    peers = {
        ALONG_UP: {"hst": hst, "chip": (z + 1) % n_chip},
        ALONG_DOWN: {"hst": hst, "chip": (z + n_chip - 1) % n_chip},
        ACROSS: {"hst": (1 - far) * 2 + c, "chip": z},
        SIDE: {"hst": far * 2 + 1 - c, "chip": z},
    }

    barrier = pltpu.get_barrier_semaphore()

    def greet(way):
        pl.semaphore_signal(barrier, inc=1, device_id=peers[way], device_id_type=MESH)

    greet(ACROSS)
    greet(SIDE)
    pl.when(not_last)(lambda: greet(ALONG_UP))
    pl.when(not_first)(lambda: greet(ALONG_DOWN))
    inner = jnp.logical_and(not_last, not_first)
    pl.when(inner)(lambda: pl.semaphore_wait(barrier, 4))
    pl.when(jnp.logical_not(inner))(lambda: pl.semaphore_wait(barrier, 3))

    def copy(a, way, shard, source=None):
        return pltpu.make_async_remote_copy(
            src_ref=outs[a].at[shard] if source is None else source,
            dst_ref=outs[a].at[shard],
            send_sem=send_sem.at[a, way, shard],
            recv_sem=recv_sem.at[a, shard],
            device_id=peers[way],
            device_id_type=MESH,
        )

    def each(act):
        for t in range(n_chip + 1):
            for a in range(2):
                if t == 0:
                    act(a, (), own, None, True)
                elif t < n_chip:
                    below = z - t
                    act(a, (ALONG_UP,), hst * n_chip + below, below >= 0, False)
                    above = z + t
                    act(a, (ALONG_DOWN,), hst * n_chip + above, above < n_chip, False)
            for a in range(2):
                if t >= 1:
                    base = ((1 - far) * 2 + c) * n_chip
                    if t == 1:
                        act(a, None, base + z, None, False)
                    else:
                        act(a, None, base + z - (t - 1), z - (t - 1) >= 0, False)
                        act(a, None, base + z + (t - 1), z + (t - 1) < n_chip, False)

    def guarded(condition, run):
        if condition is None:
            run()
        else:
            pl.when(condition)(run)

    def forward(a, ways, shard, condition, is_own):
        def run():
            if not is_own:
                copy(a, SIDE, shard).wait_recv()
            source = ins[a] if is_own else None
            if ways is not None:
                if is_own or ALONG_UP in ways:
                    pl.when(not_last)(lambda: copy(a, ALONG_UP, shard, source).start())
                if is_own or ALONG_DOWN in ways:
                    pl.when(not_first)(lambda: copy(a, ALONG_DOWN, shard, source).start())
                copy(a, ACROSS, shard, source).start()
            copy(a, SIDE, shard, source).start()

        guarded(condition, run)

    def finish(a, ways, shard, condition, is_own):
        def run():
            source = ins[a] if is_own else None
            if ways is not None:
                if is_own or ALONG_UP in ways:
                    pl.when(not_last)(lambda: copy(a, ALONG_UP, shard, source).wait_send())
                if is_own or ALONG_DOWN in ways:
                    pl.when(not_first)(lambda: copy(a, ALONG_DOWN, shard, source).wait_send())
                copy(a, ACROSS, shard, source).wait_send()
            copy(a, SIDE, shard, source).wait_send()

        guarded(condition, run)

    each(forward)
    mine = [pltpu.make_async_copy(ins[a], outs[a].at[own], own_sem.at[a]) for a in range(2)]
    for m in mine:
        m.start()
    for half in range(2):
        for place in range(n_chip):
            for a in range(2):
                copy(a, SIDE, (half * 2 + 1 - c) * n_chip + place).wait_recv()
    each(finish)
    for m in mine:
        m.wait()


def gather_call(n_hst, n_chip, tokens, out_grad):
    if n_hst != 4:
        return [
            lax.all_gather(v, ("hst", "chip"), axis=0, tiled=False) for v in (tokens, out_grad)
        ]
    shards = n_hst * n_chip
    return pl.pallas_call(
        functools.partial(gather_kernel, n_chip),
        in_specs=[pl.BlockSpec(memory_space=pltpu.VMEM)] * 2,
        out_specs=[pl.BlockSpec(memory_space=pl.ANY)] * 2,
        out_shape=[jax.ShapeDtypeStruct((shards, *v.shape), v.dtype) for v in (tokens, out_grad)],
        scratch_shapes=[
            pltpu.SemaphoreType.DMA((2, 4, shards)),
            pltpu.SemaphoreType.DMA((2, shards)),
            pltpu.SemaphoreType.DMA((2,)),
        ],
        compiler_params=pltpu.CompilerParams(collective_id=0, has_side_effects=True),
    )(tokens, out_grad)


def scatter_kernel(n_chip, part, out, side, cross, up, down, cross_out, line_out, send_sem, recv_sem):
    hst, z = lax.axis_index("hst"), lax.axis_index("chip")
    far, c = hst // 2, hst % 2
    not_last, not_first = z < n_chip - 1, z > 0
    peers = {
        ALONG_UP: {"hst": hst, "chip": (z + 1) % n_chip},
        ALONG_DOWN: {"hst": hst, "chip": (z + n_chip - 1) % n_chip},
        ACROSS: {"hst": (1 - far) * 2 + c, "chip": z},
        SIDE: {"hst": far * 2 + 1 - c, "chip": z},
    }
    barrier = pltpu.get_barrier_semaphore()

    def greet(way):
        pl.semaphore_signal(barrier, inc=1, device_id=peers[way], device_id_type=MESH)

    greet(ACROSS)
    greet(SIDE)
    pl.when(not_last)(lambda: greet(ALONG_UP))
    pl.when(not_first)(lambda: greet(ALONG_DOWN))
    inner = jnp.logical_and(not_last, not_first)
    pl.when(inner)(lambda: pl.semaphore_wait(barrier, 4))
    pl.when(jnp.logical_not(inner))(lambda: pl.semaphore_wait(barrier, 3))

    def copy(way, source, target, slot):
        return pltpu.make_async_remote_copy(
            src_ref=source,
            dst_ref=target,
            send_sem=send_sem.at[way, slot],
            recv_sem=recv_sem.at[way, slot],
            device_id=peers[way],
            device_id_type=MESH,
        )

    def side_copy(half, place):
        slot = half * n_chip + place
        return copy(SIDE, part.at[(half * 2 + 1 - c) * n_chip + place], side.at[slot], slot)

    def cross_copy(place):
        return copy(ACROSS, cross_out.at[place], cross.at[place], place)

    def up_copy(place):
        return copy(ALONG_UP, line_out.at[place], up.at[place], place)

    def down_copy(place):
        return copy(ALONG_DOWN, line_out.at[place], down.at[place], place)

    def each(act):
        for t in range(n_chip - 1, 0, -1):
            pl.when(z + t < n_chip)(lambda t=t: act(z + t, 1))
            pl.when(z - t >= 0)(lambda t=t: act(z - t, -1))
        act(z, 0)

    rows = part.shape[1]
    chunk = 32 if rows % 32 == 0 else rows

    def total(store, terms):
        def body(i, carry):
            at = pl.ds(pl.multiple_of(i * chunk, chunk), chunk)
            value = None
            for ref, slot in terms:
                term = ref[slot, at, :].astype(jnp.float32)
                value = term if value is None else value + term
            store(at, value.astype(jnp.bfloat16))
            return carry

        lax.fori_loop(0, rows // chunk, body, 0)

    def to(ref, slot):
        def store(at, value):
            ref[slot, at, :] = value

        return store

    def to_out(at, value):
        out[at, :] = value

    each(lambda place, _: side_copy(1 - far, place).start())
    each(lambda place, _: side_copy(far, place).start())

    def cross_step(place, _):
        slot = (1 - far) * n_chip + place
        side_copy(1 - far, place).wait_recv()
        total(to(cross_out, place), [(part, ((1 - far) * 2 + c) * n_chip + place), (side, slot)])
        cross_copy(place).start()

    each(cross_step)

    def line_step(place, sign):
        slot = far * n_chip + place
        side_copy(far, place).wait_recv()
        cross_copy(place).wait_recv()
        base = [(part, (far * 2 + c) * n_chip + place), (side, slot), (cross, place)]
        if sign > 0:

            @pl.when(not_first)
            def _():
                up_copy(place).wait_recv()
                total(to(line_out, place), base + [(up, place)])

            @pl.when(jnp.logical_not(not_first))
            def _():
                total(to(line_out, place), base)

            up_copy(place).start()
        elif sign < 0:

            @pl.when(not_last)
            def _():
                down_copy(place).wait_recv()
                total(to(line_out, place), base + [(down, place)])

            @pl.when(jnp.logical_not(not_last))
            def _():
                total(to(line_out, place), base)

            down_copy(place).start()
        else:

            @pl.when(inner)
            def _():
                up_copy(place).wait_recv()
                down_copy(place).wait_recv()
                total(to_out, base + [(up, place), (down, place)])

            @pl.when(jnp.logical_not(not_first))
            def _():
                down_copy(place).wait_recv()
                total(to_out, base + [(down, place)])

            @pl.when(jnp.logical_not(not_last))
            def _():
                up_copy(place).wait_recv()
                total(to_out, base + [(up, place)])

    each(line_step)

    def finish(place, sign):
        side_copy(1 - far, place).wait_send()
        side_copy(far, place).wait_send()
        cross_copy(place).wait_send()
        if sign > 0:
            up_copy(place).wait_send()
        elif sign < 0:
            down_copy(place).wait_send()

    each(finish)


def scatter_call(n_hst, n_chip, part):
    if n_hst != 4 or n_chip < 2:
        return lax.psum_scatter(part, ("hst", "chip"), scatter_dimension=0, tiled=False)
    shards, rows, width = part.shape
    whole = pl.BlockSpec(memory_space=pltpu.VMEM)

    def slots(count):
        return pltpu.VMEM((count, rows, width), jnp.bfloat16)

    return pl.pallas_call(
        functools.partial(scatter_kernel, n_chip),
        in_specs=[whole],
        out_specs=whole,
        out_shape=jax.ShapeDtypeStruct((rows, width), jnp.bfloat16),
        scratch_shapes=[slots(2 * n_chip)]
        + [slots(n_chip)] * 5
        + [pltpu.SemaphoreType.DMA((4, 2 * n_chip))] * 2,
        compiler_params=pltpu.CompilerParams(
            collective_id=1, has_side_effects=True, vmem_limit_bytes=24 * 2**20
        ),
        cost_estimate=pl.CostEstimate(
            flops=shards * rows * width, bytes_accessed=120 * 2**20, transcendentals=0
        ),
    )(part)

PAIR, MATE = 4, 5


def fused_kernel(
    n_chip,
    inv,
    up_cols,
    down_cols,
    tokens,
    out_grad,
    up_hbm,
    down_hbm,
    in_ref,
    up_ref,
    down_ref,
    own,
    oth_x,
    oth_dy,
    wts,
    dense,
    pre,
    lhs,
    lhs_o,
    back,
    part,
    side,
    cross,
    cross_out,
    up_in,
    down_in,
    line_out,
    g_send,
    g_recv,
    o_send,
    o_recv,
    l_send,
    l_recv,
    s_send,
    s_recv,
    own_sem,
    w_sem,
):
    dp, hst, z = lax.axis_index("dp"), lax.axis_index("hst"), lax.axis_index("chip")
    y, c = hst // 2, hst % 2
    _, rows, count_1, width, _ = wts.shape
    count = count_1 - 1
    tok = back.shape[0]
    per = dense.shape[1] // width
    half = width // 2
    events = 2 * n_chip
    not_last, not_first = z < n_chip - 1, z > 0
    inner = jnp.logical_and(not_last, not_first)
    toward = 1 - 2 * (z % 2)
    peers = {
        ALONG_UP: {"dp": dp, "hst": hst, "chip": (z + 1) % n_chip},
        ALONG_DOWN: {"dp": dp, "hst": hst, "chip": (z + n_chip - 1) % n_chip},
        ACROSS: {"dp": dp, "hst": (1 - y) * 2 + c, "chip": z},
        SIDE: {"dp": dp, "hst": y * 2 + 1 - c, "chip": z},
        PAIR: {"dp": 1 - dp, "hst": hst, "chip": z},
        MATE: {"dp": dp, "hst": hst, "chip": z + toward},
    }
    ins, oth = (tokens, out_grad), (oth_x, oth_dy)
    mine = hst * n_chip + z

    def blocks_of(shard):
        return pl.ds(shard * per, per)

    locals_ = [
        pltpu.make_async_copy(
            ins[a].at[:, pl.ds(b * width, width)], own.at[a, mine * per + b], own_sem.at[a, b]
        )
        for a in range(2)
        for b in range(per)
    ]
    weights = [
        pltpu.make_async_copy(w, wts.at[a, :, pl.ds(0, count)], w_sem.at[a])
        for a, w in enumerate((up_hbm, down_hbm))
    ]
    for m in locals_ + weights:
        m.start()

    barrier = pltpu.get_barrier_semaphore()

    def greet(way):
        pl.semaphore_signal(barrier, inc=1, device_id=peers[way], device_id_type=MESH)

    for way in (ACROSS, SIDE, PAIR):
        greet(way)
    pl.when(not_last)(lambda: greet(ALONG_UP))
    pl.when(not_first)(lambda: greet(ALONG_DOWN))
    pl.when(inner)(lambda: pl.semaphore_wait(barrier, 5))
    pl.when(jnp.logical_not(inner))(lambda: pl.semaphore_wait(barrier, 4))

    for m in locals_:
        m.wait()

    short = jnp.minimum(z, n_chip - 1 - z)

    def place_of(i):
        both = z + toward * (2 * (i % 2) - 1) * ((i + 1) // 2)
        return jnp.where(i <= 2 * short, both, jnp.where(2 * z < n_chip - 1, i, n_chip - 1 - i))

    last = n_chip - 1
    order = [(0, 0, 0), (0, 0, 1), (0, 1, 0), (1, 0, 0), (0, 1, 1), (1, 0, 1)]
    if n_chip > 2:
        order += [(0, 2, 0), (1, 1, 0), (0, 2, 1)]
    else:
        order += [(1, 1, 0)]
    for i in range(3, n_chip):
        order += [(1, i - 1, 0), (0, i, 0), (1, i - 1, 1), (0, i, 1)]
    if n_chip > 2:
        order += [(1, last, 0), (1, last, 1)]
    order += [(1, 1, 1)]
    units = len(order)
    lined = max(order.index((0, last, 1)), order.index((1, 0, 1)))

    def pick(n, values):
        found = values[0]
        for m in range(1, len(values)):
            found = jnp.where(n == m, values[m], found)
        return found

    def unit_of(n):
        return tuple(pick(n, [u[m] for u in order]) for m in range(3))

    def shard_of(far, i, core):
        column = far * (1 - y) + (1 - far) * y
        return (column * 2 + core) * n_chip + place_of(i)

    def g_copy(a, way, shard, slot):
        return pltpu.make_async_remote_copy(
            src_ref=own.at[a, blocks_of(shard)],
            dst_ref=own.at[a, blocks_of(shard)],
            send_sem=g_send.at[a, way, slot],
            recv_sem=g_recv.at[a, shard],
            device_id=peers[way],
            device_id_type=MESH,
        )

    def x_copy(a, shard, slot):
        return pltpu.make_async_remote_copy(
            src_ref=own.at[a, blocks_of(shard)],
            dst_ref=oth[a].at[blocks_of(shard)],
            send_sem=g_send.at[a, PAIR, slot],
            recv_sem=o_recv.at[a, shard],
            device_id=peers[PAIR],
            device_id_type=MESH,
        )

    def o_copy(a, way, shard, slot):
        return pltpu.make_async_remote_copy(
            src_ref=oth[a].at[blocks_of(shard)],
            dst_ref=oth[a].at[blocks_of(shard)],
            send_sem=o_send.at[a, (SIDE, MATE, ACROSS).index(way), slot],
            recv_sem=o_recv.at[a, shard],
            device_id=peers[way],
            device_id_type=MESH,
        )

    def own_ways(far, i, a, act):
        place, shard, slot = place_of(i), shard_of(far, i, c), far * n_chip + i
        near = far == 0
        act(g_copy(a, SIDE, shard, slot))
        pl.when(near & (place <= z) & not_last)(lambda: act(g_copy(a, ALONG_UP, shard, slot)))
        pl.when(near & (place >= z) & not_first)(lambda: act(g_copy(a, ALONG_DOWN, shard, slot)))
        pl.when(near & ((i != 1) | (a == 0)))(lambda: act(g_copy(a, ACROSS, shard, slot)))
        crossed = (far == 1) & (i == 2)
        pl.when((a == 0) & (i != 1) & jnp.logical_not(crossed))(lambda: act(x_copy(0, shard, slot)))
        pl.when((a == 1) & ((i == 0) | (i == 2)))(lambda: act(x_copy(1, shard, slot)))

    def mate_way(act):
        act(g_copy(1, MATE, shard_of(1, 0, c), n_chip))

    def assemble(a, shard):
        for j in range(rows):
            for b in range(per):
                dense[j * width : (j + 1) * width, b * width : (b + 1) * width] = wts[
                    a, j, inv[a, j, shard * per + b]
                ]

    def service(far, i, a):
        shard, slot = shard_of(far, i, c), far * n_chip + i
        o_copy(a, SIDE, shard, slot).wait_recv()
        o_copy(a, SIDE, shard, slot).start()

    def mate_service(far, a):
        o_copy(a, MATE, shard_of(far, 0, c), far * n_chip).start()

    def cross_over():
        return o_copy(0, ACROSS, shard_of(0, 2, c), 2)

    def gather_step(n, carry):
        @pl.when(n < units)
        def _():
            far, i, a = unit_of(n)
            pl.when(n > 1)(lambda: g_copy(a, SIDE, shard_of(far, i, c), 0).wait_recv())
            own_ways(far, i, a, lambda d: d.start())
            pl.when(n == lined)(lambda: mate_way(lambda d: d.start()))

        for far, at in ((0, units // 2 - 1), (1, units - 5)):

            @pl.when(n == at)
            def _():
                for a in range(2):
                    service(far, 0, a)
                    pl.when(jnp.logical_not(inner))(lambda: mate_service(far, a))

        if n_chip > 2:

            @pl.when(n == lined + 1)
            def _():
                service(0, 2, 0)
                cross_over().start()

        @pl.when(n == 0)
        def _():
            for m in weights:
                m.wait()
            for a in range(2):
                wts[a, :, count] = jnp.zeros((rows, width, width), wts.dtype)
            pre[...] = jnp.zeros_like(pre)

        def unit(sib, carry):
            now = n - sib

            @pl.when((now >= 0) & (now < units))
            def _():
                far, i, a = unit_of(now)
                shard = shard_of(far, i, jnp.where(sib == 1, 1 - c, c))
                pl.when(sib == 1)(lambda: g_copy(a, SIDE, shard, 0).wait_recv())
                assemble(a, shard)
                taken = [own[a, shard * per + b] for b in range(per)]
                pre[a] += lax.dot_general(
                    dense[...],
                    jnp.concatenate(taken, axis=1),
                    NT,
                    preferred_element_type=jnp.float32,
                )

            return carry

        lax.fori_loop(0, 2, unit, 0)
        return carry

    lax.fori_loop(0, units + 1, gather_step, 0)

    def gates(j, carry):
        at = pl.ds(pl.multiple_of(j * width, width), width)
        p, h = pre[0, at, :], pre[1, at, :]
        sig = 1.0 / (1.0 + jnp.exp(-p))
        act = (p * sig).astype(jnp.bfloat16)
        grad_f = h * sig * (1.0 + p * (1.0 - sig))
        grad = grad_f.astype(jnp.bfloat16)
        for f in range(2):
            lhs[0, f, j] = grad[f * half : (f + 1) * half]
            lhs[1, f, j] = act[f * half : (f + 1) * half]
        back[:, at] = grad_f.T.astype(jnp.bfloat16)
        return carry

    lax.fori_loop(0, rows, gates, 0)

    def l_copy(a):
        return pltpu.make_async_remote_copy(
            src_ref=lhs.at[a, 1 - dp],
            dst_ref=lhs_o.at[a],
            send_sem=l_send.at[a],
            recv_sem=l_recv.at[a],
            device_id=peers[PAIR],
            device_id_type=MESH,
        )

    def late_ways(act):
        for i in range(3, n_chip):
            for far in range(2):
                act(x_copy(1, shard_of(far, i, c), far * n_chip + i))

    l_copy(0).start()
    l_copy(1).start()
    late_ways(lambda d: d.start())

    @pl.when(inner)
    def _():
        for a in range(2):
            for far in range(2):
                mate_service(far, a)

    def copy(way, source, target, slot):
        return pltpu.make_async_remote_copy(
            src_ref=source,
            dst_ref=target,
            send_sem=s_send.at[way, slot],
            recv_sem=s_recv.at[way, slot],
            device_id=peers[way],
            device_id_type=MESH,
        )

    def side_copy(column, place):
        slot = column * n_chip + place
        return copy(SIDE, part.at[(column * 2 + 1 - c) * n_chip + place], side.at[slot], slot)

    def cross_copy(place):
        return copy(ACROSS, cross_out.at[place], cross.at[place], place)

    def up_copy(place):
        return copy(ALONG_UP, line_out.at[place], up_in.at[place], place)

    def down_copy(place):
        return copy(ALONG_DOWN, line_out.at[place], down_in.at[place], place)

    chunk = 32 if tok % 32 == 0 else tok

    def total(store, terms):
        def body(i, carry):
            at = pl.ds(pl.multiple_of(i * chunk, chunk), chunk)
            value = None
            for ref, slot in terms:
                term = ref[slot, at, :].astype(jnp.float32)
                value = term if value is None else value + term
            store(at, value.astype(jnp.bfloat16))
            return carry

        lax.fori_loop(0, tok // chunk, body, 0)

    def to(ref, slot):
        def store(at, value):
            ref[slot, at, :] = value

        return store

    def to_out(at, value):
        in_ref[at, :] = value

    def pieces(column, place):
        def body(q, carry):
            core = jnp.where(q == 0, 1 - c, c)
            shard = (column * 2 + core) * n_chip + place
            assemble(0, shard)
            part[shard] = jnp.dot(
                back[...], dense[...], preferred_element_type=jnp.float32
            ).astype(jnp.bfloat16)
            pl.when(q == 0)(lambda: side_copy(column, place).start())
            return carry

        lax.fori_loop(0, 2, body, 0)

    def piece_step(r, carry):
        @pl.when(r < events)
        def _():
            column = jnp.where(r < n_chip, 1 - y, y)
            pieces(column, place_of(n_chip - 1 - r % n_chip))

        @pl.when((r > 0) & (r <= n_chip))
        def _():
            place = place_of(n_chip - r)
            slot = (1 - y) * n_chip + place
            side_copy(1 - y, place).wait_recv()
            total(to(cross_out, place), [(part, ((1 - y) * 2 + c) * n_chip + place), (side, slot)])
            cross_copy(place).start()

        return carry

    lax.fori_loop(0, events, piece_step, 0)

    def line_step(place):
        slot = y * n_chip + place
        side_copy(y, place).wait_recv()
        cross_copy(place).wait_recv()
        base = [(part, (y * 2 + c) * n_chip + place), (side, slot), (cross, place)]

        @pl.when(place > z)
        def _():
            @pl.when(not_first)
            def _():
                up_copy(place).wait_recv()
                total(to(line_out, place), base + [(up_in, place)])

            @pl.when(jnp.logical_not(not_first))
            def _():
                total(to(line_out, place), base)

            up_copy(place).start()

        @pl.when(place < z)
        def _():
            @pl.when(not_last)
            def _():
                down_copy(place).wait_recv()
                total(to(line_out, place), base + [(down_in, place)])

            @pl.when(jnp.logical_not(not_last))
            def _():
                total(to(line_out, place), base)

            down_copy(place).start()

        @pl.when(place == z)
        def _():
            @pl.when(inner)
            def _():
                up_copy(place).wait_recv()
                down_copy(place).wait_recv()
                total(to_out, base + [(up_in, place), (down_in, place)])

            @pl.when(jnp.logical_not(not_first))
            def _():
                down_copy(place).wait_recv()
                total(to_out, base + [(down_in, place)])

            @pl.when(jnp.logical_not(not_last))
            def _():
                up_copy(place).wait_recv()
                total(to_out, base + [(up_in, place)])

    cols, outs = (up_cols, down_cols), (up_ref, down_ref)
    step = 4 if count % 4 == 0 else 1

    def grad_row(a, left, source, j, add):
        for first in range(0, count, step):
            picked = [source(cols[a][j, k]) for k in range(first, first + step)]
            value = jnp.dot(
                left, jnp.concatenate(picked, axis=1), preferred_element_type=jnp.float32
            )
            for i in range(step):
                block = value[:, i * width : (i + 1) * width]
                if add:
                    outs[a][j, first + i] += block
                else:
                    outs[a][j, first + i] = block

    share = -(-rows // n_chip)

    def line_rows(r):
        def body(j, carry):
            for a in range(2):
                grad_row(a, lhs[a, dp, j], lambda col, a=a: own[a, col], j, False)
            return carry

        lax.fori_loop(min(r * share, rows), min((r + 1) * share, rows), body, 0)

    far_near = [(far, i) for i in range(3, n_chip) for far in range(2)]
    early = {0: [(far, i, 0) for far, i in far_near], 1: [(0, 1, 0), (1, 1, 0)]}
    if n_chip > 2:
        early[0] += [(1, 2, 0), (0, 2, 1), (1, 2, 1)]
    early[n_chip - 1] = early.get(n_chip - 1, []) + [(0, 1, 1), (1, 1, 1)]
    for r in range(n_chip):
        line_rows(r)
        for far, i, a in early.get(r, []):
            service(far, i, a)
        line_step(place_of(n_chip - 1 - r))

    for a in range(2):
        if a == 1:
            for far, i in far_near:
                service(far, i, a)
        for far in range(2):
            for i in range(n_chip):
                o_copy(a, SIDE, shard_of(far, i, 1 - c), far * n_chip + i).wait_recv()
        l_copy(a).wait_recv()

        def body(j, carry, a=a):
            grad_row(a, lhs_o[a, j], lambda col: oth[a][col], j, True)
            return carry

        lax.fori_loop(0, rows, body, 0)

    def settle(n, carry):
        far, i, a = unit_of(n)
        own_ways(far, i, a, lambda d: d.wait_send())
        return carry

    lax.fori_loop(0, units, settle, 0)
    mate_way(lambda d: d.wait_send())
    if n_chip > 2:
        cross_over().wait_send()
    late_ways(lambda d: d.wait_send())
    for a in range(2):
        for far in range(2):
            for i in range(n_chip):
                o_copy(a, SIDE, shard_of(far, i, c), far * n_chip + i).wait_send()
            o_copy(a, MATE, shard_of(far, 0, c), far * n_chip).wait_send()
        l_copy(a).wait_send()

    def settle_sum(place, carry):
        side_copy(1 - y, place).wait_send()
        side_copy(y, place).wait_send()
        cross_copy(place).wait_send()
        pl.when(place > z)(lambda: up_copy(place).wait_send())
        pl.when(place < z)(lambda: down_copy(place).wait_send())
        return carry

    lax.fori_loop(0, n_chip, settle_sum, 0)


def fused_call(n_hst, n_chip, tokens, out_grad, up_blocks, up_cols, down_blocks, down_cols):
    rows, count, width, _ = up_blocks.shape
    tok, part = tokens.shape
    shards = n_hst * n_chip
    blocks = shards * part // width
    names = jnp.arange(blocks, dtype=jnp.int32)
    ranks = jnp.arange(count, dtype=jnp.int32)[None, None, :, None] - count
    cols = jnp.stack([up_cols, down_cols])
    hits = cols[:, :, :, None] == names
    inv = jnp.sum(jnp.where(hits, ranks, 0), axis=2, dtype=jnp.int32) + count
    hidden = rows * width
    bf, f32 = jnp.bfloat16, jnp.float32
    dma = pltpu.SemaphoreType.DMA
    whole = pl.BlockSpec(memory_space=pltpu.VMEM)
    smem = pl.BlockSpec(memory_space=pltpu.SMEM)
    anywhere = pl.BlockSpec(memory_space=pl.ANY)
    grads = jax.ShapeDtypeStruct((rows, count, width // 2, width), f32)

    def slots(amount):
        return pltpu.VMEM((amount, tok, part), bf)

    return pl.pallas_call(
        functools.partial(fused_kernel, n_chip),
        in_specs=[smem] * 3 + [anywhere] * 4,
        out_specs=[whole] * 3,
        out_shape=[jax.ShapeDtypeStruct((tok, part), bf), grads, grads],
        scratch_shapes=[
            pltpu.VMEM((2, blocks, tok, width), bf),
            pltpu.VMEM((blocks, tok, width), bf),
            pltpu.VMEM((blocks, tok, width), bf),
            pltpu.VMEM((2, rows, count + 1, width, width), bf),
            pltpu.VMEM((hidden, part), bf),
            pltpu.VMEM((2, hidden, tok), f32),
            pltpu.VMEM((2, 2, rows, width // 2, tok), bf),
            pltpu.VMEM((2, rows, width // 2, tok), bf),
            pltpu.VMEM((tok, hidden), bf),
            slots(shards),
            slots(2 * n_chip),
        ]
        + [slots(n_chip)] * 5
        + [
            dma((2, 6, 2 * n_chip)),
            dma((2, shards)),
            dma((2, 3, 2 * n_chip)),
            dma((2, shards)),
            dma((2,)),
            dma((2,)),
            dma((4, 2 * n_chip)),
            dma((4, 2 * n_chip)),
            dma((2, part // width)),
            dma((2,)),
        ],
        compiler_params=pltpu.CompilerParams(
            collective_id=2, has_side_effects=True, vmem_limit_bytes=58 * 2**20
        ),
        cost_estimate=pl.CostEstimate(
            flops=22 * tok * hidden * shards * part // 4,
            bytes_accessed=20 * 2**20,
            transcendentals=hidden * tok,
        ),
    )(inv, up_cols, down_cols, tokens, out_grad, up_blocks, down_blocks)


def local(n_dp, n_hst, n_chip, tokens, out_grad, up_blocks, up_cols, down_blocks, down_cols):
    if n_dp == 2 and n_hst == 4 and n_chip >= 2 and n_chip % 2 == 0:
        return tuple(
            fused_call(
                n_hst, n_chip, tokens, out_grad, up_blocks, up_cols, down_blocks, down_cols
            )
        )
    whole_x, whole_dy = gather_call(n_hst, n_chip, tokens, out_grad)
    split = n_dp == 2
    partial_value, *grads = rows_call(
        split, whole_x, whole_dy, up_blocks, up_cols, down_blocks, down_cols
    )
    if split:
        swap = [(0, 1), (1, 0)]
        sums = [
            grads[i].astype(jnp.float32)
            + lax.ppermute(grads[i + 1], "dp", swap).astype(jnp.float32)
            for i in (0, 2)
        ]
    else:
        sums = [
            lax.psum_scatter(g, "dp", scatter_dimension=2, tiled=True).astype(jnp.float32)
            for g in grads
        ]
    summed = scatter_call(n_hst, n_chip, partial_value)
    return (summed, *sums)


def solution(mesh):
    placed = (
        P("dp", ("hst", "chip")),
        P("dp", ("hst", "chip")),
        P(("hst", "chip"), None, None, None),
        P(("hst", "chip"), None),
        P(("hst", "chip"), None, None, None),
        P(("hst", "chip"), None),
    )
    return jax.shard_map(
        functools.partial(local, mesh.shape["dp"], mesh.shape["hst"], mesh.shape["chip"]),
        mesh=mesh,
        in_specs=placed,
        out_specs=(
            P("dp", ("hst", "chip")),
            P(("hst", "chip"), None, "dp", None),
            P(("hst", "chip"), None, "dp", None),
        ),
        check_vma=False,
    )
```

```python
import functools

import jax
import jax.numpy as jnp
from jax import lax
from jax.experimental import pallas as pl
from jax.experimental.pallas import tpu as pltpu
from jax.sharding import PartitionSpec as P

NT = (((1,), (1,)), ((), ()))


def rows_kernel(
    split,
    up_cols,
    down_cols,
    me,
    x_ref,
    dy_ref,
    up_ref,
    down_ref,
    in_ref,
    *rest,
):
    outs, (acc, xs, dys, us, ds) = rest[:-5], rest[-5:]
    row = pl.program_id(0)
    width = up_ref.shape[-1]
    per_shard = x_ref.shape[2] // width
    count = up_ref.shape[1]

    @pl.when(row == 0)
    def _():
        acc[...] = jnp.zeros_like(acc)

    def place(col):
        return col // per_shard, pl.ds(pl.multiple_of((col % per_shard) * width, width), width)

    for k in range(count):
        lanes = pl.ds(k * width, width)
        shard, at = place(up_cols[row, k])
        xs[:, lanes] = x_ref[shard, :, at]
        shard, at = place(down_cols[row, k])
        dys[:, lanes] = dy_ref[shard, :, at]
        us[:, lanes] = up_ref[0, k]
        ds[:, lanes] = down_ref[0, k]
    pre = lax.dot_general(us[...], xs[...], NT, preferred_element_type=jnp.float32)
    hid = lax.dot_general(ds[...], dys[...], NT, preferred_element_type=jnp.float32)
    sig = 1.0 / (1.0 + jnp.exp(-pre))
    act = (pre * sig).astype(jnp.bfloat16)
    pre_grad_f = hid * sig * (1.0 + pre * (1.0 - sig))
    pre_grad = pre_grad_f.astype(jnp.bfloat16)
    pre_grad_t = pre_grad_f.T.astype(jnp.bfloat16)

    step = 4
    for base in range(0, count, step):
        lanes = pl.ds(base * width, step * width)
        up_part = jnp.dot(pre_grad, xs[:, lanes], preferred_element_type=jnp.float32)
        down_part = jnp.dot(act, dys[:, lanes], preferred_element_type=jnp.float32)
        back = jnp.dot(pre_grad_t, us[:, lanes], preferred_element_type=jnp.float32)
        for i in range(step):
            k = base + i
            cut = slice(i * width, (i + 1) * width)
            for part, out in ((up_part, outs[: len(outs) // 2]), (down_part, outs[len(outs) // 2 :])):
                block = part[:, cut].astype(jnp.bfloat16)
                if split:
                    half = width // 2
                    first = me[0] == 0
                    out[0][0, k] = jnp.where(first, block[:half], block[half:])
                    out[1][0, k] = jnp.where(first, block[half:], block[:half])
                else:
                    out[0][0, k] = block
            shard, at = place(up_cols[row, k])
            acc[shard, :, at] += back[:, cut]

    @pl.when(row == pl.num_programs(0) - 1)
    def _():
        for s in range(acc.shape[0]):
            in_ref[s] = acc[s].astype(jnp.bfloat16)


def rows_call(split, whole_x, whole_dy, up_blocks, up_cols, down_blocks, down_cols):
    rows, count, width, _ = up_blocks.shape
    shards, tok, part = whole_x.shape
    out_h = width // 2 if split else width
    n_out = 4 if split else 2
    whole = pl.BlockSpec(memory_space=pltpu.VMEM)
    smem = pl.BlockSpec(memory_space=pltpu.SMEM)

    def block(h):
        return pl.BlockSpec((1, count, h, width), lambda r: (r, 0, 0, 0))

    me = lax.axis_index("dp").astype(jnp.int32).reshape(1)
    flops = 10 * tok * rows * count * width * width
    return pl.pallas_call(
        functools.partial(rows_kernel, split),
        grid=(rows,),
        in_specs=[smem, smem, smem, whole, whole, block(width), block(width)],
        out_specs=[whole] + [block(out_h)] * n_out,
        out_shape=[jax.ShapeDtypeStruct(whole_x.shape, jnp.bfloat16)]
        + [jax.ShapeDtypeStruct((rows, count, out_h, width), jnp.bfloat16)] * n_out,
        scratch_shapes=[
            pltpu.VMEM(whole_x.shape, jnp.float32),
            pltpu.VMEM((tok, count * width), jnp.bfloat16),
            pltpu.VMEM((tok, count * width), jnp.bfloat16),
            pltpu.VMEM((width, count * width), jnp.bfloat16),
            pltpu.VMEM((width, count * width), jnp.bfloat16),
        ],
        compiler_params=pltpu.CompilerParams(
            dimension_semantics=("arbitrary",), vmem_limit_bytes=56 * 2**20
        ),
        cost_estimate=pl.CostEstimate(
            flops=flops, bytes_accessed=30 * 2**20, transcendentals=rows * width * tok
        ),
    )(up_cols, down_cols, me, whole_x, whole_dy, up_blocks, down_blocks)


MESH = pl.DeviceIdType.MESH
ALONG_UP, ALONG_DOWN, ACROSS, SIDE = range(4)


def gather_kernel(n_chip, x_ref, dy_ref, x_out, dy_out, send_sem, recv_sem, own_sem):
    hst, z = lax.axis_index("hst"), lax.axis_index("chip")
    far, c = hst // 2, hst % 2
    own = hst * n_chip + z
    ins, outs = (x_ref, dy_ref), (x_out, dy_out)
    not_last, not_first = z < n_chip - 1, z > 0
    peers = {
        ALONG_UP: {"hst": hst, "chip": (z + 1) % n_chip},
        ALONG_DOWN: {"hst": hst, "chip": (z + n_chip - 1) % n_chip},
        ACROSS: {"hst": (1 - far) * 2 + c, "chip": z},
        SIDE: {"hst": far * 2 + 1 - c, "chip": z},
    }

    barrier = pltpu.get_barrier_semaphore()

    def greet(way):
        pl.semaphore_signal(barrier, inc=1, device_id=peers[way], device_id_type=MESH)

    greet(ACROSS)
    greet(SIDE)
    pl.when(not_last)(lambda: greet(ALONG_UP))
    pl.when(not_first)(lambda: greet(ALONG_DOWN))
    inner = jnp.logical_and(not_last, not_first)
    pl.when(inner)(lambda: pl.semaphore_wait(barrier, 4))
    pl.when(jnp.logical_not(inner))(lambda: pl.semaphore_wait(barrier, 3))

    def copy(a, way, shard, source=None):
        return pltpu.make_async_remote_copy(
            src_ref=outs[a].at[shard] if source is None else source,
            dst_ref=outs[a].at[shard],
            send_sem=send_sem.at[a, way, shard],
            recv_sem=recv_sem.at[a, shard],
            device_id=peers[way],
            device_id_type=MESH,
        )

    def each(act):
        for t in range(n_chip + 1):
            for a in range(2):
                if t == 0:
                    act(a, (), own, None, True)
                elif t < n_chip:
                    below = z - t
                    act(a, (ALONG_UP,), hst * n_chip + below, below >= 0, False)
                    above = z + t
                    act(a, (ALONG_DOWN,), hst * n_chip + above, above < n_chip, False)
            for a in range(2):
                if t >= 1:
                    base = ((1 - far) * 2 + c) * n_chip
                    if t == 1:
                        act(a, None, base + z, None, False)
                    else:
                        act(a, None, base + z - (t - 1), z - (t - 1) >= 0, False)
                        act(a, None, base + z + (t - 1), z + (t - 1) < n_chip, False)

    def guarded(condition, run):
        if condition is None:
            run()
        else:
            pl.when(condition)(run)

    def forward(a, ways, shard, condition, is_own):
        def run():
            if not is_own:
                copy(a, SIDE, shard).wait_recv()
            source = ins[a] if is_own else None
            if ways is not None:
                if is_own or ALONG_UP in ways:
                    pl.when(not_last)(lambda: copy(a, ALONG_UP, shard, source).start())
                if is_own or ALONG_DOWN in ways:
                    pl.when(not_first)(lambda: copy(a, ALONG_DOWN, shard, source).start())
                copy(a, ACROSS, shard, source).start()
            copy(a, SIDE, shard, source).start()

        guarded(condition, run)

    def finish(a, ways, shard, condition, is_own):
        def run():
            source = ins[a] if is_own else None
            if ways is not None:
                if is_own or ALONG_UP in ways:
                    pl.when(not_last)(lambda: copy(a, ALONG_UP, shard, source).wait_send())
                if is_own or ALONG_DOWN in ways:
                    pl.when(not_first)(lambda: copy(a, ALONG_DOWN, shard, source).wait_send())
                copy(a, ACROSS, shard, source).wait_send()
            copy(a, SIDE, shard, source).wait_send()

        guarded(condition, run)

    each(forward)
    mine = [pltpu.make_async_copy(ins[a], outs[a].at[own], own_sem.at[a]) for a in range(2)]
    for m in mine:
        m.start()
    for half in range(2):
        for place in range(n_chip):
            for a in range(2):
                copy(a, SIDE, (half * 2 + 1 - c) * n_chip + place).wait_recv()
    each(finish)
    for m in mine:
        m.wait()


def gather_call(n_hst, n_chip, tokens, out_grad):
    if n_hst != 4:
        return [
            lax.all_gather(v, ("hst", "chip"), axis=0, tiled=False) for v in (tokens, out_grad)
        ]
    shards = n_hst * n_chip
    return pl.pallas_call(
        functools.partial(gather_kernel, n_chip),
        in_specs=[pl.BlockSpec(memory_space=pltpu.VMEM)] * 2,
        out_specs=[pl.BlockSpec(memory_space=pl.ANY)] * 2,
        out_shape=[jax.ShapeDtypeStruct((shards, *v.shape), v.dtype) for v in (tokens, out_grad)],
        scratch_shapes=[
            pltpu.SemaphoreType.DMA((2, 4, shards)),
            pltpu.SemaphoreType.DMA((2, shards)),
            pltpu.SemaphoreType.DMA((2,)),
        ],
        compiler_params=pltpu.CompilerParams(collective_id=0, has_side_effects=True),
    )(tokens, out_grad)


def scatter_kernel(n_chip, part, out, side, cross, up, down, cross_out, line_out, send_sem, recv_sem):
    hst, z = lax.axis_index("hst"), lax.axis_index("chip")
    far, c = hst // 2, hst % 2
    not_last, not_first = z < n_chip - 1, z > 0
    peers = {
        ALONG_UP: {"hst": hst, "chip": (z + 1) % n_chip},
        ALONG_DOWN: {"hst": hst, "chip": (z + n_chip - 1) % n_chip},
        ACROSS: {"hst": (1 - far) * 2 + c, "chip": z},
        SIDE: {"hst": far * 2 + 1 - c, "chip": z},
    }
    barrier = pltpu.get_barrier_semaphore()

    def greet(way):
        pl.semaphore_signal(barrier, inc=1, device_id=peers[way], device_id_type=MESH)

    greet(ACROSS)
    greet(SIDE)
    pl.when(not_last)(lambda: greet(ALONG_UP))
    pl.when(not_first)(lambda: greet(ALONG_DOWN))
    inner = jnp.logical_and(not_last, not_first)
    pl.when(inner)(lambda: pl.semaphore_wait(barrier, 4))
    pl.when(jnp.logical_not(inner))(lambda: pl.semaphore_wait(barrier, 3))

    def copy(way, source, target, slot):
        return pltpu.make_async_remote_copy(
            src_ref=source,
            dst_ref=target,
            send_sem=send_sem.at[way, slot],
            recv_sem=recv_sem.at[way, slot],
            device_id=peers[way],
            device_id_type=MESH,
        )

    def side_copy(half, place):
        slot = half * n_chip + place
        return copy(SIDE, part.at[(half * 2 + 1 - c) * n_chip + place], side.at[slot], slot)

    def cross_copy(place):
        return copy(ACROSS, cross_out.at[place], cross.at[place], place)

    def up_copy(place):
        return copy(ALONG_UP, line_out.at[place], up.at[place], place)

    def down_copy(place):
        return copy(ALONG_DOWN, line_out.at[place], down.at[place], place)

    def each(act):
        for t in range(n_chip - 1, 0, -1):
            pl.when(z + t < n_chip)(lambda t=t: act(z + t, 1))
            pl.when(z - t >= 0)(lambda t=t: act(z - t, -1))
        act(z, 0)

    rows = part.shape[1]
    chunk = 32 if rows % 32 == 0 else rows

    def total(store, terms):
        def body(i, carry):
            at = pl.ds(pl.multiple_of(i * chunk, chunk), chunk)
            value = None
            for ref, slot in terms:
                term = ref[slot, at, :].astype(jnp.float32)
                value = term if value is None else value + term
            store(at, value.astype(jnp.bfloat16))
            return carry

        lax.fori_loop(0, rows // chunk, body, 0)

    def to(ref, slot):
        def store(at, value):
            ref[slot, at, :] = value

        return store

    def to_out(at, value):
        out[at, :] = value

    each(lambda place, _: side_copy(1 - far, place).start())
    each(lambda place, _: side_copy(far, place).start())

    def cross_step(place, _):
        slot = (1 - far) * n_chip + place
        side_copy(1 - far, place).wait_recv()
        total(to(cross_out, place), [(part, ((1 - far) * 2 + c) * n_chip + place), (side, slot)])
        cross_copy(place).start()

    each(cross_step)

    def line_step(place, sign):
        slot = far * n_chip + place
        side_copy(far, place).wait_recv()
        cross_copy(place).wait_recv()
        base = [(part, (far * 2 + c) * n_chip + place), (side, slot), (cross, place)]
        if sign > 0:

            @pl.when(not_first)
            def _():
                up_copy(place).wait_recv()
                total(to(line_out, place), base + [(up, place)])

            @pl.when(jnp.logical_not(not_first))
            def _():
                total(to(line_out, place), base)

            up_copy(place).start()
        elif sign < 0:

            @pl.when(not_last)
            def _():
                down_copy(place).wait_recv()
                total(to(line_out, place), base + [(down, place)])

            @pl.when(jnp.logical_not(not_last))
            def _():
                total(to(line_out, place), base)

            down_copy(place).start()
        else:

            @pl.when(inner)
            def _():
                up_copy(place).wait_recv()
                down_copy(place).wait_recv()
                total(to_out, base + [(up, place), (down, place)])

            @pl.when(jnp.logical_not(not_first))
            def _():
                down_copy(place).wait_recv()
                total(to_out, base + [(down, place)])

            @pl.when(jnp.logical_not(not_last))
            def _():
                up_copy(place).wait_recv()
                total(to_out, base + [(up, place)])

    each(line_step)

    def finish(place, sign):
        side_copy(1 - far, place).wait_send()
        side_copy(far, place).wait_send()
        cross_copy(place).wait_send()
        if sign > 0:
            up_copy(place).wait_send()
        elif sign < 0:
            down_copy(place).wait_send()

    each(finish)


def scatter_call(n_hst, n_chip, part):
    if n_hst != 4 or n_chip < 2:
        return lax.psum_scatter(part, ("hst", "chip"), scatter_dimension=0, tiled=False)
    shards, rows, width = part.shape
    whole = pl.BlockSpec(memory_space=pltpu.VMEM)

    def slots(count):
        return pltpu.VMEM((count, rows, width), jnp.bfloat16)

    return pl.pallas_call(
        functools.partial(scatter_kernel, n_chip),
        in_specs=[whole],
        out_specs=whole,
        out_shape=jax.ShapeDtypeStruct((rows, width), jnp.bfloat16),
        scratch_shapes=[slots(2 * n_chip)]
        + [slots(n_chip)] * 5
        + [pltpu.SemaphoreType.DMA((4, 2 * n_chip))] * 2,
        compiler_params=pltpu.CompilerParams(
            collective_id=1, has_side_effects=True, vmem_limit_bytes=24 * 2**20
        ),
        cost_estimate=pl.CostEstimate(
            flops=shards * rows * width, bytes_accessed=120 * 2**20, transcendentals=0
        ),
    )(part)

PAIR, MATE = 4, 5


def fused_kernel(
    n_chip,
    inv,
    up_cols,
    down_cols,
    tokens,
    out_grad,
    up_hbm,
    down_hbm,
    in_ref,
    up_ref,
    down_ref,
    own,
    oth_x,
    oth_dy,
    wts,
    dense,
    pre,
    lhs,
    lhs_o,
    back,
    part,
    side,
    cross,
    cross_out,
    up_in,
    down_in,
    line_out,
    g_send,
    g_recv,
    o_send,
    o_recv,
    l_send,
    l_recv,
    s_send,
    s_recv,
    own_sem,
    w_sem,
):
    dp, hst, z = lax.axis_index("dp"), lax.axis_index("hst"), lax.axis_index("chip")
    y, c = hst // 2, hst % 2
    _, rows, count_1, width, _ = wts.shape
    count = count_1 - 1
    tok = back.shape[0]
    per = dense.shape[1] // width
    half = width // 2
    events = 2 * n_chip
    not_last, not_first = z < n_chip - 1, z > 0
    inner = jnp.logical_and(not_last, not_first)
    toward = 1 - 2 * (z % 2)
    peers = {
        ALONG_UP: {"dp": dp, "hst": hst, "chip": (z + 1) % n_chip},
        ALONG_DOWN: {"dp": dp, "hst": hst, "chip": (z + n_chip - 1) % n_chip},
        ACROSS: {"dp": dp, "hst": (1 - y) * 2 + c, "chip": z},
        SIDE: {"dp": dp, "hst": y * 2 + 1 - c, "chip": z},
        PAIR: {"dp": 1 - dp, "hst": hst, "chip": z},
        MATE: {"dp": dp, "hst": hst, "chip": z + toward},
    }
    ins, oth = (tokens, out_grad), (oth_x, oth_dy)
    mine = hst * n_chip + z

    def blocks_of(shard):
        return pl.ds(shard * per, per)

    locals_ = [
        pltpu.make_async_copy(
            ins[a].at[:, pl.ds(b * width, width)], own.at[a, mine * per + b], own_sem.at[a, b]
        )
        for a in range(2)
        for b in range(per)
    ]
    weights = [
        pltpu.make_async_copy(w, wts.at[a, :, pl.ds(0, count)], w_sem.at[a])
        for a, w in enumerate((up_hbm, down_hbm))
    ]
    for m in locals_ + weights:
        m.start()

    barrier = pltpu.get_barrier_semaphore()

    def greet(way):
        pl.semaphore_signal(barrier, inc=1, device_id=peers[way], device_id_type=MESH)

    for way in (ACROSS, SIDE, PAIR):
        greet(way)
    pl.when(not_last)(lambda: greet(ALONG_UP))
    pl.when(not_first)(lambda: greet(ALONG_DOWN))
    pl.when(inner)(lambda: pl.semaphore_wait(barrier, 5))
    pl.when(jnp.logical_not(inner))(lambda: pl.semaphore_wait(barrier, 4))

    for m in locals_:
        m.wait()

    short = jnp.minimum(z, n_chip - 1 - z)

    def place_of(i):
        both = z + toward * (2 * (i % 2) - 1) * ((i + 1) // 2)
        return jnp.where(i <= 2 * short, both, jnp.where(2 * z < n_chip - 1, i, n_chip - 1 - i))

    last = n_chip - 1
    order = [(0, 0, 0), (0, 0, 1)]
    for i in range(1, n_chip):
        order += [(0, i, 0), (1, i - 1, 0), (0, i, 1), (1, i - 1, 1)]
    order += [(1, last, 1), (1, last, 0)]
    units = len(order)

    def pick(n, values):
        found = values[0]
        for m in range(1, len(values)):
            found = jnp.where(n == m, values[m], found)
        return found

    def unit_of(n):
        return tuple(pick(n, [u[m] for u in order]) for m in range(3))

    def shard_of(far, i, core):
        column = far * (1 - y) + (1 - far) * y
        return (column * 2 + core) * n_chip + place_of(i)

    def g_copy(a, way, shard, slot):
        return pltpu.make_async_remote_copy(
            src_ref=own.at[a, blocks_of(shard)],
            dst_ref=own.at[a, blocks_of(shard)],
            send_sem=g_send.at[a, way, slot],
            recv_sem=g_recv.at[a, shard],
            device_id=peers[way],
            device_id_type=MESH,
        )

    def x_copy(a, shard, slot):
        return pltpu.make_async_remote_copy(
            src_ref=own.at[a, blocks_of(shard)],
            dst_ref=oth[a].at[blocks_of(shard)],
            send_sem=g_send.at[a, PAIR, slot],
            recv_sem=o_recv.at[a, shard],
            device_id=peers[PAIR],
            device_id_type=MESH,
        )

    def o_copy(a, way, shard, slot):
        return pltpu.make_async_remote_copy(
            src_ref=oth[a].at[blocks_of(shard)],
            dst_ref=oth[a].at[blocks_of(shard)],
            send_sem=o_send.at[a, (SIDE, MATE, ACROSS).index(way), slot],
            recv_sem=o_recv.at[a, shard],
            device_id=peers[way],
            device_id_type=MESH,
        )

    def own_ways(far, i, a, act):
        place, shard, slot = place_of(i), shard_of(far, i, c), far * n_chip + i
        near = far == 0
        lined = (a == 1) & ((place == 0) | (place == last))
        along = near | lined
        act(g_copy(a, SIDE, shard, slot))
        pl.when(along & (place <= z) & not_last)(lambda: act(g_copy(a, ALONG_UP, shard, slot)))
        pl.when(along & (place >= z) & not_first)(lambda: act(g_copy(a, ALONG_DOWN, shard, slot)))
        across = near & (jnp.logical_not(lined) | (place == z))
        pl.when(across)(lambda: act(g_copy(a, ACROSS, shard, slot)))
        crossed = (far == 1) & (i == 2)
        pl.when((a == 0) & (i != 1) & jnp.logical_not(crossed))(lambda: act(x_copy(0, shard, slot)))
        pl.when((a == 1) & ((i == 0) | (i == 2)))(lambda: act(x_copy(1, shard, slot)))

    def assemble(a, shard):
        for j in range(rows):
            for b in range(per):
                dense[j * width : (j + 1) * width, b * width : (b + 1) * width] = wts[
                    a, j, inv[a, j, shard * per + b]
                ]

    def service(far, i, a):
        shard, slot = shard_of(far, i, c), far * n_chip + i
        o_copy(a, SIDE, shard, slot).wait_recv()
        o_copy(a, SIDE, shard, slot).start()

    def mate_service(far, a):
        o_copy(a, MATE, shard_of(far, 0, c), far * n_chip).start()

    def cross_over():
        return o_copy(0, ACROSS, shard_of(0, 2, c), 2)

    def gather_step(n, carry):
        @pl.when(n < units)
        def _():
            far, i, a = unit_of(n)
            pl.when(n > 1)(lambda: g_copy(a, SIDE, shard_of(far, i, c), 0).wait_recv())
            own_ways(far, i, a, lambda d: d.start())

        for far, at in ((0, units // 2 - 1), (1, units - 5)):

            @pl.when(n == at)
            def _():
                for a in range(2):
                    service(far, 0, a)
                    pl.when(jnp.logical_not(inner))(lambda: mate_service(far, a))

        if n_chip > 2:

            @pl.when(n == units - 3)
            def _():
                service(0, 2, 0)
                cross_over().start()

        @pl.when(n == 0)
        def _():
            for m in weights:
                m.wait()
            for a in range(2):
                wts[a, :, count] = jnp.zeros((rows, width, width), wts.dtype)
            pre[...] = jnp.zeros_like(pre)

        def unit(sib, carry):
            now = n - sib

            @pl.when((now >= 0) & (now < units))
            def _():
                far, i, a = unit_of(now)
                shard = shard_of(far, i, jnp.where(sib == 1, 1 - c, c))
                pl.when(sib == 1)(lambda: g_copy(a, SIDE, shard, 0).wait_recv())
                assemble(a, shard)
                taken = [own[a, shard * per + b] for b in range(per)]
                pre[a] += lax.dot_general(
                    dense[...],
                    jnp.concatenate(taken, axis=1),
                    NT,
                    preferred_element_type=jnp.float32,
                )

            return carry

        lax.fori_loop(0, 2, unit, 0)
        return carry

    lax.fori_loop(0, units + 1, gather_step, 0)

    def gates(j, carry):
        at = pl.ds(pl.multiple_of(j * width, width), width)
        p, h = pre[0, at, :], pre[1, at, :]
        sig = 1.0 / (1.0 + jnp.exp(-p))
        act = (p * sig).astype(jnp.bfloat16)
        grad_f = h * sig * (1.0 + p * (1.0 - sig))
        grad = grad_f.astype(jnp.bfloat16)
        for f in range(2):
            lhs[0, f, j] = grad[f * half : (f + 1) * half]
            lhs[1, f, j] = act[f * half : (f + 1) * half]
        back[:, at] = grad_f.T.astype(jnp.bfloat16)
        return carry

    lax.fori_loop(0, rows, gates, 0)

    def l_copy(a):
        return pltpu.make_async_remote_copy(
            src_ref=lhs.at[a, 1 - dp],
            dst_ref=lhs_o.at[a],
            send_sem=l_send.at[a],
            recv_sem=l_recv.at[a],
            device_id=peers[PAIR],
            device_id_type=MESH,
        )

    def late_ways(act):
        for i in range(3, n_chip):
            for far in range(2):
                act(x_copy(1, shard_of(far, i, c), far * n_chip + i))

    l_copy(0).start()
    l_copy(1).start()
    late_ways(lambda d: d.start())

    @pl.when(inner)
    def _():
        for a in range(2):
            for far in range(2):
                mate_service(far, a)

    def copy(way, source, target, slot):
        return pltpu.make_async_remote_copy(
            src_ref=source,
            dst_ref=target,
            send_sem=s_send.at[way, slot],
            recv_sem=s_recv.at[way, slot],
            device_id=peers[way],
            device_id_type=MESH,
        )

    def side_copy(column, place):
        slot = column * n_chip + place
        return copy(SIDE, part.at[(column * 2 + 1 - c) * n_chip + place], side.at[slot], slot)

    def cross_copy(place):
        return copy(ACROSS, cross_out.at[place], cross.at[place], place)

    def up_copy(place):
        return copy(ALONG_UP, line_out.at[place], up_in.at[place], place)

    def down_copy(place):
        return copy(ALONG_DOWN, line_out.at[place], down_in.at[place], place)

    chunk = 32 if tok % 32 == 0 else tok

    def total(store, terms):
        def body(i, carry):
            at = pl.ds(pl.multiple_of(i * chunk, chunk), chunk)
            value = None
            for ref, slot in terms:
                term = ref[slot, at, :].astype(jnp.float32)
                value = term if value is None else value + term
            store(at, value.astype(jnp.bfloat16))
            return carry

        lax.fori_loop(0, tok // chunk, body, 0)

    def to(ref, slot):
        def store(at, value):
            ref[slot, at, :] = value

        return store

    def to_out(at, value):
        in_ref[at, :] = value

    def pieces(column, place):
        def body(q, carry):
            core = jnp.where(q == 0, 1 - c, c)
            shard = (column * 2 + core) * n_chip + place
            assemble(0, shard)
            part[shard] = jnp.dot(
                back[...], dense[...], preferred_element_type=jnp.float32
            ).astype(jnp.bfloat16)
            pl.when(q == 0)(lambda: side_copy(column, place).start())
            return carry

        lax.fori_loop(0, 2, body, 0)

    def piece_step(r, carry):
        @pl.when((r > 0) & (r <= n_chip))
        def _():
            place = place_of(n_chip - r)
            slot = (1 - y) * n_chip + place
            side_copy(1 - y, place).wait_recv()
            total(to(cross_out, place), [(part, ((1 - y) * 2 + c) * n_chip + place), (side, slot)])
            cross_copy(place).start()

        column = jnp.where(r < n_chip, 1 - y, y)
        pieces(column, place_of(n_chip - 1 - r % n_chip))
        return carry

    lax.fori_loop(0, events, piece_step, 0)

    def line_step(place):
        slot = y * n_chip + place
        side_copy(y, place).wait_recv()
        cross_copy(place).wait_recv()
        base = [(part, (y * 2 + c) * n_chip + place), (side, slot), (cross, place)]

        @pl.when(place > z)
        def _():
            @pl.when(not_first)
            def _():
                up_copy(place).wait_recv()
                total(to(line_out, place), base + [(up_in, place)])

            @pl.when(jnp.logical_not(not_first))
            def _():
                total(to(line_out, place), base)

            up_copy(place).start()

        @pl.when(place < z)
        def _():
            @pl.when(not_last)
            def _():
                down_copy(place).wait_recv()
                total(to(line_out, place), base + [(down_in, place)])

            @pl.when(jnp.logical_not(not_last))
            def _():
                total(to(line_out, place), base)

            down_copy(place).start()

        @pl.when(place == z)
        def _():
            @pl.when(inner)
            def _():
                up_copy(place).wait_recv()
                down_copy(place).wait_recv()
                total(to_out, base + [(up_in, place), (down_in, place)])

            @pl.when(jnp.logical_not(not_first))
            def _():
                down_copy(place).wait_recv()
                total(to_out, base + [(down_in, place)])

            @pl.when(jnp.logical_not(not_last))
            def _():
                up_copy(place).wait_recv()
                total(to_out, base + [(up_in, place)])

    cols, outs = (up_cols, down_cols), (up_ref, down_ref)
    step = 4 if count % 4 == 0 else 1

    def grad_row(a, left, source, j, add):
        for first in range(0, count, step):
            picked = [source(cols[a][j, k]) for k in range(first, first + step)]
            value = jnp.dot(
                left, jnp.concatenate(picked, axis=1), preferred_element_type=jnp.float32
            )
            for i in range(step):
                block = value[:, i * width : (i + 1) * width]
                if add:
                    outs[a][j, first + i] += block
                else:
                    outs[a][j, first + i] = block

    share = -(-rows // (n_chip - 1))

    def line_rows(r):
        def body(j, carry):
            for a in range(2):
                grad_row(a, lhs[a, dp, j], lambda col, a=a: own[a, col], j, False)
            return carry

        lax.fori_loop(min(r * share, rows), min((r + 1) * share, rows), body, 0)

    far_near = [(far, i) for i in range(3, n_chip) for far in range(2)]
    early = {0: [(far, i, 0) for far, i in far_near], 1: [(0, 1, 0), (1, 1, 0)]}
    if n_chip > 2:
        early[0] += [(1, 2, 0), (0, 2, 1), (1, 2, 1)]
    early[n_chip - 2] = early.get(n_chip - 2, []) + [(0, 1, 1), (1, 1, 1)]
    for r in range(n_chip):
        line_step(place_of(n_chip - 1 - r))
        for far, i, a in early.get(r, []):
            service(far, i, a)
        if r < n_chip - 1:
            line_rows(r)

    for a in range(2):
        if a == 1:
            for far, i in far_near:
                service(far, i, a)
        for far in range(2):
            for i in range(n_chip):
                o_copy(a, SIDE, shard_of(far, i, 1 - c), far * n_chip + i).wait_recv()
        l_copy(a).wait_recv()

        def body(j, carry, a=a):
            grad_row(a, lhs_o[a, j], lambda col: oth[a][col], j, True)
            return carry

        lax.fori_loop(0, rows, body, 0)

    def settle(n, carry):
        far, i, a = unit_of(n)
        own_ways(far, i, a, lambda d: d.wait_send())
        return carry

    lax.fori_loop(0, units, settle, 0)
    if n_chip > 2:
        cross_over().wait_send()
    late_ways(lambda d: d.wait_send())
    for a in range(2):
        for far in range(2):
            for i in range(n_chip):
                o_copy(a, SIDE, shard_of(far, i, c), far * n_chip + i).wait_send()
            o_copy(a, MATE, shard_of(far, 0, c), far * n_chip).wait_send()
        l_copy(a).wait_send()

    def settle_sum(place, carry):
        side_copy(1 - y, place).wait_send()
        side_copy(y, place).wait_send()
        cross_copy(place).wait_send()
        pl.when(place > z)(lambda: up_copy(place).wait_send())
        pl.when(place < z)(lambda: down_copy(place).wait_send())
        return carry

    lax.fori_loop(0, n_chip, settle_sum, 0)


def fused_call(n_hst, n_chip, tokens, out_grad, up_blocks, up_cols, down_blocks, down_cols):
    rows, count, width, _ = up_blocks.shape
    tok, part = tokens.shape
    shards = n_hst * n_chip
    blocks = shards * part // width
    names = jnp.arange(blocks, dtype=jnp.int32)
    ranks = jnp.arange(count, dtype=jnp.int32)[None, None, :, None] - count
    cols = jnp.stack([up_cols, down_cols])
    hits = cols[:, :, :, None] == names
    inv = jnp.sum(jnp.where(hits, ranks, 0), axis=2, dtype=jnp.int32) + count
    hidden = rows * width
    bf, f32 = jnp.bfloat16, jnp.float32
    dma = pltpu.SemaphoreType.DMA
    whole = pl.BlockSpec(memory_space=pltpu.VMEM)
    smem = pl.BlockSpec(memory_space=pltpu.SMEM)
    anywhere = pl.BlockSpec(memory_space=pl.ANY)
    grads = jax.ShapeDtypeStruct((rows, count, width // 2, width), f32)

    def slots(amount):
        return pltpu.VMEM((amount, tok, part), bf)

    return pl.pallas_call(
        functools.partial(fused_kernel, n_chip),
        in_specs=[smem] * 3 + [anywhere] * 4,
        out_specs=[whole] * 3,
        out_shape=[jax.ShapeDtypeStruct((tok, part), bf), grads, grads],
        scratch_shapes=[
            pltpu.VMEM((2, blocks, tok, width), bf),
            pltpu.VMEM((blocks, tok, width), bf),
            pltpu.VMEM((blocks, tok, width), bf),
            pltpu.VMEM((2, rows, count + 1, width, width), bf),
            pltpu.VMEM((hidden, part), bf),
            pltpu.VMEM((2, hidden, tok), f32),
            pltpu.VMEM((2, 2, rows, width // 2, tok), bf),
            pltpu.VMEM((2, rows, width // 2, tok), bf),
            pltpu.VMEM((tok, hidden), bf),
            slots(shards),
            slots(2 * n_chip),
        ]
        + [slots(n_chip)] * 5
        + [
            dma((2, 6, 2 * n_chip)),
            dma((2, shards)),
            dma((2, 3, 2 * n_chip)),
            dma((2, shards)),
            dma((2,)),
            dma((2,)),
            dma((4, 2 * n_chip)),
            dma((4, 2 * n_chip)),
            dma((2, part // width)),
            dma((2,)),
        ],
        compiler_params=pltpu.CompilerParams(
            collective_id=2, has_side_effects=True, vmem_limit_bytes=58 * 2**20
        ),
        cost_estimate=pl.CostEstimate(
            flops=22 * tok * hidden * shards * part // 4,
            bytes_accessed=20 * 2**20,
            transcendentals=hidden * tok,
        ),
    )(inv, up_cols, down_cols, tokens, out_grad, up_blocks, down_blocks)


def local(n_dp, n_hst, n_chip, tokens, out_grad, up_blocks, up_cols, down_blocks, down_cols):
    if n_dp == 2 and n_hst == 4 and n_chip >= 2 and n_chip % 2 == 0:
        return tuple(
            fused_call(
                n_hst, n_chip, tokens, out_grad, up_blocks, up_cols, down_blocks, down_cols
            )
        )
    whole_x, whole_dy = gather_call(n_hst, n_chip, tokens, out_grad)
    split = n_dp == 2
    partial_value, *grads = rows_call(
        split, whole_x, whole_dy, up_blocks, up_cols, down_blocks, down_cols
    )
    if split:
        swap = [(0, 1), (1, 0)]
        sums = [
            grads[i].astype(jnp.float32)
            + lax.ppermute(grads[i + 1], "dp", swap).astype(jnp.float32)
            for i in (0, 2)
        ]
    else:
        sums = [
            lax.psum_scatter(g, "dp", scatter_dimension=2, tiled=True).astype(jnp.float32)
            for g in grads
        ]
    summed = scatter_call(n_hst, n_chip, partial_value)
    return (summed, *sums)


def solution(mesh):
    placed = (
        P("dp", ("hst", "chip")),
        P("dp", ("hst", "chip")),
        P(("hst", "chip"), None, None, None),
        P(("hst", "chip"), None),
        P(("hst", "chip"), None, None, None),
        P(("hst", "chip"), None),
    )
    return jax.shard_map(
        functools.partial(local, mesh.shape["dp"], mesh.shape["hst"], mesh.shape["chip"]),
        mesh=mesh,
        in_specs=placed,
        out_specs=(
            P("dp", ("hst", "chip")),
            P(("hst", "chip"), None, "dp", None),
            P(("hst", "chip"), None, "dp", None),
        ),
        check_vma=False,
    )
```

```python
import functools

import jax
import jax.numpy as jnp
from jax import lax
from jax.experimental import pallas as pl
from jax.experimental.pallas import tpu as pltpu
from jax.sharding import PartitionSpec as P

NT = (((1,), (1,)), ((), ()))


def rows_kernel(
    split,
    up_cols,
    down_cols,
    me,
    x_ref,
    dy_ref,
    up_ref,
    down_ref,
    in_ref,
    *rest,
):
    outs, (acc, xs, dys, us, ds) = rest[:-5], rest[-5:]
    row = pl.program_id(0)
    width = up_ref.shape[-1]
    per_shard = x_ref.shape[2] // width
    count = up_ref.shape[1]

    @pl.when(row == 0)
    def _():
        acc[...] = jnp.zeros_like(acc)

    def place(col):
        return col // per_shard, pl.ds(pl.multiple_of((col % per_shard) * width, width), width)

    for k in range(count):
        lanes = pl.ds(k * width, width)
        shard, at = place(up_cols[row, k])
        xs[:, lanes] = x_ref[shard, :, at]
        shard, at = place(down_cols[row, k])
        dys[:, lanes] = dy_ref[shard, :, at]
        us[:, lanes] = up_ref[0, k]
        ds[:, lanes] = down_ref[0, k]
    pre = lax.dot_general(us[...], xs[...], NT, preferred_element_type=jnp.float32)
    hid = lax.dot_general(ds[...], dys[...], NT, preferred_element_type=jnp.float32)
    sig = 1.0 / (1.0 + jnp.exp(-pre))
    act = (pre * sig).astype(jnp.bfloat16)
    pre_grad_f = hid * sig * (1.0 + pre * (1.0 - sig))
    pre_grad = pre_grad_f.astype(jnp.bfloat16)
    pre_grad_t = pre_grad_f.T.astype(jnp.bfloat16)

    step = 4
    for base in range(0, count, step):
        lanes = pl.ds(base * width, step * width)
        up_part = jnp.dot(pre_grad, xs[:, lanes], preferred_element_type=jnp.float32)
        down_part = jnp.dot(act, dys[:, lanes], preferred_element_type=jnp.float32)
        back = jnp.dot(pre_grad_t, us[:, lanes], preferred_element_type=jnp.float32)
        for i in range(step):
            k = base + i
            cut = slice(i * width, (i + 1) * width)
            for part, out in ((up_part, outs[: len(outs) // 2]), (down_part, outs[len(outs) // 2 :])):
                block = part[:, cut].astype(jnp.bfloat16)
                if split:
                    half = width // 2
                    first = me[0] == 0
                    out[0][0, k] = jnp.where(first, block[:half], block[half:])
                    out[1][0, k] = jnp.where(first, block[half:], block[:half])
                else:
                    out[0][0, k] = block
            shard, at = place(up_cols[row, k])
            acc[shard, :, at] += back[:, cut]

    @pl.when(row == pl.num_programs(0) - 1)
    def _():
        for s in range(acc.shape[0]):
            in_ref[s] = acc[s].astype(jnp.bfloat16)


def rows_call(split, whole_x, whole_dy, up_blocks, up_cols, down_blocks, down_cols):
    rows, count, width, _ = up_blocks.shape
    shards, tok, part = whole_x.shape
    out_h = width // 2 if split else width
    n_out = 4 if split else 2
    whole = pl.BlockSpec(memory_space=pltpu.VMEM)
    smem = pl.BlockSpec(memory_space=pltpu.SMEM)

    def block(h):
        return pl.BlockSpec((1, count, h, width), lambda r: (r, 0, 0, 0))

    me = lax.axis_index("dp").astype(jnp.int32).reshape(1)
    flops = 10 * tok * rows * count * width * width
    return pl.pallas_call(
        functools.partial(rows_kernel, split),
        grid=(rows,),
        in_specs=[smem, smem, smem, whole, whole, block(width), block(width)],
        out_specs=[whole] + [block(out_h)] * n_out,
        out_shape=[jax.ShapeDtypeStruct(whole_x.shape, jnp.bfloat16)]
        + [jax.ShapeDtypeStruct((rows, count, out_h, width), jnp.bfloat16)] * n_out,
        scratch_shapes=[
            pltpu.VMEM(whole_x.shape, jnp.float32),
            pltpu.VMEM((tok, count * width), jnp.bfloat16),
            pltpu.VMEM((tok, count * width), jnp.bfloat16),
            pltpu.VMEM((width, count * width), jnp.bfloat16),
            pltpu.VMEM((width, count * width), jnp.bfloat16),
        ],
        compiler_params=pltpu.CompilerParams(
            dimension_semantics=("arbitrary",), vmem_limit_bytes=56 * 2**20
        ),
        cost_estimate=pl.CostEstimate(
            flops=flops, bytes_accessed=30 * 2**20, transcendentals=rows * width * tok
        ),
    )(up_cols, down_cols, me, whole_x, whole_dy, up_blocks, down_blocks)


MESH = pl.DeviceIdType.MESH
ALONG_UP, ALONG_DOWN, ACROSS, SIDE = range(4)


def gather_kernel(n_chip, x_ref, dy_ref, x_out, dy_out, send_sem, recv_sem, own_sem):
    hst, z = lax.axis_index("hst"), lax.axis_index("chip")
    far, c = hst // 2, hst % 2
    own = hst * n_chip + z
    ins, outs = (x_ref, dy_ref), (x_out, dy_out)
    not_last, not_first = z < n_chip - 1, z > 0
    peers = {
        ALONG_UP: {"hst": hst, "chip": (z + 1) % n_chip},
        ALONG_DOWN: {"hst": hst, "chip": (z + n_chip - 1) % n_chip},
        ACROSS: {"hst": (1 - far) * 2 + c, "chip": z},
        SIDE: {"hst": far * 2 + 1 - c, "chip": z},
    }

    barrier = pltpu.get_barrier_semaphore()

    def greet(way):
        pl.semaphore_signal(barrier, inc=1, device_id=peers[way], device_id_type=MESH)

    greet(ACROSS)
    greet(SIDE)
    pl.when(not_last)(lambda: greet(ALONG_UP))
    pl.when(not_first)(lambda: greet(ALONG_DOWN))
    inner = jnp.logical_and(not_last, not_first)
    pl.when(inner)(lambda: pl.semaphore_wait(barrier, 4))
    pl.when(jnp.logical_not(inner))(lambda: pl.semaphore_wait(barrier, 3))

    def copy(a, way, shard, source=None):
        return pltpu.make_async_remote_copy(
            src_ref=outs[a].at[shard] if source is None else source,
            dst_ref=outs[a].at[shard],
            send_sem=send_sem.at[a, way, shard],
            recv_sem=recv_sem.at[a, shard],
            device_id=peers[way],
            device_id_type=MESH,
        )

    def each(act):
        for t in range(n_chip + 1):
            for a in range(2):
                if t == 0:
                    act(a, (), own, None, True)
                elif t < n_chip:
                    below = z - t
                    act(a, (ALONG_UP,), hst * n_chip + below, below >= 0, False)
                    above = z + t
                    act(a, (ALONG_DOWN,), hst * n_chip + above, above < n_chip, False)
            for a in range(2):
                if t >= 1:
                    base = ((1 - far) * 2 + c) * n_chip
                    if t == 1:
                        act(a, None, base + z, None, False)
                    else:
                        act(a, None, base + z - (t - 1), z - (t - 1) >= 0, False)
                        act(a, None, base + z + (t - 1), z + (t - 1) < n_chip, False)

    def guarded(condition, run):
        if condition is None:
            run()
        else:
            pl.when(condition)(run)

    def forward(a, ways, shard, condition, is_own):
        def run():
            if not is_own:
                copy(a, SIDE, shard).wait_recv()
            source = ins[a] if is_own else None
            if ways is not None:
                if is_own or ALONG_UP in ways:
                    pl.when(not_last)(lambda: copy(a, ALONG_UP, shard, source).start())
                if is_own or ALONG_DOWN in ways:
                    pl.when(not_first)(lambda: copy(a, ALONG_DOWN, shard, source).start())
                copy(a, ACROSS, shard, source).start()
            copy(a, SIDE, shard, source).start()

        guarded(condition, run)

    def finish(a, ways, shard, condition, is_own):
        def run():
            source = ins[a] if is_own else None
            if ways is not None:
                if is_own or ALONG_UP in ways:
                    pl.when(not_last)(lambda: copy(a, ALONG_UP, shard, source).wait_send())
                if is_own or ALONG_DOWN in ways:
                    pl.when(not_first)(lambda: copy(a, ALONG_DOWN, shard, source).wait_send())
                copy(a, ACROSS, shard, source).wait_send()
            copy(a, SIDE, shard, source).wait_send()

        guarded(condition, run)

    each(forward)
    mine = [pltpu.make_async_copy(ins[a], outs[a].at[own], own_sem.at[a]) for a in range(2)]
    for m in mine:
        m.start()
    for half in range(2):
        for place in range(n_chip):
            for a in range(2):
                copy(a, SIDE, (half * 2 + 1 - c) * n_chip + place).wait_recv()
    each(finish)
    for m in mine:
        m.wait()


def gather_call(n_hst, n_chip, tokens, out_grad):
    if n_hst != 4:
        return [
            lax.all_gather(v, ("hst", "chip"), axis=0, tiled=False) for v in (tokens, out_grad)
        ]
    shards = n_hst * n_chip
    return pl.pallas_call(
        functools.partial(gather_kernel, n_chip),
        in_specs=[pl.BlockSpec(memory_space=pltpu.VMEM)] * 2,
        out_specs=[pl.BlockSpec(memory_space=pl.ANY)] * 2,
        out_shape=[jax.ShapeDtypeStruct((shards, *v.shape), v.dtype) for v in (tokens, out_grad)],
        scratch_shapes=[
            pltpu.SemaphoreType.DMA((2, 4, shards)),
            pltpu.SemaphoreType.DMA((2, shards)),
            pltpu.SemaphoreType.DMA((2,)),
        ],
        compiler_params=pltpu.CompilerParams(collective_id=0, has_side_effects=True),
    )(tokens, out_grad)


def scatter_kernel(n_chip, part, out, side, cross, up, down, cross_out, line_out, send_sem, recv_sem):
    hst, z = lax.axis_index("hst"), lax.axis_index("chip")
    far, c = hst // 2, hst % 2
    not_last, not_first = z < n_chip - 1, z > 0
    peers = {
        ALONG_UP: {"hst": hst, "chip": (z + 1) % n_chip},
        ALONG_DOWN: {"hst": hst, "chip": (z + n_chip - 1) % n_chip},
        ACROSS: {"hst": (1 - far) * 2 + c, "chip": z},
        SIDE: {"hst": far * 2 + 1 - c, "chip": z},
    }
    barrier = pltpu.get_barrier_semaphore()

    def greet(way):
        pl.semaphore_signal(barrier, inc=1, device_id=peers[way], device_id_type=MESH)

    greet(ACROSS)
    greet(SIDE)
    pl.when(not_last)(lambda: greet(ALONG_UP))
    pl.when(not_first)(lambda: greet(ALONG_DOWN))
    inner = jnp.logical_and(not_last, not_first)
    pl.when(inner)(lambda: pl.semaphore_wait(barrier, 4))
    pl.when(jnp.logical_not(inner))(lambda: pl.semaphore_wait(barrier, 3))

    def copy(way, source, target, slot):
        return pltpu.make_async_remote_copy(
            src_ref=source,
            dst_ref=target,
            send_sem=send_sem.at[way, slot],
            recv_sem=recv_sem.at[way, slot],
            device_id=peers[way],
            device_id_type=MESH,
        )

    def side_copy(half, place):
        slot = half * n_chip + place
        return copy(SIDE, part.at[(half * 2 + 1 - c) * n_chip + place], side.at[slot], slot)

    def cross_copy(place):
        return copy(ACROSS, cross_out.at[place], cross.at[place], place)

    def up_copy(place):
        return copy(ALONG_UP, line_out.at[place], up.at[place], place)

    def down_copy(place):
        return copy(ALONG_DOWN, line_out.at[place], down.at[place], place)

    def each(act):
        for t in range(n_chip - 1, 0, -1):
            pl.when(z + t < n_chip)(lambda t=t: act(z + t, 1))
            pl.when(z - t >= 0)(lambda t=t: act(z - t, -1))
        act(z, 0)

    rows = part.shape[1]
    chunk = 32 if rows % 32 == 0 else rows

    def total(store, terms):
        def body(i, carry):
            at = pl.ds(pl.multiple_of(i * chunk, chunk), chunk)
            value = None
            for ref, slot in terms:
                term = ref[slot, at, :].astype(jnp.float32)
                value = term if value is None else value + term
            store(at, value.astype(jnp.bfloat16))
            return carry

        lax.fori_loop(0, rows // chunk, body, 0)

    def to(ref, slot):
        def store(at, value):
            ref[slot, at, :] = value

        return store

    def to_out(at, value):
        out[at, :] = value

    each(lambda place, _: side_copy(1 - far, place).start())
    each(lambda place, _: side_copy(far, place).start())

    def cross_step(place, _):
        slot = (1 - far) * n_chip + place
        side_copy(1 - far, place).wait_recv()
        total(to(cross_out, place), [(part, ((1 - far) * 2 + c) * n_chip + place), (side, slot)])
        cross_copy(place).start()

    each(cross_step)

    def line_step(place, sign):
        slot = far * n_chip + place
        side_copy(far, place).wait_recv()
        cross_copy(place).wait_recv()
        base = [(part, (far * 2 + c) * n_chip + place), (side, slot), (cross, place)]
        if sign > 0:

            @pl.when(not_first)
            def _():
                up_copy(place).wait_recv()
                total(to(line_out, place), base + [(up, place)])

            @pl.when(jnp.logical_not(not_first))
            def _():
                total(to(line_out, place), base)

            up_copy(place).start()
        elif sign < 0:

            @pl.when(not_last)
            def _():
                down_copy(place).wait_recv()
                total(to(line_out, place), base + [(down, place)])

            @pl.when(jnp.logical_not(not_last))
            def _():
                total(to(line_out, place), base)

            down_copy(place).start()
        else:

            @pl.when(inner)
            def _():
                up_copy(place).wait_recv()
                down_copy(place).wait_recv()
                total(to_out, base + [(up, place), (down, place)])

            @pl.when(jnp.logical_not(not_first))
            def _():
                down_copy(place).wait_recv()
                total(to_out, base + [(down, place)])

            @pl.when(jnp.logical_not(not_last))
            def _():
                up_copy(place).wait_recv()
                total(to_out, base + [(up, place)])

    each(line_step)

    def finish(place, sign):
        side_copy(1 - far, place).wait_send()
        side_copy(far, place).wait_send()
        cross_copy(place).wait_send()
        if sign > 0:
            up_copy(place).wait_send()
        elif sign < 0:
            down_copy(place).wait_send()

    each(finish)


def scatter_call(n_hst, n_chip, part):
    if n_hst != 4 or n_chip < 2:
        return lax.psum_scatter(part, ("hst", "chip"), scatter_dimension=0, tiled=False)
    shards, rows, width = part.shape
    whole = pl.BlockSpec(memory_space=pltpu.VMEM)

    def slots(count):
        return pltpu.VMEM((count, rows, width), jnp.bfloat16)

    return pl.pallas_call(
        functools.partial(scatter_kernel, n_chip),
        in_specs=[whole],
        out_specs=whole,
        out_shape=jax.ShapeDtypeStruct((rows, width), jnp.bfloat16),
        scratch_shapes=[slots(2 * n_chip)]
        + [slots(n_chip)] * 5
        + [pltpu.SemaphoreType.DMA((4, 2 * n_chip))] * 2,
        compiler_params=pltpu.CompilerParams(
            collective_id=1, has_side_effects=True, vmem_limit_bytes=24 * 2**20
        ),
        cost_estimate=pl.CostEstimate(
            flops=shards * rows * width, bytes_accessed=120 * 2**20, transcendentals=0
        ),
    )(part)

PAIR, MATE = 4, 5


def fused_kernel(
    n_chip,
    inv,
    up_cols,
    down_cols,
    tokens,
    out_grad,
    up_hbm,
    down_hbm,
    in_ref,
    up_ref,
    down_ref,
    oth_dy,
    left_dy,
    own,
    oth_x,
    wts,
    dense,
    pre,
    lhs,
    left_x,
    back,
    part,
    side,
    cross,
    cross_out,
    up_in,
    down_in,
    line_out,
    g_send,
    g_recv,
    o_send,
    o_recv,
    l_send,
    l_recv,
    s_send,
    s_recv,
    own_sem,
    w_sem,
):
    dp, hst, z = lax.axis_index("dp"), lax.axis_index("hst"), lax.axis_index("chip")
    y, c = hst // 2, hst % 2
    _, rows, count_1, width, _ = wts.shape
    count = count_1 - 1
    tok = back.shape[0]
    per = dense.shape[1] // width
    half = width // 2
    events = 2 * n_chip
    not_last, not_first = z < n_chip - 1, z > 0
    inner = jnp.logical_and(not_last, not_first)
    toward = 1 - 2 * (z % 2)
    peers = {
        ALONG_UP: {"dp": dp, "hst": hst, "chip": (z + 1) % n_chip},
        ALONG_DOWN: {"dp": dp, "hst": hst, "chip": (z + n_chip - 1) % n_chip},
        ACROSS: {"dp": dp, "hst": (1 - y) * 2 + c, "chip": z},
        SIDE: {"dp": dp, "hst": y * 2 + 1 - c, "chip": z},
        PAIR: {"dp": 1 - dp, "hst": hst, "chip": z},
        MATE: {"dp": dp, "hst": hst, "chip": z + toward},
    }
    ins, oth = (tokens, out_grad), (oth_x, oth_dy)
    mine = hst * n_chip + z

    def blocks_of(shard):
        return pl.ds(shard * per, per)

    locals_ = [
        pltpu.make_async_copy(
            ins[a].at[:, pl.ds(b * width, width)], own.at[a, mine * per + b], own_sem.at[a, b]
        )
        for a in range(2)
        for b in range(per)
    ]
    weights = [
        pltpu.make_async_copy(w, wts.at[a, :, pl.ds(0, count)], w_sem.at[a])
        for a, w in enumerate((up_hbm, down_hbm))
    ]
    for m in locals_ + weights:
        m.start()

    barrier = pltpu.get_barrier_semaphore()

    def greet(way):
        pl.semaphore_signal(barrier, inc=1, device_id=peers[way], device_id_type=MESH)

    for way in (ACROSS, SIDE, PAIR):
        greet(way)
    pl.when(not_last)(lambda: greet(ALONG_UP))
    pl.when(not_first)(lambda: greet(ALONG_DOWN))
    pl.when(inner)(lambda: pl.semaphore_wait(barrier, 5))
    pl.when(jnp.logical_not(inner))(lambda: pl.semaphore_wait(barrier, 4))

    for m in locals_:
        m.wait()

    short = jnp.minimum(z, n_chip - 1 - z)

    def place_of(i):
        both = z + toward * (2 * (i % 2) - 1) * ((i + 1) // 2)
        return jnp.where(i <= 2 * short, both, jnp.where(2 * z < n_chip - 1, i, n_chip - 1 - i))

    last = n_chip - 1
    order = [(0, 0, 0), (0, 0, 1)]
    for i in range(1, n_chip):
        order += [(0, i, 0), (1, i - 1, 0), (0, i, 1), (1, i - 1, 1)]
    order += [(1, last, 1), (1, last, 0)]
    units = len(order)

    def pick(n, values):
        found = values[0]
        for m in range(1, len(values)):
            found = jnp.where(n == m, values[m], found)
        return found

    def unit_of(n):
        return tuple(pick(n, [u[m] for u in order]) for m in range(3))

    def shard_of(far, i, core):
        column = far * (1 - y) + (1 - far) * y
        return (column * 2 + core) * n_chip + place_of(i)

    def g_copy(a, way, shard, slot):
        return pltpu.make_async_remote_copy(
            src_ref=own.at[a, blocks_of(shard)],
            dst_ref=own.at[a, blocks_of(shard)],
            send_sem=g_send.at[a, way, slot],
            recv_sem=g_recv.at[a, shard],
            device_id=peers[way],
            device_id_type=MESH,
        )

    def x_copy(a, shard, slot):
        return pltpu.make_async_remote_copy(
            src_ref=own.at[a, blocks_of(shard)],
            dst_ref=oth[a].at[blocks_of(shard)],
            send_sem=g_send.at[a, PAIR, slot],
            recv_sem=o_recv.at[a, shard],
            device_id=peers[PAIR],
            device_id_type=MESH,
        )

    def o_copy(a, way, shard, slot):
        return pltpu.make_async_remote_copy(
            src_ref=oth[a].at[blocks_of(shard)],
            dst_ref=oth[a].at[blocks_of(shard)],
            send_sem=o_send.at[a, (SIDE, MATE, ACROSS).index(way), slot],
            recv_sem=o_recv.at[a, shard],
            device_id=peers[way],
            device_id_type=MESH,
        )

    def own_ways(far, i, a, act):
        place, shard, slot = place_of(i), shard_of(far, i, c), far * n_chip + i
        near = far == 0
        lined = (a == 1) & ((place == 0) | (place == last))
        along = near | lined
        act(g_copy(a, SIDE, shard, slot))
        pl.when(along & (place <= z) & not_last)(lambda: act(g_copy(a, ALONG_UP, shard, slot)))
        pl.when(along & (place >= z) & not_first)(lambda: act(g_copy(a, ALONG_DOWN, shard, slot)))
        across = near & (jnp.logical_not(lined) | (place == z))
        pl.when(across)(lambda: act(g_copy(a, ACROSS, shard, slot)))
        crossed = (far == 1) & (i == 2)
        pl.when((a == 0) & (i != 1) & jnp.logical_not(crossed))(lambda: act(x_copy(0, shard, slot)))
        pl.when((a == 1) & ((i == 0) | (i == 2)))(lambda: act(x_copy(1, shard, slot)))

    def assemble(a, shard):
        for j in range(rows):
            for b in range(per):
                dense[j * width : (j + 1) * width, b * width : (b + 1) * width] = wts[
                    a, j, inv[a, j, shard * per + b]
                ]

    def service(far, i, a):
        shard, slot = shard_of(far, i, c), far * n_chip + i
        o_copy(a, SIDE, shard, slot).wait_recv()
        o_copy(a, SIDE, shard, slot).start()

    def mate_service(far, a):
        o_copy(a, MATE, shard_of(far, 0, c), far * n_chip).start()

    def cross_over():
        return o_copy(0, ACROSS, shard_of(0, 2, c), 2)

    def gather_step(n, carry):
        @pl.when(n < units)
        def _():
            far, i, a = unit_of(n)
            pl.when(n > 1)(lambda: g_copy(a, SIDE, shard_of(far, i, c), 0).wait_recv())
            own_ways(far, i, a, lambda d: d.start())

        for far, at in ((0, units // 2 - 1), (1, units - 5)):

            @pl.when(n == at)
            def _():
                for a in range(2):
                    service(far, 0, a)
                    pl.when(jnp.logical_not(inner))(lambda: mate_service(far, a))

        if n_chip > 2:

            @pl.when(n == units - 3)
            def _():
                service(0, 2, 0)
                cross_over().start()

        @pl.when(n == 0)
        def _():
            for m in weights:
                m.wait()
            for a in range(2):
                wts[a, :, count] = jnp.zeros((rows, width, width), wts.dtype)
            pre[...] = jnp.zeros_like(pre)

        def unit(sib, carry):
            now = n - sib

            @pl.when((now >= 0) & (now < units))
            def _():
                far, i, a = unit_of(now)
                shard = shard_of(far, i, jnp.where(sib == 1, 1 - c, c))
                pl.when(sib == 1)(lambda: g_copy(a, SIDE, shard, 0).wait_recv())
                assemble(a, shard)
                taken = [own[a, shard * per + b] for b in range(per)]
                pre[a] += lax.dot_general(
                    dense[...],
                    jnp.concatenate(taken, axis=1),
                    NT,
                    preferred_element_type=jnp.float32,
                )

            return carry

        lax.fori_loop(0, 2, unit, 0)
        return carry

    lax.fori_loop(0, units + 1, gather_step, 0)

    def gates(j, carry):
        at = pl.ds(pl.multiple_of(j * width, width), width)
        p, h = pre[0, at, :], pre[1, at, :]
        sig = 1.0 / (1.0 + jnp.exp(-p))
        act = (p * sig).astype(jnp.bfloat16)
        grad_f = h * sig * (1.0 + p * (1.0 - sig))
        grad = grad_f.astype(jnp.bfloat16)
        for f in range(2):
            lhs[0, f, j] = grad[f * half : (f + 1) * half]
            lhs[1, f, j] = act[f * half : (f + 1) * half]
        back[:, at] = grad_f.T.astype(jnp.bfloat16)
        return carry

    lax.fori_loop(0, rows, gates, 0)

    def l_copy(a):
        return pltpu.make_async_remote_copy(
            src_ref=lhs.at[a, 1 - dp],
            dst_ref=(left_x, left_dy)[a],
            send_sem=l_send.at[a],
            recv_sem=l_recv.at[a],
            device_id=peers[PAIR],
            device_id_type=MESH,
        )

    def late_ways(act):
        for i in range(3, n_chip):
            for far in range(2):
                act(x_copy(1, shard_of(far, i, c), far * n_chip + i))

    l_copy(0).start()
    l_copy(1).start()
    late_ways(lambda d: d.start())

    @pl.when(inner)
    def _():
        for a in range(2):
            for far in range(2):
                mate_service(far, a)

    def copy(way, source, target, slot):
        return pltpu.make_async_remote_copy(
            src_ref=source,
            dst_ref=target,
            send_sem=s_send.at[way, slot],
            recv_sem=s_recv.at[way, slot],
            device_id=peers[way],
            device_id_type=MESH,
        )

    def side_copy(column, place):
        slot = column * n_chip + place
        return copy(SIDE, part.at[(column * 2 + 1 - c) * n_chip + place], side.at[slot], slot)

    def cross_copy(place):
        return copy(ACROSS, cross_out.at[place], cross.at[place], place)

    def up_copy(place):
        return copy(ALONG_UP, line_out.at[place], up_in.at[place], place)

    def down_copy(place):
        return copy(ALONG_DOWN, line_out.at[place], down_in.at[place], place)

    chunk = 32 if tok % 32 == 0 else tok

    def total(store, terms):
        def body(i, carry):
            at = pl.ds(pl.multiple_of(i * chunk, chunk), chunk)
            value = None
            for ref, slot in terms:
                term = ref[slot, at, :].astype(jnp.float32)
                value = term if value is None else value + term
            store(at, value.astype(jnp.bfloat16))
            return carry

        lax.fori_loop(0, tok // chunk, body, 0)

    def to(ref, slot):
        def store(at, value):
            ref[slot, at, :] = value

        return store

    def to_out(at, value):
        in_ref[at, :] = value

    def pieces(column, place):
        def body(q, carry):
            core = jnp.where(q == 0, 1 - c, c)
            shard = (column * 2 + core) * n_chip + place
            assemble(0, shard)
            part[shard] = jnp.dot(
                back[...], dense[...], preferred_element_type=jnp.float32
            ).astype(jnp.bfloat16)
            pl.when(q == 0)(lambda: side_copy(column, place).start())
            return carry

        lax.fori_loop(0, 2, body, 0)

    def piece_step(r, carry):
        @pl.when((r > 0) & (r <= n_chip))
        def _():
            place = place_of(n_chip - r)
            slot = (1 - y) * n_chip + place
            side_copy(1 - y, place).wait_recv()
            total(to(cross_out, place), [(part, ((1 - y) * 2 + c) * n_chip + place), (side, slot)])
            cross_copy(place).start()

        column = jnp.where(r < n_chip, 1 - y, y)
        pieces(column, place_of(n_chip - 1 - r % n_chip))
        return carry

    lax.fori_loop(0, events, piece_step, 0)

    def line_step(place):
        slot = y * n_chip + place
        side_copy(y, place).wait_recv()
        cross_copy(place).wait_recv()
        base = [(part, (y * 2 + c) * n_chip + place), (side, slot), (cross, place)]

        @pl.when(place > z)
        def _():
            @pl.when(not_first)
            def _():
                up_copy(place).wait_recv()
                total(to(line_out, place), base + [(up_in, place)])

            @pl.when(jnp.logical_not(not_first))
            def _():
                total(to(line_out, place), base)

            up_copy(place).start()

        @pl.when(place < z)
        def _():
            @pl.when(not_last)
            def _():
                down_copy(place).wait_recv()
                total(to(line_out, place), base + [(down_in, place)])

            @pl.when(jnp.logical_not(not_last))
            def _():
                total(to(line_out, place), base)

            down_copy(place).start()

        @pl.when(place == z)
        def _():
            @pl.when(inner)
            def _():
                up_copy(place).wait_recv()
                down_copy(place).wait_recv()
                total(to_out, base + [(up_in, place), (down_in, place)])

            @pl.when(jnp.logical_not(not_first))
            def _():
                down_copy(place).wait_recv()
                total(to_out, base + [(down_in, place)])

            @pl.when(jnp.logical_not(not_last))
            def _():
                up_copy(place).wait_recv()
                total(to_out, base + [(up_in, place)])

    cols, outs = (up_cols, down_cols), (up_ref, down_ref)
    step = 4 if count % 4 == 0 else 1

    def grad_row(a, left, source, j, add):
        for first in range(0, count, step):
            picked = [source(cols[a][j, k]) for k in range(first, first + step)]
            value = jnp.dot(
                left, jnp.concatenate(picked, axis=1), preferred_element_type=jnp.float32
            )
            for i in range(step):
                block = value[:, i * width : (i + 1) * width]
                if add:
                    outs[a][j, first + i] += block
                else:
                    outs[a][j, first + i] = block

    share = -(-rows // (n_chip - 1))

    def line_rows(r):
        def body(j, carry):
            for a in range(2):
                grad_row(a, lhs[a, dp, j], lambda col, a=a: own[a, col], j, False)
            return carry

        lax.fori_loop(min(r * share, rows), min((r + 1) * share, rows), body, 0)

    far_near = [(far, i) for i in range(3, n_chip) for far in range(2)]
    early = {0: [(far, i, 0) for far, i in far_near], 1: [(0, 1, 0), (1, 1, 0)]}
    if n_chip > 2:
        early[0] += [(1, 2, 0), (0, 2, 1), (1, 2, 1)]
    early[n_chip - 2] = early.get(n_chip - 2, []) + [(0, 1, 1), (1, 1, 1)]
    for r in range(n_chip):
        line_step(place_of(n_chip - 1 - r))
        for far, i, a in early.get(r, []):
            service(far, i, a)
        if r < n_chip - 1:
            line_rows(r)

    def other_row(j, carry):
        grad_row(0, left_x[j], lambda col: oth_x[col], j, True)
        return carry

    for a in range(2):
        if a == 1:
            for far, i in far_near:
                service(far, i, a)
        for far in range(2):
            for i in range(n_chip):
                o_copy(a, SIDE, shard_of(far, i, 1 - c), far * n_chip + i).wait_recv()
        l_copy(a).wait_recv()
        if a == 0:
            lax.fori_loop(0, rows, other_row, 0)

    def settle(n, carry):
        far, i, a = unit_of(n)
        own_ways(far, i, a, lambda d: d.wait_send())
        return carry

    lax.fori_loop(0, units, settle, 0)
    if n_chip > 2:
        cross_over().wait_send()
    late_ways(lambda d: d.wait_send())
    for a in range(2):
        for far in range(2):
            for i in range(n_chip):
                o_copy(a, SIDE, shard_of(far, i, c), far * n_chip + i).wait_send()
            o_copy(a, MATE, shard_of(far, 0, c), far * n_chip).wait_send()
        l_copy(a).wait_send()

    def settle_sum(place, carry):
        side_copy(1 - y, place).wait_send()
        side_copy(y, place).wait_send()
        cross_copy(place).wait_send()
        pl.when(place > z)(lambda: up_copy(place).wait_send())
        pl.when(place < z)(lambda: down_copy(place).wait_send())
        return carry

    lax.fori_loop(0, n_chip, settle_sum, 0)


def finish_kernel(
    cols, in_held, up_held, down_held, other, left, in_out, up_out, down_out, sums, sems
):
    rows, count, _, width = sums.shape
    step = 4 if count % 4 == 0 else 1
    through = [
        pltpu.make_async_copy(in_held, in_out, sems.at[rows]),
        pltpu.make_async_copy(up_held, up_out, sems.at[rows + 1]),
    ]
    for m in through:
        m.start()

    def out_copy(j):
        return pltpu.make_async_copy(sums.at[j], down_out.at[j], sems.at[j])

    def row(j, carry):
        for first in range(0, count, step):
            picked = [other[cols[j, k]] for k in range(first, first + step)]
            value = jnp.dot(
                left[j], jnp.concatenate(picked, axis=1), preferred_element_type=jnp.float32
            )
            for i in range(step):
                block = value[:, i * width : (i + 1) * width]
                sums[j, first + i] = down_held[j, first + i] + block
        out_copy(j).start()
        return carry

    lax.fori_loop(0, rows, row, 0)
    for j in range(rows):
        out_copy(j).wait()
    for m in through:
        m.wait()


def fused_call(n_hst, n_chip, tokens, out_grad, up_blocks, up_cols, down_blocks, down_cols):
    rows, count, width, _ = up_blocks.shape
    tok, part = tokens.shape
    shards = n_hst * n_chip
    blocks = shards * part // width
    names = jnp.arange(blocks, dtype=jnp.int32)
    ranks = jnp.arange(count, dtype=jnp.int32)[None, None, :, None] - count
    cols = jnp.stack([up_cols, down_cols])
    hits = cols[:, :, :, None] == names
    inv = jnp.sum(jnp.where(hits, ranks, 0), axis=2, dtype=jnp.int32) + count
    hidden = rows * width
    bf, f32 = jnp.bfloat16, jnp.float32
    dma = pltpu.SemaphoreType.DMA
    whole = pl.BlockSpec(memory_space=pltpu.VMEM)
    smem = pl.BlockSpec(memory_space=pltpu.SMEM)
    anywhere = pl.BlockSpec(memory_space=pl.ANY)
    grads = jax.ShapeDtypeStruct((rows, count, width // 2, width), f32)

    def slots(amount):
        return pltpu.VMEM((amount, tok, part), bf)

    held = pl.pallas_call(
        functools.partial(fused_kernel, n_chip),
        in_specs=[smem] * 3 + [anywhere] * 4,
        out_specs=[whole] * 3 + [anywhere] * 2,
        out_shape=[
            pltpu.VMEM((tok, part), bf),
            pltpu.VMEM(grads.shape, f32),
            pltpu.VMEM(grads.shape, f32),
            pltpu.VMEM((blocks, tok, width), bf),
            pltpu.VMEM((rows, width // 2, tok), bf),
        ],
        scratch_shapes=[
            pltpu.VMEM((2, blocks, tok, width), bf),
            pltpu.VMEM((blocks, tok, width), bf),
            pltpu.VMEM((2, rows, count + 1, width, width), bf),
            pltpu.VMEM((hidden, part), bf),
            pltpu.VMEM((2, hidden, tok), f32),
            pltpu.VMEM((2, 2, rows, width // 2, tok), bf),
            pltpu.VMEM((rows, width // 2, tok), bf),
            pltpu.VMEM((tok, hidden), bf),
            slots(shards),
            slots(2 * n_chip),
        ]
        + [slots(n_chip)] * 5
        + [
            dma((2, 6, 2 * n_chip)),
            dma((2, shards)),
            dma((2, 3, 2 * n_chip)),
            dma((2, shards)),
            dma((2,)),
            dma((2,)),
            dma((4, 2 * n_chip)),
            dma((4, 2 * n_chip)),
            dma((2, part // width)),
            dma((2,)),
        ],
        compiler_params=pltpu.CompilerParams(
            collective_id=2, has_side_effects=True, vmem_limit_bytes=46 * 2**20
        ),
        cost_estimate=pl.CostEstimate(
            flops=22 * tok * hidden * shards * part // 4,
            bytes_accessed=20 * 2**20,
            transcendentals=hidden * tok,
        ),
    )(inv, up_cols, down_cols, tokens, out_grad, up_blocks, down_blocks)
    return pl.pallas_call(
        finish_kernel,
        in_specs=[smem] + [whole] * 5,
        out_specs=[anywhere] * 3,
        out_shape=[jax.ShapeDtypeStruct((tok, part), bf), grads, grads],
        scratch_shapes=[pltpu.VMEM(grads.shape, f32), dma((rows + 2,))],
        compiler_params=pltpu.CompilerParams(vmem_limit_bytes=24 * 2**20),
        cost_estimate=pl.CostEstimate(
            flops=2 * tok * hidden * count * width // 2,
            bytes_accessed=8 * 2**20,
            transcendentals=0,
        ),
    )(down_cols, *held)


def local(n_dp, n_hst, n_chip, tokens, out_grad, up_blocks, up_cols, down_blocks, down_cols):
    if n_dp == 2 and n_hst == 4 and n_chip >= 2 and n_chip % 2 == 0:
        return tuple(
            fused_call(
                n_hst, n_chip, tokens, out_grad, up_blocks, up_cols, down_blocks, down_cols
            )
        )
    whole_x, whole_dy = gather_call(n_hst, n_chip, tokens, out_grad)
    split = n_dp == 2
    partial_value, *grads = rows_call(
        split, whole_x, whole_dy, up_blocks, up_cols, down_blocks, down_cols
    )
    if split:
        swap = [(0, 1), (1, 0)]
        sums = [
            grads[i].astype(jnp.float32)
            + lax.ppermute(grads[i + 1], "dp", swap).astype(jnp.float32)
            for i in (0, 2)
        ]
    else:
        sums = [
            lax.psum_scatter(g, "dp", scatter_dimension=2, tiled=True).astype(jnp.float32)
            for g in grads
        ]
    summed = scatter_call(n_hst, n_chip, partial_value)
    return (summed, *sums)


def solution(mesh):
    placed = (
        P("dp", ("hst", "chip")),
        P("dp", ("hst", "chip")),
        P(("hst", "chip"), None, None, None),
        P(("hst", "chip"), None),
        P(("hst", "chip"), None, None, None),
        P(("hst", "chip"), None),
    )
    return jax.shard_map(
        functools.partial(local, mesh.shape["dp"], mesh.shape["hst"], mesh.shape["chip"]),
        mesh=mesh,
        in_specs=placed,
        out_specs=(
            P("dp", ("hst", "chip")),
            P(("hst", "chip"), None, "dp", None),
            P(("hst", "chip"), None, "dp", None),
        ),
        check_vma=False,
    )
```

```python
import functools

import jax
import jax.numpy as jnp
from jax import lax
from jax.experimental import pallas as pl
from jax.experimental.pallas import tpu as pltpu
from jax.sharding import PartitionSpec as P

NT = (((1,), (1,)), ((), ()))


def rows_kernel(
    split,
    up_cols,
    down_cols,
    me,
    x_ref,
    dy_ref,
    up_ref,
    down_ref,
    in_ref,
    *rest,
):
    outs, (acc, xs, dys, us, ds) = rest[:-5], rest[-5:]
    row = pl.program_id(0)
    width = up_ref.shape[-1]
    per_shard = x_ref.shape[2] // width
    count = up_ref.shape[1]

    @pl.when(row == 0)
    def _():
        acc[...] = jnp.zeros_like(acc)

    def place(col):
        return col // per_shard, pl.ds(pl.multiple_of((col % per_shard) * width, width), width)

    for k in range(count):
        lanes = pl.ds(k * width, width)
        shard, at = place(up_cols[row, k])
        xs[:, lanes] = x_ref[shard, :, at]
        shard, at = place(down_cols[row, k])
        dys[:, lanes] = dy_ref[shard, :, at]
        us[:, lanes] = up_ref[0, k]
        ds[:, lanes] = down_ref[0, k]
    pre = lax.dot_general(us[...], xs[...], NT, preferred_element_type=jnp.float32)
    hid = lax.dot_general(ds[...], dys[...], NT, preferred_element_type=jnp.float32)
    sig = 1.0 / (1.0 + jnp.exp(-pre))
    act = (pre * sig).astype(jnp.bfloat16)
    pre_grad_f = hid * sig * (1.0 + pre * (1.0 - sig))
    pre_grad = pre_grad_f.astype(jnp.bfloat16)
    pre_grad_t = pre_grad_f.T.astype(jnp.bfloat16)

    step = 4
    for base in range(0, count, step):
        lanes = pl.ds(base * width, step * width)
        up_part = jnp.dot(pre_grad, xs[:, lanes], preferred_element_type=jnp.float32)
        down_part = jnp.dot(act, dys[:, lanes], preferred_element_type=jnp.float32)
        back = jnp.dot(pre_grad_t, us[:, lanes], preferred_element_type=jnp.float32)
        for i in range(step):
            k = base + i
            cut = slice(i * width, (i + 1) * width)
            for part, out in ((up_part, outs[: len(outs) // 2]), (down_part, outs[len(outs) // 2 :])):
                block = part[:, cut].astype(jnp.bfloat16)
                if split:
                    half = width // 2
                    first = me[0] == 0
                    out[0][0, k] = jnp.where(first, block[:half], block[half:])
                    out[1][0, k] = jnp.where(first, block[half:], block[:half])
                else:
                    out[0][0, k] = block
            shard, at = place(up_cols[row, k])
            acc[shard, :, at] += back[:, cut]

    @pl.when(row == pl.num_programs(0) - 1)
    def _():
        for s in range(acc.shape[0]):
            in_ref[s] = acc[s].astype(jnp.bfloat16)


def rows_call(split, whole_x, whole_dy, up_blocks, up_cols, down_blocks, down_cols):
    rows, count, width, _ = up_blocks.shape
    shards, tok, part = whole_x.shape
    out_h = width // 2 if split else width
    n_out = 4 if split else 2
    whole = pl.BlockSpec(memory_space=pltpu.VMEM)
    smem = pl.BlockSpec(memory_space=pltpu.SMEM)

    def block(h):
        return pl.BlockSpec((1, count, h, width), lambda r: (r, 0, 0, 0))

    me = lax.axis_index("dp").astype(jnp.int32).reshape(1)
    flops = 10 * tok * rows * count * width * width
    return pl.pallas_call(
        functools.partial(rows_kernel, split),
        grid=(rows,),
        in_specs=[smem, smem, smem, whole, whole, block(width), block(width)],
        out_specs=[whole] + [block(out_h)] * n_out,
        out_shape=[jax.ShapeDtypeStruct(whole_x.shape, jnp.bfloat16)]
        + [jax.ShapeDtypeStruct((rows, count, out_h, width), jnp.bfloat16)] * n_out,
        scratch_shapes=[
            pltpu.VMEM(whole_x.shape, jnp.float32),
            pltpu.VMEM((tok, count * width), jnp.bfloat16),
            pltpu.VMEM((tok, count * width), jnp.bfloat16),
            pltpu.VMEM((width, count * width), jnp.bfloat16),
            pltpu.VMEM((width, count * width), jnp.bfloat16),
        ],
        compiler_params=pltpu.CompilerParams(
            dimension_semantics=("arbitrary",), vmem_limit_bytes=56 * 2**20
        ),
        cost_estimate=pl.CostEstimate(
            flops=flops, bytes_accessed=30 * 2**20, transcendentals=rows * width * tok
        ),
    )(up_cols, down_cols, me, whole_x, whole_dy, up_blocks, down_blocks)


MESH = pl.DeviceIdType.MESH
ALONG_UP, ALONG_DOWN, ACROSS, SIDE = range(4)


def gather_kernel(n_chip, x_ref, dy_ref, x_out, dy_out, send_sem, recv_sem, own_sem):
    hst, z = lax.axis_index("hst"), lax.axis_index("chip")
    far, c = hst // 2, hst % 2
    own = hst * n_chip + z
    ins, outs = (x_ref, dy_ref), (x_out, dy_out)
    not_last, not_first = z < n_chip - 1, z > 0
    peers = {
        ALONG_UP: {"hst": hst, "chip": (z + 1) % n_chip},
        ALONG_DOWN: {"hst": hst, "chip": (z + n_chip - 1) % n_chip},
        ACROSS: {"hst": (1 - far) * 2 + c, "chip": z},
        SIDE: {"hst": far * 2 + 1 - c, "chip": z},
    }

    barrier = pltpu.get_barrier_semaphore()

    def greet(way):
        pl.semaphore_signal(barrier, inc=1, device_id=peers[way], device_id_type=MESH)

    greet(ACROSS)
    greet(SIDE)
    pl.when(not_last)(lambda: greet(ALONG_UP))
    pl.when(not_first)(lambda: greet(ALONG_DOWN))
    inner = jnp.logical_and(not_last, not_first)
    pl.when(inner)(lambda: pl.semaphore_wait(barrier, 4))
    pl.when(jnp.logical_not(inner))(lambda: pl.semaphore_wait(barrier, 3))

    def copy(a, way, shard, source=None):
        return pltpu.make_async_remote_copy(
            src_ref=outs[a].at[shard] if source is None else source,
            dst_ref=outs[a].at[shard],
            send_sem=send_sem.at[a, way, shard],
            recv_sem=recv_sem.at[a, shard],
            device_id=peers[way],
            device_id_type=MESH,
        )

    def each(act):
        for t in range(n_chip + 1):
            for a in range(2):
                if t == 0:
                    act(a, (), own, None, True)
                elif t < n_chip:
                    below = z - t
                    act(a, (ALONG_UP,), hst * n_chip + below, below >= 0, False)
                    above = z + t
                    act(a, (ALONG_DOWN,), hst * n_chip + above, above < n_chip, False)
            for a in range(2):
                if t >= 1:
                    base = ((1 - far) * 2 + c) * n_chip
                    if t == 1:
                        act(a, None, base + z, None, False)
                    else:
                        act(a, None, base + z - (t - 1), z - (t - 1) >= 0, False)
                        act(a, None, base + z + (t - 1), z + (t - 1) < n_chip, False)

    def guarded(condition, run):
        if condition is None:
            run()
        else:
            pl.when(condition)(run)

    def forward(a, ways, shard, condition, is_own):
        def run():
            if not is_own:
                copy(a, SIDE, shard).wait_recv()
            source = ins[a] if is_own else None
            if ways is not None:
                if is_own or ALONG_UP in ways:
                    pl.when(not_last)(lambda: copy(a, ALONG_UP, shard, source).start())
                if is_own or ALONG_DOWN in ways:
                    pl.when(not_first)(lambda: copy(a, ALONG_DOWN, shard, source).start())
                copy(a, ACROSS, shard, source).start()
            copy(a, SIDE, shard, source).start()

        guarded(condition, run)

    def finish(a, ways, shard, condition, is_own):
        def run():
            source = ins[a] if is_own else None
            if ways is not None:
                if is_own or ALONG_UP in ways:
                    pl.when(not_last)(lambda: copy(a, ALONG_UP, shard, source).wait_send())
                if is_own or ALONG_DOWN in ways:
                    pl.when(not_first)(lambda: copy(a, ALONG_DOWN, shard, source).wait_send())
                copy(a, ACROSS, shard, source).wait_send()
            copy(a, SIDE, shard, source).wait_send()

        guarded(condition, run)

    each(forward)
    mine = [pltpu.make_async_copy(ins[a], outs[a].at[own], own_sem.at[a]) for a in range(2)]
    for m in mine:
        m.start()
    for half in range(2):
        for place in range(n_chip):
            for a in range(2):
                copy(a, SIDE, (half * 2 + 1 - c) * n_chip + place).wait_recv()
    each(finish)
    for m in mine:
        m.wait()


def gather_call(n_hst, n_chip, tokens, out_grad):
    if n_hst != 4:
        return [
            lax.all_gather(v, ("hst", "chip"), axis=0, tiled=False) for v in (tokens, out_grad)
        ]
    shards = n_hst * n_chip
    return pl.pallas_call(
        functools.partial(gather_kernel, n_chip),
        in_specs=[pl.BlockSpec(memory_space=pltpu.VMEM)] * 2,
        out_specs=[pl.BlockSpec(memory_space=pl.ANY)] * 2,
        out_shape=[jax.ShapeDtypeStruct((shards, *v.shape), v.dtype) for v in (tokens, out_grad)],
        scratch_shapes=[
            pltpu.SemaphoreType.DMA((2, 4, shards)),
            pltpu.SemaphoreType.DMA((2, shards)),
            pltpu.SemaphoreType.DMA((2,)),
        ],
        compiler_params=pltpu.CompilerParams(collective_id=0, has_side_effects=True),
    )(tokens, out_grad)


def scatter_kernel(n_chip, part, out, side, cross, up, down, cross_out, line_out, send_sem, recv_sem):
    hst, z = lax.axis_index("hst"), lax.axis_index("chip")
    far, c = hst // 2, hst % 2
    not_last, not_first = z < n_chip - 1, z > 0
    peers = {
        ALONG_UP: {"hst": hst, "chip": (z + 1) % n_chip},
        ALONG_DOWN: {"hst": hst, "chip": (z + n_chip - 1) % n_chip},
        ACROSS: {"hst": (1 - far) * 2 + c, "chip": z},
        SIDE: {"hst": far * 2 + 1 - c, "chip": z},
    }
    barrier = pltpu.get_barrier_semaphore()

    def greet(way):
        pl.semaphore_signal(barrier, inc=1, device_id=peers[way], device_id_type=MESH)

    greet(ACROSS)
    greet(SIDE)
    pl.when(not_last)(lambda: greet(ALONG_UP))
    pl.when(not_first)(lambda: greet(ALONG_DOWN))
    inner = jnp.logical_and(not_last, not_first)
    pl.when(inner)(lambda: pl.semaphore_wait(barrier, 4))
    pl.when(jnp.logical_not(inner))(lambda: pl.semaphore_wait(barrier, 3))

    def copy(way, source, target, slot):
        return pltpu.make_async_remote_copy(
            src_ref=source,
            dst_ref=target,
            send_sem=send_sem.at[way, slot],
            recv_sem=recv_sem.at[way, slot],
            device_id=peers[way],
            device_id_type=MESH,
        )

    def side_copy(half, place):
        slot = half * n_chip + place
        return copy(SIDE, part.at[(half * 2 + 1 - c) * n_chip + place], side.at[slot], slot)

    def cross_copy(place):
        return copy(ACROSS, cross_out.at[place], cross.at[place], place)

    def up_copy(place):
        return copy(ALONG_UP, line_out.at[place], up.at[place], place)

    def down_copy(place):
        return copy(ALONG_DOWN, line_out.at[place], down.at[place], place)

    def each(act):
        for t in range(n_chip - 1, 0, -1):
            pl.when(z + t < n_chip)(lambda t=t: act(z + t, 1))
            pl.when(z - t >= 0)(lambda t=t: act(z - t, -1))
        act(z, 0)

    rows = part.shape[1]
    chunk = 32 if rows % 32 == 0 else rows

    def total(store, terms):
        def body(i, carry):
            at = pl.ds(pl.multiple_of(i * chunk, chunk), chunk)
            value = None
            for ref, slot in terms:
                term = ref[slot, at, :].astype(jnp.float32)
                value = term if value is None else value + term
            store(at, value.astype(jnp.bfloat16))
            return carry

        lax.fori_loop(0, rows // chunk, body, 0)

    def to(ref, slot):
        def store(at, value):
            ref[slot, at, :] = value

        return store

    def to_out(at, value):
        out[at, :] = value

    each(lambda place, _: side_copy(1 - far, place).start())
    each(lambda place, _: side_copy(far, place).start())

    def cross_step(place, _):
        slot = (1 - far) * n_chip + place
        side_copy(1 - far, place).wait_recv()
        total(to(cross_out, place), [(part, ((1 - far) * 2 + c) * n_chip + place), (side, slot)])
        cross_copy(place).start()

    each(cross_step)

    def line_step(place, sign):
        slot = far * n_chip + place
        side_copy(far, place).wait_recv()
        cross_copy(place).wait_recv()
        base = [(part, (far * 2 + c) * n_chip + place), (side, slot), (cross, place)]
        if sign > 0:

            @pl.when(not_first)
            def _():
                up_copy(place).wait_recv()
                total(to(line_out, place), base + [(up, place)])

            @pl.when(jnp.logical_not(not_first))
            def _():
                total(to(line_out, place), base)

            up_copy(place).start()
        elif sign < 0:

            @pl.when(not_last)
            def _():
                down_copy(place).wait_recv()
                total(to(line_out, place), base + [(down, place)])

            @pl.when(jnp.logical_not(not_last))
            def _():
                total(to(line_out, place), base)

            down_copy(place).start()
        else:

            @pl.when(inner)
            def _():
                up_copy(place).wait_recv()
                down_copy(place).wait_recv()
                total(to_out, base + [(up, place), (down, place)])

            @pl.when(jnp.logical_not(not_first))
            def _():
                down_copy(place).wait_recv()
                total(to_out, base + [(down, place)])

            @pl.when(jnp.logical_not(not_last))
            def _():
                up_copy(place).wait_recv()
                total(to_out, base + [(up, place)])

    each(line_step)

    def finish(place, sign):
        side_copy(1 - far, place).wait_send()
        side_copy(far, place).wait_send()
        cross_copy(place).wait_send()
        if sign > 0:
            up_copy(place).wait_send()
        elif sign < 0:
            down_copy(place).wait_send()

    each(finish)


def scatter_call(n_hst, n_chip, part):
    if n_hst != 4 or n_chip < 2:
        return lax.psum_scatter(part, ("hst", "chip"), scatter_dimension=0, tiled=False)
    shards, rows, width = part.shape
    whole = pl.BlockSpec(memory_space=pltpu.VMEM)

    def slots(count):
        return pltpu.VMEM((count, rows, width), jnp.bfloat16)

    return pl.pallas_call(
        functools.partial(scatter_kernel, n_chip),
        in_specs=[whole],
        out_specs=whole,
        out_shape=jax.ShapeDtypeStruct((rows, width), jnp.bfloat16),
        scratch_shapes=[slots(2 * n_chip)]
        + [slots(n_chip)] * 5
        + [pltpu.SemaphoreType.DMA((4, 2 * n_chip))] * 2,
        compiler_params=pltpu.CompilerParams(
            collective_id=1, has_side_effects=True, vmem_limit_bytes=24 * 2**20
        ),
        cost_estimate=pl.CostEstimate(
            flops=shards * rows * width, bytes_accessed=120 * 2**20, transcendentals=0
        ),
    )(part)

PAIR, MATE = 4, 5


def fused_kernel(
    n_chip,
    inv,
    up_cols,
    down_cols,
    tokens,
    out_grad,
    up_hbm,
    down_hbm,
    in_ref,
    up_ref,
    down_ref,
    oth_dy,
    left_dy,
    own,
    oth_x,
    wts,
    dense,
    pre,
    lhs,
    left_x,
    back,
    part,
    side,
    cross,
    cross_out,
    up_in,
    down_in,
    line_out,
    far_up,
    far_down,
    g_send,
    g_recv,
    o_send,
    o_recv,
    l_send,
    l_recv,
    s_send,
    s_recv,
    own_sem,
    w_sem,
):
    dp, hst, z = lax.axis_index("dp"), lax.axis_index("hst"), lax.axis_index("chip")
    y, c = hst // 2, hst % 2
    _, rows, count_1, width, _ = wts.shape
    count = count_1 - 1
    tok = back.shape[0]
    per = dense.shape[1] // width
    half = width // 2
    events = 2 * n_chip
    not_last, not_first = z < n_chip - 1, z > 0
    inner = jnp.logical_and(not_last, not_first)
    toward = 1 - 2 * (z % 2)
    peers = {
        ALONG_UP: {"dp": dp, "hst": hst, "chip": (z + 1) % n_chip},
        ALONG_DOWN: {"dp": dp, "hst": hst, "chip": (z + n_chip - 1) % n_chip},
        ACROSS: {"dp": dp, "hst": (1 - y) * 2 + c, "chip": z},
        SIDE: {"dp": dp, "hst": y * 2 + 1 - c, "chip": z},
        PAIR: {"dp": 1 - dp, "hst": hst, "chip": z},
        MATE: {"dp": dp, "hst": hst, "chip": z + toward},
    }
    ins, oth = (tokens, out_grad), (oth_x, oth_dy)
    mine = hst * n_chip + z

    def blocks_of(shard):
        return pl.ds(shard * per, per)

    locals_ = [
        pltpu.make_async_copy(
            ins[a].at[:, pl.ds(b * width, width)], own.at[a, mine * per + b], own_sem.at[a, b]
        )
        for a in range(2)
        for b in range(per)
    ]
    weights = [
        pltpu.make_async_copy(w, wts.at[a, :, pl.ds(0, count)], w_sem.at[a])
        for a, w in enumerate((up_hbm, down_hbm))
    ]
    for m in locals_ + weights:
        m.start()

    barrier = pltpu.get_barrier_semaphore()

    def greet(way):
        pl.semaphore_signal(barrier, inc=1, device_id=peers[way], device_id_type=MESH)

    for way in (ACROSS, SIDE, PAIR):
        greet(way)
    pl.when(not_last)(lambda: greet(ALONG_UP))
    pl.when(not_first)(lambda: greet(ALONG_DOWN))
    pl.when(inner)(lambda: pl.semaphore_wait(barrier, 5))
    pl.when(jnp.logical_not(inner))(lambda: pl.semaphore_wait(barrier, 4))

    for m in locals_:
        m.wait()

    short = jnp.minimum(z, n_chip - 1 - z)

    def place_of(i):
        both = z + toward * (2 * (i % 2) - 1) * ((i + 1) // 2)
        return jnp.where(i <= 2 * short, both, jnp.where(2 * z < n_chip - 1, i, n_chip - 1 - i))

    last = n_chip - 1
    order = [(0, 0, 0), (0, 0, 1)]
    for i in range(1, n_chip):
        order += [(0, i, 0), (1, i - 1, 0), (0, i, 1), (1, i - 1, 1)]
    order += [(1, last, 1), (1, last, 0)]
    units = len(order)

    def pick(n, values):
        found = values[0]
        for m in range(1, len(values)):
            found = jnp.where(n == m, values[m], found)
        return found

    def unit_of(n):
        return tuple(pick(n, [u[m] for u in order]) for m in range(3))

    def shard_of(far, i, core):
        column = far * (1 - y) + (1 - far) * y
        return (column * 2 + core) * n_chip + place_of(i)

    def g_copy(a, way, shard, slot):
        return pltpu.make_async_remote_copy(
            src_ref=own.at[a, blocks_of(shard)],
            dst_ref=own.at[a, blocks_of(shard)],
            send_sem=g_send.at[a, way, slot],
            recv_sem=g_recv.at[a, shard],
            device_id=peers[way],
            device_id_type=MESH,
        )

    def x_copy(a, shard, slot):
        return pltpu.make_async_remote_copy(
            src_ref=own.at[a, blocks_of(shard)],
            dst_ref=oth[a].at[blocks_of(shard)],
            send_sem=g_send.at[a, PAIR, slot],
            recv_sem=o_recv.at[a, shard],
            device_id=peers[PAIR],
            device_id_type=MESH,
        )

    def o_copy(a, way, shard, slot):
        return pltpu.make_async_remote_copy(
            src_ref=oth[a].at[blocks_of(shard)],
            dst_ref=oth[a].at[blocks_of(shard)],
            send_sem=o_send.at[a, (SIDE, MATE, ACROSS).index(way), slot],
            recv_sem=o_recv.at[a, shard],
            device_id=peers[way],
            device_id_type=MESH,
        )

    def own_ways(far, i, a, act):
        place, shard, slot = place_of(i), shard_of(far, i, c), far * n_chip + i
        near = far == 0
        lined = (a == 1) & ((place == 0) | (place == last))
        along = near | lined
        act(g_copy(a, SIDE, shard, slot))
        pl.when(along & (place <= z) & not_last)(lambda: act(g_copy(a, ALONG_UP, shard, slot)))
        pl.when(along & (place >= z) & not_first)(lambda: act(g_copy(a, ALONG_DOWN, shard, slot)))
        across = near & (jnp.logical_not(lined) | (place == z))
        pl.when(across)(lambda: act(g_copy(a, ACROSS, shard, slot)))
        crossed = (far == 1) & (i == 2)
        pl.when((a == 0) & (i != 1) & jnp.logical_not(crossed))(lambda: act(x_copy(0, shard, slot)))
        pl.when((a == 1) & ((i == 0) | (i == 2)))(lambda: act(x_copy(1, shard, slot)))

    def assemble(a, shard):
        for j in range(rows):
            for b in range(per):
                dense[j * width : (j + 1) * width, b * width : (b + 1) * width] = wts[
                    a, j, inv[a, j, shard * per + b]
                ]

    def service(far, i, a):
        shard, slot = shard_of(far, i, c), far * n_chip + i
        o_copy(a, SIDE, shard, slot).wait_recv()
        o_copy(a, SIDE, shard, slot).start()

    def mate_service(far, a):
        o_copy(a, MATE, shard_of(far, 0, c), far * n_chip).start()

    def cross_over():
        return o_copy(0, ACROSS, shard_of(0, 2, c), 2)

    def gather_step(n, carry):
        @pl.when(n < units)
        def _():
            far, i, a = unit_of(n)
            pl.when(n > 1)(lambda: g_copy(a, SIDE, shard_of(far, i, c), 0).wait_recv())
            own_ways(far, i, a, lambda d: d.start())

        for far, at in ((0, units // 2 - 1), (1, units - 5)):

            @pl.when(n == at)
            def _():
                for a in range(2):
                    service(far, 0, a)
                    pl.when(jnp.logical_not(inner))(lambda: mate_service(far, a))

        if n_chip > 2:

            @pl.when(n == units - 3)
            def _():
                service(0, 2, 0)
                cross_over().start()

        @pl.when(n == 0)
        def _():
            for m in weights:
                m.wait()
            for a in range(2):
                wts[a, :, count] = jnp.zeros((rows, width, width), wts.dtype)
            pre[...] = jnp.zeros_like(pre)

        def unit(sib, carry):
            now = n - sib

            @pl.when((now >= 0) & (now < units))
            def _():
                far, i, a = unit_of(now)
                shard = shard_of(far, i, jnp.where(sib == 1, 1 - c, c))
                pl.when(sib == 1)(lambda: g_copy(a, SIDE, shard, 0).wait_recv())
                assemble(a, shard)
                taken = [own[a, shard * per + b] for b in range(per)]
                pre[a] += lax.dot_general(
                    dense[...],
                    jnp.concatenate(taken, axis=1),
                    NT,
                    preferred_element_type=jnp.float32,
                )

            return carry

        lax.fori_loop(0, 2, unit, 0)
        return carry

    lax.fori_loop(0, units + 1, gather_step, 0)

    def gates(j, carry):
        at = pl.ds(pl.multiple_of(j * width, width), width)
        p, h = pre[0, at, :], pre[1, at, :]
        sig = 1.0 / (1.0 + jnp.exp(-p))
        act = (p * sig).astype(jnp.bfloat16)
        grad_f = h * sig * (1.0 + p * (1.0 - sig))
        grad = grad_f.astype(jnp.bfloat16)
        for f in range(2):
            lhs[0, f, j] = grad[f * half : (f + 1) * half]
            lhs[1, f, j] = act[f * half : (f + 1) * half]
        back[:, at] = grad_f.T.astype(jnp.bfloat16)
        return carry

    lax.fori_loop(0, rows, gates, 0)

    def l_copy(a):
        return pltpu.make_async_remote_copy(
            src_ref=lhs.at[a, 1 - dp],
            dst_ref=(left_x, left_dy)[a],
            send_sem=l_send.at[a],
            recv_sem=l_recv.at[a],
            device_id=peers[PAIR],
            device_id_type=MESH,
        )

    def late_ways(act):
        for i in range(3, n_chip):
            for far in range(2):
                act(x_copy(1, shard_of(far, i, c), far * n_chip + i))

    l_copy(0).start()
    l_copy(1).start()
    late_ways(lambda d: d.start())

    @pl.when(inner)
    def _():
        for a in range(2):
            for far in range(2):
                mate_service(far, a)

    def copy(way, source, target, slot):
        return pltpu.make_async_remote_copy(
            src_ref=source,
            dst_ref=target,
            send_sem=s_send.at[way, slot],
            recv_sem=s_recv.at[way, slot],
            device_id=peers[way],
            device_id_type=MESH,
        )

    def side_copy(column, place):
        slot = column * n_chip + place
        return copy(SIDE, part.at[(column * 2 + 1 - c) * n_chip + place], side.at[slot], slot)

    def between(place):
        return (place > 0) & (place < last)

    low, high = pl.ds(0, tok // 2), pl.ds(tok // 2, tok // 2)

    def cross_act(place, act):
        def send(at, slot):
            return copy(ACROSS, cross_out.at[place, at], cross.at[place, at], slot)

        pl.when(between(place))(lambda: act(send(low, place)))
        pl.when(jnp.logical_not(between(place)))(lambda: act(send(pl.ds(0, tok), place)))

    def late_cross(place):
        return copy(
            ACROSS, cross_out.at[place, high], cross.at[place, high], n_chip + place
        )

    def far_copy(way, place):
        target = far_up if way == ALONG_UP else far_down
        return copy(way, cross_out.at[place, high], target.at[place], n_chip + place)

    def up_copy(place):
        return copy(ALONG_UP, line_out.at[place], up_in.at[place], place)

    def down_copy(place):
        return copy(ALONG_DOWN, line_out.at[place], down_in.at[place], place)

    chunk = 32 if tok % 32 == 0 else tok

    def total(store, terms, start=0, stop=tok // chunk):
        def body(i, carry):
            at = pl.ds(pl.multiple_of(i * chunk, chunk), chunk)
            value = None
            for ref, slot, above in terms:
                rows_at = pl.ds(pl.multiple_of(i * chunk - above, chunk), chunk)
                term = ref[slot, rows_at, :].astype(jnp.float32)
                value = term if value is None else value + term
            store(at, value.astype(jnp.bfloat16))
            return carry

        lax.fori_loop(start, stop, body, 0)

    def to(ref, slot):
        def store(at, value):
            ref[slot, at, :] = value

        return store

    def to_out(at, value):
        in_ref[at, :] = value

    def pieces(column, place):
        def body(q, carry):
            core = jnp.where(q == 0, 1 - c, c)
            shard = (column * 2 + core) * n_chip + place
            assemble(0, shard)
            part[shard] = jnp.dot(
                back[...], dense[...], preferred_element_type=jnp.float32
            ).astype(jnp.bfloat16)
            pl.when(q == 0)(lambda: side_copy(column, place).start())
            return carry

        lax.fori_loop(0, 2, body, 0)

    def far_send(place):
        pl.when(z < place)(lambda: far_copy(ALONG_UP, place).start())
        pl.when(z > place)(lambda: far_copy(ALONG_DOWN, place).start())

    half_chunks = tok // 2 // chunk

    def far_step(place):
        terms = [(cross_out, place, 0)]
        upper, middle = (far_up, place, tok // 2), (far_down, place, tok // 2)

        @pl.when((z < place) & not_first)
        def _():
            far_copy(ALONG_UP, place).wait_recv()
            total(to(cross_out, place), terms + [upper], half_chunks, 2 * half_chunks)
            far_send(place)

        @pl.when((z > place) & not_last)
        def _():
            far_copy(ALONG_DOWN, place).wait_recv()
            total(to(cross_out, place), terms + [middle], half_chunks, 2 * half_chunks)
            far_send(place)

    def far_end():
        @pl.when(between(z))
        def _():
            far_copy(ALONG_UP, z).wait_recv()
            far_copy(ALONG_DOWN, z).wait_recv()
            terms = [(cross_out, z, 0), (far_up, z, tok // 2), (far_down, z, tok // 2)]
            total(to(cross_out, z), terms, half_chunks, 2 * half_chunks)
            late_cross(z).start()

    def piece_step(r, carry):
        @pl.when((r > 0) & (r <= n_chip))
        def _():
            place = place_of(n_chip - r)
            slot = (1 - y) * n_chip + place
            side_copy(1 - y, place).wait_recv()
            total(
                to(cross_out, place),
                [(part, ((1 - y) * 2 + c) * n_chip + place, 0), (side, slot, 0)],
            )
            cross_act(place, lambda d: d.start())
            ends = jnp.logical_or(
                (z < place) & jnp.logical_not(not_first), (z > place) & jnp.logical_not(not_last)
            )
            pl.when(between(place) & ends)(lambda: far_send(place))

        column = jnp.where(r < n_chip, 1 - y, y)
        pieces(column, place_of(n_chip - 1 - r % n_chip))
        return carry

    lax.fori_loop(0, n_chip + 2, piece_step, 0)

    for place in range(1, last):
        far_step(place)

    def line_step(place):
        slot = y * n_chip + place
        side_copy(y, place).wait_recv()
        cross_act(place, lambda d: d.wait_recv())
        pl.when((place == z) & between(place))(lambda: late_cross(place).wait_recv())
        full = jnp.where(between(place) & (place != z), half_chunks, tok // chunk)
        base = [(part, (y * 2 + c) * n_chip + place, 0), (side, slot, 0)]

        def sums(store, more):
            total(store, base + more + [(cross, place, 0)], 0, full)
            total(store, base + more, full, tok // chunk)

        @pl.when(place > z)
        def _():
            @pl.when(not_first)
            def _():
                up_copy(place).wait_recv()
                sums(to(line_out, place), [(up_in, place, 0)])

            @pl.when(jnp.logical_not(not_first))
            def _():
                sums(to(line_out, place), [])

            up_copy(place).start()

        @pl.when(place < z)
        def _():
            @pl.when(not_last)
            def _():
                down_copy(place).wait_recv()
                sums(to(line_out, place), [(down_in, place, 0)])

            @pl.when(jnp.logical_not(not_last))
            def _():
                sums(to(line_out, place), [])

            down_copy(place).start()

        @pl.when(place == z)
        def _():
            @pl.when(inner)
            def _():
                up_copy(place).wait_recv()
                down_copy(place).wait_recv()
                sums(to_out, [(up_in, place, 0), (down_in, place, 0)])

            @pl.when(jnp.logical_not(not_first))
            def _():
                down_copy(place).wait_recv()
                sums(to_out, [(down_in, place, 0)])

            @pl.when(jnp.logical_not(not_last))
            def _():
                up_copy(place).wait_recv()
                sums(to_out, [(up_in, place, 0)])

    cols, outs = (up_cols, down_cols), (up_ref, down_ref)
    step = 4 if count % 4 == 0 else 1

    def grad_row(a, left, source, j, add):
        for first in range(0, count, step):
            picked = [source(cols[a][j, k]) for k in range(first, first + step)]
            value = jnp.dot(
                left, jnp.concatenate(picked, axis=1), preferred_element_type=jnp.float32
            )
            for i in range(step):
                block = value[:, i * width : (i + 1) * width]
                if add:
                    outs[a][j, first + i] += block
                else:
                    outs[a][j, first + i] = block

    share = -(-rows // (n_chip - 1))

    def own_row(j, carry):
        for a in range(2):
            grad_row(a, lhs[a, dp, j], lambda col, a=a: own[a, col], j, False)
        return carry

    far_near = [(far, i) for i in range(3, n_chip) for far in range(2)]
    early = {0: [(far, i, 0) for far, i in far_near], 1: [(0, 1, 0), (1, 1, 0)]}
    if n_chip > 2:
        early[0] += [(1, 2, 0), (0, 2, 1), (1, 2, 1)]
    early[n_chip - 2] = early.get(n_chip - 2, []) + [(0, 1, 1), (1, 1, 1)]
    def line_loop(r, carry):
        line_step(place_of(n_chip - 1 - r))
        pl.when(r == 0)(far_end)
        pl.when(r + 2 < n_chip)(lambda: pieces(y, place_of(jnp.maximum(n_chip - 3 - r, 0))))
        for at, listed in early.items():

            @pl.when(r == at)
            def _():
                for far, i, a in listed:
                    service(far, i, a)

        lax.fori_loop(
            jnp.minimum(r * share, rows), jnp.minimum((r + 1) * share, rows), own_row, 0
        )
        return carry

    lax.fori_loop(0, n_chip, line_loop, 0)

    def other_row(j, carry):
        grad_row(0, left_x[j], lambda col: oth_x[col], j, True)
        return carry

    for a in range(2):
        if a == 1:
            for far, i in far_near:
                service(far, i, a)
        for far in range(2):
            for i in range(n_chip):
                o_copy(a, SIDE, shard_of(far, i, 1 - c), far * n_chip + i).wait_recv()
        l_copy(a).wait_recv()
        if a == 0:
            lax.fori_loop(0, rows, other_row, 0)

    def settle(n, carry):
        far, i, a = unit_of(n)
        own_ways(far, i, a, lambda d: d.wait_send())
        return carry

    lax.fori_loop(0, units, settle, 0)
    if n_chip > 2:
        cross_over().wait_send()
    late_ways(lambda d: d.wait_send())
    for a in range(2):
        for far in range(2):
            for i in range(n_chip):
                o_copy(a, SIDE, shard_of(far, i, c), far * n_chip + i).wait_send()
            o_copy(a, MATE, shard_of(far, 0, c), far * n_chip).wait_send()
        l_copy(a).wait_send()

    def settle_sum(place, carry):
        side_copy(1 - y, place).wait_send()
        side_copy(y, place).wait_send()
        cross_act(place, lambda d: d.wait_send())

        @pl.when(between(place))
        def _():
            pl.when(z < place)(lambda: far_copy(ALONG_UP, place).wait_send())
            pl.when(z > place)(lambda: far_copy(ALONG_DOWN, place).wait_send())
            pl.when(z == place)(lambda: late_cross(place).wait_send())

        pl.when(place > z)(lambda: up_copy(place).wait_send())
        pl.when(place < z)(lambda: down_copy(place).wait_send())
        return carry

    lax.fori_loop(0, n_chip, settle_sum, 0)


def finish_kernel(
    cols, in_held, up_held, down_held, other, left, in_out, up_out, down_out, sums, sems
):
    rows, count, _, width = sums.shape
    step = 4 if count % 4 == 0 else 1
    through = [
        pltpu.make_async_copy(in_held, in_out, sems.at[rows]),
        pltpu.make_async_copy(up_held, up_out, sems.at[rows + 1]),
    ]
    for m in through:
        m.start()

    def out_copy(j):
        return pltpu.make_async_copy(sums.at[j], down_out.at[j], sems.at[j])

    def row(j, carry):
        for first in range(0, count, step):
            picked = [other[cols[j, k]] for k in range(first, first + step)]
            value = jnp.dot(
                left[j], jnp.concatenate(picked, axis=1), preferred_element_type=jnp.float32
            )
            for i in range(step):
                block = value[:, i * width : (i + 1) * width]
                sums[j, first + i] = down_held[j, first + i] + block
        out_copy(j).start()
        return carry

    lax.fori_loop(0, rows, row, 0)
    for j in range(rows):
        out_copy(j).wait()
    for m in through:
        m.wait()


def fused_call(n_hst, n_chip, tokens, out_grad, up_blocks, up_cols, down_blocks, down_cols):
    rows, count, width, _ = up_blocks.shape
    tok, part = tokens.shape
    shards = n_hst * n_chip
    blocks = shards * part // width
    names = jnp.arange(blocks, dtype=jnp.int32)
    ranks = jnp.arange(count, dtype=jnp.int32)[None, None, :, None] - count
    cols = jnp.stack([up_cols, down_cols])
    hits = cols[:, :, :, None] == names
    inv = jnp.sum(jnp.where(hits, ranks, 0), axis=2, dtype=jnp.int32) + count
    hidden = rows * width
    bf, f32 = jnp.bfloat16, jnp.float32
    dma = pltpu.SemaphoreType.DMA
    whole = pl.BlockSpec(memory_space=pltpu.VMEM)
    smem = pl.BlockSpec(memory_space=pltpu.SMEM)
    anywhere = pl.BlockSpec(memory_space=pl.ANY)
    grads = jax.ShapeDtypeStruct((rows, count, width // 2, width), f32)

    def slots(amount):
        return pltpu.VMEM((amount, tok, part), bf)

    held = pl.pallas_call(
        functools.partial(fused_kernel, n_chip),
        in_specs=[smem] * 3 + [anywhere] * 4,
        out_specs=[whole] * 3 + [anywhere] * 2,
        out_shape=[
            pltpu.VMEM((tok, part), bf),
            pltpu.VMEM(grads.shape, f32),
            pltpu.VMEM(grads.shape, f32),
            pltpu.VMEM((blocks, tok, width), bf),
            pltpu.VMEM((rows, width // 2, tok), bf),
        ],
        scratch_shapes=[
            pltpu.VMEM((2, blocks, tok, width), bf),
            pltpu.VMEM((blocks, tok, width), bf),
            pltpu.VMEM((2, rows, count + 1, width, width), bf),
            pltpu.VMEM((hidden, part), bf),
            pltpu.VMEM((2, hidden, tok), f32),
            pltpu.VMEM((2, 2, rows, width // 2, tok), bf),
            pltpu.VMEM((rows, width // 2, tok), bf),
            pltpu.VMEM((tok, hidden), bf),
            slots(shards),
            slots(2 * n_chip),
        ]
        + [slots(n_chip)] * 5
        + [pltpu.VMEM((n_chip, tok // 2, part), bf)] * 2
        + [
            dma((2, 6, 2 * n_chip)),
            dma((2, shards)),
            dma((2, 3, 2 * n_chip)),
            dma((2, shards)),
            dma((2,)),
            dma((2,)),
            dma((4, 2 * n_chip)),
            dma((4, 2 * n_chip)),
            dma((2, part // width)),
            dma((2,)),
        ],
        compiler_params=pltpu.CompilerParams(
            collective_id=2, has_side_effects=True, vmem_limit_bytes=46 * 2**20
        ),
        cost_estimate=pl.CostEstimate(
            flops=22 * tok * hidden * shards * part // 4,
            bytes_accessed=20 * 2**20,
            transcendentals=hidden * tok,
        ),
    )(inv, up_cols, down_cols, tokens, out_grad, up_blocks, down_blocks)
    return pl.pallas_call(
        finish_kernel,
        in_specs=[smem] + [whole] * 5,
        out_specs=[anywhere] * 3,
        out_shape=[jax.ShapeDtypeStruct((tok, part), bf), grads, grads],
        scratch_shapes=[pltpu.VMEM(grads.shape, f32), dma((rows + 2,))],
        compiler_params=pltpu.CompilerParams(vmem_limit_bytes=24 * 2**20),
        cost_estimate=pl.CostEstimate(
            flops=2 * tok * hidden * count * width // 2,
            bytes_accessed=8 * 2**20,
            transcendentals=0,
        ),
    )(down_cols, *held)


def local(n_dp, n_hst, n_chip, tokens, out_grad, up_blocks, up_cols, down_blocks, down_cols):
    if n_dp == 2 and n_hst == 4 and n_chip >= 2 and n_chip % 2 == 0:
        return tuple(
            fused_call(
                n_hst, n_chip, tokens, out_grad, up_blocks, up_cols, down_blocks, down_cols
            )
        )
    whole_x, whole_dy = gather_call(n_hst, n_chip, tokens, out_grad)
    split = n_dp == 2
    partial_value, *grads = rows_call(
        split, whole_x, whole_dy, up_blocks, up_cols, down_blocks, down_cols
    )
    if split:
        swap = [(0, 1), (1, 0)]
        sums = [
            grads[i].astype(jnp.float32)
            + lax.ppermute(grads[i + 1], "dp", swap).astype(jnp.float32)
            for i in (0, 2)
        ]
    else:
        sums = [
            lax.psum_scatter(g, "dp", scatter_dimension=2, tiled=True).astype(jnp.float32)
            for g in grads
        ]
    summed = scatter_call(n_hst, n_chip, partial_value)
    return (summed, *sums)


def solution(mesh):
    placed = (
        P("dp", ("hst", "chip")),
        P("dp", ("hst", "chip")),
        P(("hst", "chip"), None, None, None),
        P(("hst", "chip"), None),
        P(("hst", "chip"), None, None, None),
        P(("hst", "chip"), None),
    )
    return jax.shard_map(
        functools.partial(local, mesh.shape["dp"], mesh.shape["hst"], mesh.shape["chip"]),
        mesh=mesh,
        in_specs=placed,
        out_specs=(
            P("dp", ("hst", "chip")),
            P(("hst", "chip"), None, "dp", None),
            P(("hst", "chip"), None, "dp", None),
        ),
        check_vma=False,
    )
```

```python
import functools

import jax
import jax.numpy as jnp
from jax import lax
from jax.experimental import pallas as pl
from jax.experimental.pallas import tpu as pltpu
from jax.sharding import PartitionSpec as P

NT = (((1,), (1,)), ((), ()))


def rows_kernel(
    split,
    up_cols,
    down_cols,
    me,
    x_ref,
    dy_ref,
    up_ref,
    down_ref,
    in_ref,
    *rest,
):
    outs, (acc, xs, dys, us, ds) = rest[:-5], rest[-5:]
    row = pl.program_id(0)
    width = up_ref.shape[-1]
    per_shard = x_ref.shape[2] // width
    count = up_ref.shape[1]

    @pl.when(row == 0)
    def _():
        acc[...] = jnp.zeros_like(acc)

    def place(col):
        return col // per_shard, pl.ds(pl.multiple_of((col % per_shard) * width, width), width)

    for k in range(count):
        lanes = pl.ds(k * width, width)
        shard, at = place(up_cols[row, k])
        xs[:, lanes] = x_ref[shard, :, at]
        shard, at = place(down_cols[row, k])
        dys[:, lanes] = dy_ref[shard, :, at]
        us[:, lanes] = up_ref[0, k]
        ds[:, lanes] = down_ref[0, k]
    pre = lax.dot_general(us[...], xs[...], NT, preferred_element_type=jnp.float32)
    hid = lax.dot_general(ds[...], dys[...], NT, preferred_element_type=jnp.float32)
    sig = 1.0 / (1.0 + jnp.exp(-pre))
    act = (pre * sig).astype(jnp.bfloat16)
    pre_grad_f = hid * sig * (1.0 + pre * (1.0 - sig))
    pre_grad = pre_grad_f.astype(jnp.bfloat16)
    pre_grad_t = pre_grad_f.T.astype(jnp.bfloat16)

    step = 4
    for base in range(0, count, step):
        lanes = pl.ds(base * width, step * width)
        up_part = jnp.dot(pre_grad, xs[:, lanes], preferred_element_type=jnp.float32)
        down_part = jnp.dot(act, dys[:, lanes], preferred_element_type=jnp.float32)
        back = jnp.dot(pre_grad_t, us[:, lanes], preferred_element_type=jnp.float32)
        for i in range(step):
            k = base + i
            cut = slice(i * width, (i + 1) * width)
            for part, out in ((up_part, outs[: len(outs) // 2]), (down_part, outs[len(outs) // 2 :])):
                block = part[:, cut].astype(jnp.bfloat16)
                if split:
                    half = width // 2
                    first = me[0] == 0
                    out[0][0, k] = jnp.where(first, block[:half], block[half:])
                    out[1][0, k] = jnp.where(first, block[half:], block[:half])
                else:
                    out[0][0, k] = block
            shard, at = place(up_cols[row, k])
            acc[shard, :, at] += back[:, cut]

    @pl.when(row == pl.num_programs(0) - 1)
    def _():
        for s in range(acc.shape[0]):
            in_ref[s] = acc[s].astype(jnp.bfloat16)


def rows_call(split, whole_x, whole_dy, up_blocks, up_cols, down_blocks, down_cols):
    rows, count, width, _ = up_blocks.shape
    shards, tok, part = whole_x.shape
    out_h = width // 2 if split else width
    n_out = 4 if split else 2
    whole = pl.BlockSpec(memory_space=pltpu.VMEM)
    smem = pl.BlockSpec(memory_space=pltpu.SMEM)

    def block(h):
        return pl.BlockSpec((1, count, h, width), lambda r: (r, 0, 0, 0))

    me = lax.axis_index("dp").astype(jnp.int32).reshape(1)
    flops = 10 * tok * rows * count * width * width
    return pl.pallas_call(
        functools.partial(rows_kernel, split),
        grid=(rows,),
        in_specs=[smem, smem, smem, whole, whole, block(width), block(width)],
        out_specs=[whole] + [block(out_h)] * n_out,
        out_shape=[jax.ShapeDtypeStruct(whole_x.shape, jnp.bfloat16)]
        + [jax.ShapeDtypeStruct((rows, count, out_h, width), jnp.bfloat16)] * n_out,
        scratch_shapes=[
            pltpu.VMEM(whole_x.shape, jnp.float32),
            pltpu.VMEM((tok, count * width), jnp.bfloat16),
            pltpu.VMEM((tok, count * width), jnp.bfloat16),
            pltpu.VMEM((width, count * width), jnp.bfloat16),
            pltpu.VMEM((width, count * width), jnp.bfloat16),
        ],
        compiler_params=pltpu.CompilerParams(
            dimension_semantics=("arbitrary",), vmem_limit_bytes=56 * 2**20
        ),
        cost_estimate=pl.CostEstimate(
            flops=flops, bytes_accessed=30 * 2**20, transcendentals=rows * width * tok
        ),
    )(up_cols, down_cols, me, whole_x, whole_dy, up_blocks, down_blocks)


MESH = pl.DeviceIdType.MESH
ALONG_UP, ALONG_DOWN, ACROSS, SIDE = range(4)


def gather_kernel(n_chip, x_ref, dy_ref, x_out, dy_out, send_sem, recv_sem, own_sem):
    hst, z = lax.axis_index("hst"), lax.axis_index("chip")
    far, c = hst // 2, hst % 2
    own = hst * n_chip + z
    ins, outs = (x_ref, dy_ref), (x_out, dy_out)
    not_last, not_first = z < n_chip - 1, z > 0
    peers = {
        ALONG_UP: {"hst": hst, "chip": (z + 1) % n_chip},
        ALONG_DOWN: {"hst": hst, "chip": (z + n_chip - 1) % n_chip},
        ACROSS: {"hst": (1 - far) * 2 + c, "chip": z},
        SIDE: {"hst": far * 2 + 1 - c, "chip": z},
    }

    barrier = pltpu.get_barrier_semaphore()

    def greet(way):
        pl.semaphore_signal(barrier, inc=1, device_id=peers[way], device_id_type=MESH)

    greet(ACROSS)
    greet(SIDE)
    pl.when(not_last)(lambda: greet(ALONG_UP))
    pl.when(not_first)(lambda: greet(ALONG_DOWN))
    inner = jnp.logical_and(not_last, not_first)
    pl.when(inner)(lambda: pl.semaphore_wait(barrier, 4))
    pl.when(jnp.logical_not(inner))(lambda: pl.semaphore_wait(barrier, 3))

    def copy(a, way, shard, source=None):
        return pltpu.make_async_remote_copy(
            src_ref=outs[a].at[shard] if source is None else source,
            dst_ref=outs[a].at[shard],
            send_sem=send_sem.at[a, way, shard],
            recv_sem=recv_sem.at[a, shard],
            device_id=peers[way],
            device_id_type=MESH,
        )

    def each(act):
        for t in range(n_chip + 1):
            for a in range(2):
                if t == 0:
                    act(a, (), own, None, True)
                elif t < n_chip:
                    below = z - t
                    act(a, (ALONG_UP,), hst * n_chip + below, below >= 0, False)
                    above = z + t
                    act(a, (ALONG_DOWN,), hst * n_chip + above, above < n_chip, False)
            for a in range(2):
                if t >= 1:
                    base = ((1 - far) * 2 + c) * n_chip
                    if t == 1:
                        act(a, None, base + z, None, False)
                    else:
                        act(a, None, base + z - (t - 1), z - (t - 1) >= 0, False)
                        act(a, None, base + z + (t - 1), z + (t - 1) < n_chip, False)

    def guarded(condition, run):
        if condition is None:
            run()
        else:
            pl.when(condition)(run)

    def forward(a, ways, shard, condition, is_own):
        def run():
            if not is_own:
                copy(a, SIDE, shard).wait_recv()
            source = ins[a] if is_own else None
            if ways is not None:
                if is_own or ALONG_UP in ways:
                    pl.when(not_last)(lambda: copy(a, ALONG_UP, shard, source).start())
                if is_own or ALONG_DOWN in ways:
                    pl.when(not_first)(lambda: copy(a, ALONG_DOWN, shard, source).start())
                copy(a, ACROSS, shard, source).start()
            copy(a, SIDE, shard, source).start()

        guarded(condition, run)

    def finish(a, ways, shard, condition, is_own):
        def run():
            source = ins[a] if is_own else None
            if ways is not None:
                if is_own or ALONG_UP in ways:
                    pl.when(not_last)(lambda: copy(a, ALONG_UP, shard, source).wait_send())
                if is_own or ALONG_DOWN in ways:
                    pl.when(not_first)(lambda: copy(a, ALONG_DOWN, shard, source).wait_send())
                copy(a, ACROSS, shard, source).wait_send()
            copy(a, SIDE, shard, source).wait_send()

        guarded(condition, run)

    each(forward)
    mine = [pltpu.make_async_copy(ins[a], outs[a].at[own], own_sem.at[a]) for a in range(2)]
    for m in mine:
        m.start()
    for half in range(2):
        for place in range(n_chip):
            for a in range(2):
                copy(a, SIDE, (half * 2 + 1 - c) * n_chip + place).wait_recv()
    each(finish)
    for m in mine:
        m.wait()


def gather_call(n_hst, n_chip, tokens, out_grad):
    if n_hst != 4:
        return [
            lax.all_gather(v, ("hst", "chip"), axis=0, tiled=False) for v in (tokens, out_grad)
        ]
    shards = n_hst * n_chip
    return pl.pallas_call(
        functools.partial(gather_kernel, n_chip),
        in_specs=[pl.BlockSpec(memory_space=pltpu.VMEM)] * 2,
        out_specs=[pl.BlockSpec(memory_space=pl.ANY)] * 2,
        out_shape=[jax.ShapeDtypeStruct((shards, *v.shape), v.dtype) for v in (tokens, out_grad)],
        scratch_shapes=[
            pltpu.SemaphoreType.DMA((2, 4, shards)),
            pltpu.SemaphoreType.DMA((2, shards)),
            pltpu.SemaphoreType.DMA((2,)),
        ],
        compiler_params=pltpu.CompilerParams(collective_id=0, has_side_effects=True),
    )(tokens, out_grad)


def scatter_kernel(n_chip, part, out, side, cross, up, down, cross_out, line_out, send_sem, recv_sem):
    hst, z = lax.axis_index("hst"), lax.axis_index("chip")
    far, c = hst // 2, hst % 2
    not_last, not_first = z < n_chip - 1, z > 0
    peers = {
        ALONG_UP: {"hst": hst, "chip": (z + 1) % n_chip},
        ALONG_DOWN: {"hst": hst, "chip": (z + n_chip - 1) % n_chip},
        ACROSS: {"hst": (1 - far) * 2 + c, "chip": z},
        SIDE: {"hst": far * 2 + 1 - c, "chip": z},
    }
    barrier = pltpu.get_barrier_semaphore()

    def greet(way):
        pl.semaphore_signal(barrier, inc=1, device_id=peers[way], device_id_type=MESH)

    greet(ACROSS)
    greet(SIDE)
    pl.when(not_last)(lambda: greet(ALONG_UP))
    pl.when(not_first)(lambda: greet(ALONG_DOWN))
    inner = jnp.logical_and(not_last, not_first)
    pl.when(inner)(lambda: pl.semaphore_wait(barrier, 4))
    pl.when(jnp.logical_not(inner))(lambda: pl.semaphore_wait(barrier, 3))

    def copy(way, source, target, slot):
        return pltpu.make_async_remote_copy(
            src_ref=source,
            dst_ref=target,
            send_sem=send_sem.at[way, slot],
            recv_sem=recv_sem.at[way, slot],
            device_id=peers[way],
            device_id_type=MESH,
        )

    def side_copy(half, place):
        slot = half * n_chip + place
        return copy(SIDE, part.at[(half * 2 + 1 - c) * n_chip + place], side.at[slot], slot)

    def cross_copy(place):
        return copy(ACROSS, cross_out.at[place], cross.at[place], place)

    def up_copy(place):
        return copy(ALONG_UP, line_out.at[place], up.at[place], place)

    def down_copy(place):
        return copy(ALONG_DOWN, line_out.at[place], down.at[place], place)

    def each(act):
        for t in range(n_chip - 1, 0, -1):
            pl.when(z + t < n_chip)(lambda t=t: act(z + t, 1))
            pl.when(z - t >= 0)(lambda t=t: act(z - t, -1))
        act(z, 0)

    rows = part.shape[1]
    chunk = 32 if rows % 32 == 0 else rows

    def total(store, terms):
        def body(i, carry):
            at = pl.ds(pl.multiple_of(i * chunk, chunk), chunk)
            value = None
            for ref, slot in terms:
                term = ref[slot, at, :].astype(jnp.float32)
                value = term if value is None else value + term
            store(at, value.astype(jnp.bfloat16))
            return carry

        lax.fori_loop(0, rows // chunk, body, 0)

    def to(ref, slot):
        def store(at, value):
            ref[slot, at, :] = value

        return store

    def to_out(at, value):
        out[at, :] = value

    each(lambda place, _: side_copy(1 - far, place).start())
    each(lambda place, _: side_copy(far, place).start())

    def cross_step(place, _):
        slot = (1 - far) * n_chip + place
        side_copy(1 - far, place).wait_recv()
        total(to(cross_out, place), [(part, ((1 - far) * 2 + c) * n_chip + place), (side, slot)])
        cross_copy(place).start()

    each(cross_step)

    def line_step(place, sign):
        slot = far * n_chip + place
        side_copy(far, place).wait_recv()
        cross_copy(place).wait_recv()
        base = [(part, (far * 2 + c) * n_chip + place), (side, slot), (cross, place)]
        if sign > 0:

            @pl.when(not_first)
            def _():
                up_copy(place).wait_recv()
                total(to(line_out, place), base + [(up, place)])

            @pl.when(jnp.logical_not(not_first))
            def _():
                total(to(line_out, place), base)

            up_copy(place).start()
        elif sign < 0:

            @pl.when(not_last)
            def _():
                down_copy(place).wait_recv()
                total(to(line_out, place), base + [(down, place)])

            @pl.when(jnp.logical_not(not_last))
            def _():
                total(to(line_out, place), base)

            down_copy(place).start()
        else:

            @pl.when(inner)
            def _():
                up_copy(place).wait_recv()
                down_copy(place).wait_recv()
                total(to_out, base + [(up, place), (down, place)])

            @pl.when(jnp.logical_not(not_first))
            def _():
                down_copy(place).wait_recv()
                total(to_out, base + [(down, place)])

            @pl.when(jnp.logical_not(not_last))
            def _():
                up_copy(place).wait_recv()
                total(to_out, base + [(up, place)])

    each(line_step)

    def finish(place, sign):
        side_copy(1 - far, place).wait_send()
        side_copy(far, place).wait_send()
        cross_copy(place).wait_send()
        if sign > 0:
            up_copy(place).wait_send()
        elif sign < 0:
            down_copy(place).wait_send()

    each(finish)


def scatter_call(n_hst, n_chip, part):
    if n_hst != 4 or n_chip < 2:
        return lax.psum_scatter(part, ("hst", "chip"), scatter_dimension=0, tiled=False)
    shards, rows, width = part.shape
    whole = pl.BlockSpec(memory_space=pltpu.VMEM)

    def slots(count):
        return pltpu.VMEM((count, rows, width), jnp.bfloat16)

    return pl.pallas_call(
        functools.partial(scatter_kernel, n_chip),
        in_specs=[whole],
        out_specs=whole,
        out_shape=jax.ShapeDtypeStruct((rows, width), jnp.bfloat16),
        scratch_shapes=[slots(2 * n_chip)]
        + [slots(n_chip)] * 5
        + [pltpu.SemaphoreType.DMA((4, 2 * n_chip))] * 2,
        compiler_params=pltpu.CompilerParams(
            collective_id=1, has_side_effects=True, vmem_limit_bytes=24 * 2**20
        ),
        cost_estimate=pl.CostEstimate(
            flops=shards * rows * width, bytes_accessed=120 * 2**20, transcendentals=0
        ),
    )(part)

PAIR, MATE = 4, 5


def fused_kernel(
    n_chip,
    inv,
    up_cols,
    down_cols,
    tokens,
    out_grad,
    up_hbm,
    down_hbm,
    in_ref,
    up_ref,
    down_ref,
    oth_dy,
    left_dy,
    own,
    oth_x,
    wts,
    dense,
    pre,
    lhs,
    left_x,
    back,
    part,
    side,
    cross,
    cross_out,
    up_in,
    down_in,
    line_out,
    far_up,
    far_down,
    g_send,
    g_recv,
    o_send,
    o_recv,
    l_send,
    l_recv,
    s_send,
    s_recv,
    own_sem,
    w_sem,
):
    dp, hst, z = lax.axis_index("dp"), lax.axis_index("hst"), lax.axis_index("chip")
    y, c = hst // 2, hst % 2
    _, rows, count_1, width, _ = wts.shape
    count = count_1 - 1
    tok = back.shape[0]
    per = dense.shape[1] // width
    half = width // 2
    events = 2 * n_chip
    not_last, not_first = z < n_chip - 1, z > 0
    inner = jnp.logical_and(not_last, not_first)
    toward = 1 - 2 * (z % 2)
    peers = {
        ALONG_UP: {"dp": dp, "hst": hst, "chip": (z + 1) % n_chip},
        ALONG_DOWN: {"dp": dp, "hst": hst, "chip": (z + n_chip - 1) % n_chip},
        ACROSS: {"dp": dp, "hst": (1 - y) * 2 + c, "chip": z},
        SIDE: {"dp": dp, "hst": y * 2 + 1 - c, "chip": z},
        PAIR: {"dp": 1 - dp, "hst": hst, "chip": z},
        MATE: {"dp": dp, "hst": hst, "chip": z + toward},
    }
    ins, oth = (tokens, out_grad), (oth_x, oth_dy)
    mine = hst * n_chip + z

    def blocks_of(shard):
        return pl.ds(shard * per, per)

    locals_ = [
        pltpu.make_async_copy(
            ins[a].at[:, pl.ds(b * width, width)], own.at[a, mine * per + b], own_sem.at[a, b]
        )
        for a in range(2)
        for b in range(per)
    ]
    weights = [
        pltpu.make_async_copy(w, wts.at[a, :, pl.ds(0, count)], w_sem.at[a])
        for a, w in enumerate((up_hbm, down_hbm))
    ]
    for m in locals_ + weights:
        m.start()

    barrier = pltpu.get_barrier_semaphore()

    def greet(way):
        pl.semaphore_signal(barrier, inc=1, device_id=peers[way], device_id_type=MESH)

    for way in (ACROSS, SIDE, PAIR):
        greet(way)
    pl.when(not_last)(lambda: greet(ALONG_UP))
    pl.when(not_first)(lambda: greet(ALONG_DOWN))
    pl.when(inner)(lambda: pl.semaphore_wait(barrier, 5))
    pl.when(jnp.logical_not(inner))(lambda: pl.semaphore_wait(barrier, 4))

    for m in locals_:
        m.wait()

    short = jnp.minimum(z, n_chip - 1 - z)

    def place_of(i):
        both = z + toward * (2 * (i % 2) - 1) * ((i + 1) // 2)
        return jnp.where(i <= 2 * short, both, jnp.where(2 * z < n_chip - 1, i, n_chip - 1 - i))

    last = n_chip - 1
    order = [(0, 0, 0), (0, 0, 1)]
    for i in range(1, n_chip):
        order += [(0, i, 0), (1, i - 1, 0), (0, i, 1), (1, i - 1, 1)]
    order += [(1, last, 1), (1, last, 0)]
    units = len(order)

    def pick(n, values):
        found = values[0]
        for m in range(1, len(values)):
            found = jnp.where(n == m, values[m], found)
        return found

    def unit_of(n):
        return tuple(pick(n, [u[m] for u in order]) for m in range(3))

    def shard_of(far, i, core):
        column = far * (1 - y) + (1 - far) * y
        return (column * 2 + core) * n_chip + place_of(i)

    def g_copy(a, way, shard, slot):
        return pltpu.make_async_remote_copy(
            src_ref=own.at[a, blocks_of(shard)],
            dst_ref=own.at[a, blocks_of(shard)],
            send_sem=g_send.at[a, way, slot],
            recv_sem=g_recv.at[a, shard],
            device_id=peers[way],
            device_id_type=MESH,
        )

    def x_copy(a, shard, slot):
        return pltpu.make_async_remote_copy(
            src_ref=own.at[a, blocks_of(shard)],
            dst_ref=oth[a].at[blocks_of(shard)],
            send_sem=g_send.at[a, PAIR, slot],
            recv_sem=o_recv.at[a, shard],
            device_id=peers[PAIR],
            device_id_type=MESH,
        )

    def o_copy(a, way, shard, slot):
        return pltpu.make_async_remote_copy(
            src_ref=oth[a].at[blocks_of(shard)],
            dst_ref=oth[a].at[blocks_of(shard)],
            send_sem=o_send.at[a, (SIDE, MATE, ACROSS).index(way), slot],
            recv_sem=o_recv.at[a, shard],
            device_id=peers[way],
            device_id_type=MESH,
        )

    def own_ways(far, i, a, act):
        place, shard, slot = place_of(i), shard_of(far, i, c), far * n_chip + i
        near = far == 0
        lined = (a == 1) & ((place == 0) | (place == last))
        along = near | lined
        act(g_copy(a, SIDE, shard, slot))
        pl.when(along & (place <= z) & not_last)(lambda: act(g_copy(a, ALONG_UP, shard, slot)))
        pl.when(along & (place >= z) & not_first)(lambda: act(g_copy(a, ALONG_DOWN, shard, slot)))
        across = near & (jnp.logical_not(lined) | (place == z))
        pl.when(across)(lambda: act(g_copy(a, ACROSS, shard, slot)))
        crossed = (far == 1) & (i == 2)
        pl.when((a == 0) & (i != 1) & jnp.logical_not(crossed))(lambda: act(x_copy(0, shard, slot)))
        pl.when((a == 1) & ((i == 0) | (i == 2)))(lambda: act(x_copy(1, shard, slot)))

    def assemble(a, shard):
        for j in range(rows):
            for b in range(per):
                dense[j * width : (j + 1) * width, b * width : (b + 1) * width] = wts[
                    a, j, inv[a, j, shard * per + b]
                ]

    def service(far, i, a):
        shard, slot = shard_of(far, i, c), far * n_chip + i
        o_copy(a, SIDE, shard, slot).wait_recv()
        o_copy(a, SIDE, shard, slot).start()

    def mate_service(far, a):
        o_copy(a, MATE, shard_of(far, 0, c), far * n_chip).start()

    def cross_over():
        return o_copy(0, ACROSS, shard_of(0, 2, c), 2)

    def gather_step(n, carry):
        @pl.when(n < units)
        def _():
            far, i, a = unit_of(n)
            pl.when(n > 1)(lambda: g_copy(a, SIDE, shard_of(far, i, c), 0).wait_recv())
            own_ways(far, i, a, lambda d: d.start())

        for far, at in ((0, units // 2 - 1), (1, units - 5)):

            @pl.when(n == at)
            def _():
                for a in range(2):
                    service(far, 0, a)
                    pl.when(jnp.logical_not(inner))(lambda: mate_service(far, a))

        if n_chip > 2:

            @pl.when(n == units - 3)
            def _():
                service(0, 2, 0)
                cross_over().start()

        @pl.when(n == 0)
        def _():
            for m in weights:
                m.wait()
            for a in range(2):
                wts[a, :, count] = jnp.zeros((rows, width, width), wts.dtype)
            pre[...] = jnp.zeros_like(pre)

        def unit(sib, carry):
            now = n - sib

            @pl.when((now >= 0) & (now < units))
            def _():
                far, i, a = unit_of(now)
                shard = shard_of(far, i, jnp.where(sib == 1, 1 - c, c))
                pl.when(sib == 1)(lambda: g_copy(a, SIDE, shard, 0).wait_recv())
                assemble(a, shard)
                taken = [own[a, shard * per + b] for b in range(per)]
                pre[a] += lax.dot_general(
                    dense[...],
                    jnp.concatenate(taken, axis=1),
                    NT,
                    preferred_element_type=jnp.float32,
                )

            return carry

        lax.fori_loop(0, 2, unit, 0)
        return carry

    lax.fori_loop(0, units + 1, gather_step, 0)

    def gates(j, carry):
        at = pl.ds(pl.multiple_of(j * width, width), width)
        p, h = pre[0, at, :], pre[1, at, :]
        sig = 1.0 / (1.0 + jnp.exp(-p))
        act = (p * sig).astype(jnp.bfloat16)
        grad_f = h * sig * (1.0 + p * (1.0 - sig))
        grad = grad_f.astype(jnp.bfloat16)
        for f in range(2):
            lhs[0, f, j] = grad[f * half : (f + 1) * half]
            lhs[1, f, j] = act[f * half : (f + 1) * half]
        back[:, at] = grad_f.T.astype(jnp.bfloat16)
        return carry

    lax.fori_loop(0, rows, gates, 0)

    def l_copy(a):
        return pltpu.make_async_remote_copy(
            src_ref=lhs.at[a, 1 - dp],
            dst_ref=(left_x, left_dy)[a],
            send_sem=l_send.at[a],
            recv_sem=l_recv.at[a],
            device_id=peers[PAIR],
            device_id_type=MESH,
        )

    def late_ways(act):
        for i in range(3, n_chip):
            for far in range(2):
                act(x_copy(1, shard_of(far, i, c), far * n_chip + i))

    l_copy(0).start()
    l_copy(1).start()
    late_ways(lambda d: d.start())

    @pl.when(inner)
    def _():
        for a, far in ((0, 0), (0, 1), (1, 0)):
            mate_service(far, a)

    def copy(way, source, target, slot):
        return pltpu.make_async_remote_copy(
            src_ref=source,
            dst_ref=target,
            send_sem=s_send.at[way, slot],
            recv_sem=s_recv.at[way, slot],
            device_id=peers[way],
            device_id_type=MESH,
        )

    def side_copy(column, place):
        slot = column * n_chip + place
        return copy(SIDE, part.at[(column * 2 + 1 - c) * n_chip + place], side.at[slot], slot)

    def between(place):
        return (place > 0) & (place < last)

    half_tok, quarter = tok // 2, tok // 4
    halves = (pl.ds(0, half_tok), pl.ds(half_tok, half_tok))
    third, top = pl.ds(half_tok, quarter), pl.ds(3 * quarter, quarter)

    def cross_act(place, h, act):
        def send(at):
            return copy(
                ACROSS, cross_out.at[place, at], cross.at[place, at], h * n_chip + place
            )

        if h == 0:
            act(send(halves[0]))
        else:
            pl.when(between(place))(lambda: act(send(third)))
            pl.when(jnp.logical_not(between(place)))(lambda: act(send(halves[1])))

    def late_cross(place):
        return copy(
            ACROSS, cross_out.at[place, top], cross.at[place, top], 2 * n_chip + place
        )

    def far_copy(way, place):
        target = far_up if way == ALONG_UP else far_down
        return copy(way, cross_out.at[place, top], target.at[place], 2 * n_chip + place)

    def up_copy(place, h):
        at = halves[h]
        return copy(
            ALONG_UP, line_out.at[place, at], up_in.at[place, at], h * n_chip + place
        )

    def down_copy(place, h):
        at = halves[h]
        return copy(
            ALONG_DOWN, line_out.at[place, at], down_in.at[place, at], h * n_chip + place
        )

    chunk = 32 if quarter % 32 == 0 else quarter

    def total(store, terms, start=0, stop=tok // chunk):
        def body(i, carry):
            at = pl.ds(pl.multiple_of(i * chunk, chunk), chunk)
            value = None
            for ref, slot, above in terms:
                rows_at = pl.ds(pl.multiple_of(i * chunk - above, chunk), chunk)
                term = ref[slot, rows_at, :].astype(jnp.float32)
                value = term if value is None else value + term
            store(at, value.astype(jnp.bfloat16))
            return carry

        lax.fori_loop(start, stop, body, 0)

    def to(ref, slot):
        def store(at, value):
            ref[slot, at, :] = value

        return store

    def to_out(at, value):
        in_ref[at, :] = value

    def pieces(column, place):
        def body(q, carry):
            core = jnp.where(q == 0, 1 - c, c)
            shard = (column * 2 + core) * n_chip + place
            assemble(0, shard)
            part[shard] = jnp.dot(
                back[...], dense[...], preferred_element_type=jnp.float32
            ).astype(jnp.bfloat16)
            pl.when(q == 0)(lambda: side_copy(column, place).start())
            return carry

        lax.fori_loop(0, 2, body, 0)

    def far_send(place):
        pl.when(z < place)(lambda: far_copy(ALONG_UP, place).start())
        pl.when(z > place)(lambda: far_copy(ALONG_DOWN, place).start())

    per_quarter = quarter // chunk

    def far_step(place):
        terms = [(cross_out, place, 0)]
        upper, middle = (far_up, place, 3 * quarter), (far_down, place, 3 * quarter)

        @pl.when((z < place) & not_first)
        def _():
            far_copy(ALONG_UP, place).wait_recv()
            total(to(cross_out, place), terms + [upper], 3 * per_quarter, 4 * per_quarter)
            far_send(place)

        @pl.when((z > place) & not_last)
        def _():
            far_copy(ALONG_DOWN, place).wait_recv()
            total(to(cross_out, place), terms + [middle], 3 * per_quarter, 4 * per_quarter)
            far_send(place)

    def far_end():
        @pl.when(between(z))
        def _():
            far_copy(ALONG_UP, z).wait_recv()
            far_copy(ALONG_DOWN, z).wait_recv()
            terms = [(cross_out, z, 0), (far_up, z, 3 * quarter), (far_down, z, 3 * quarter)]
            total(to(cross_out, z), terms, 3 * per_quarter, 4 * per_quarter)
            late_cross(z).start()

    def piece_step(r, carry):
        @pl.when((r > 0) & (r <= n_chip))
        def _():
            place = place_of(n_chip - r)
            slot = (1 - y) * n_chip + place
            side_copy(1 - y, place).wait_recv()
            total(
                to(cross_out, place),
                [(part, ((1 - y) * 2 + c) * n_chip + place, 0), (side, slot, 0)],
            )
            for h in range(2):
                cross_act(place, h, lambda d: d.start())
            ends = jnp.logical_or(
                (z < place) & jnp.logical_not(not_first), (z > place) & jnp.logical_not(not_last)
            )
            pl.when(between(place) & ends)(lambda: far_send(place))

        column = jnp.where(r < n_chip, 1 - y, y)
        pieces(column, place_of(n_chip - 1 - r % n_chip))
        return carry

    lax.fori_loop(0, n_chip + 2, piece_step, 0)

    for place in range(1, last):
        far_step(place)

    def line_half(place, h):
        slot = y * n_chip + place
        cross_act(place, h, lambda d: d.wait_recv())
        begin, end = h * 2 * per_quarter, (h + 1) * 2 * per_quarter
        full = end
        if h == 1:
            pl.when((place == z) & between(place))(lambda: late_cross(place).wait_recv())
            full = jnp.where(between(place) & (place != z), end - per_quarter, end)
        base = [(part, (y * 2 + c) * n_chip + place, 0), (side, slot, 0)]

        def sums(store, more):
            total(store, base + more + [(cross, place, 0)], begin, full)
            if h == 1:
                total(store, base + more, full, end)

        @pl.when(place > z)
        def _():
            @pl.when(not_first)
            def _():
                up_copy(place, h).wait_recv()
                sums(to(line_out, place), [(up_in, place, 0)])

            @pl.when(jnp.logical_not(not_first))
            def _():
                sums(to(line_out, place), [])

            up_copy(place, h).start()

        @pl.when(place < z)
        def _():
            @pl.when(not_last)
            def _():
                down_copy(place, h).wait_recv()
                sums(to(line_out, place), [(down_in, place, 0)])

            @pl.when(jnp.logical_not(not_last))
            def _():
                sums(to(line_out, place), [])

            down_copy(place, h).start()

        @pl.when(place == z)
        def _():
            @pl.when(inner)
            def _():
                up_copy(place, h).wait_recv()
                down_copy(place, h).wait_recv()
                sums(to_out, [(up_in, place, 0), (down_in, place, 0)])

            @pl.when(jnp.logical_not(not_first))
            def _():
                down_copy(place, h).wait_recv()
                sums(to_out, [(down_in, place, 0)])

            @pl.when(jnp.logical_not(not_last))
            def _():
                up_copy(place, h).wait_recv()
                sums(to_out, [(up_in, place, 0)])

    def line_step(place):
        side_copy(y, place).wait_recv()
        for h in range(2):
            line_half(place, h)

    cols, outs = (up_cols, down_cols), (up_ref, down_ref)
    step = 4 if count % 4 == 0 else 1

    def grad_row(a, left, source, j, add):
        for first in range(0, count, step):
            picked = [source(cols[a][j, k]) for k in range(first, first + step)]
            value = jnp.dot(
                left, jnp.concatenate(picked, axis=1), preferred_element_type=jnp.float32
            )
            for i in range(step):
                block = value[:, i * width : (i + 1) * width]
                if add:
                    outs[a][j, first + i] += block
                else:
                    outs[a][j, first + i] = block

    share = -(-rows // (n_chip - 1))

    def own_row(j, carry):
        for a in range(2):
            grad_row(a, lhs[a, dp, j], lambda col, a=a: own[a, col], j, False)
        return carry

    far_near = [(far, i) for i in range(3, n_chip) for far in range(2)]
    early = {0: [(far, i, 0) for far, i in far_near], 1: [(0, 1, 0), (1, 1, 0)]}
    if n_chip > 2:
        early[0] += [(1, 2, 0), (0, 2, 1), (1, 2, 1)]
    early[n_chip - 2] = early.get(n_chip - 2, []) + [(0, 1, 1)]
    def line_loop(r, carry):
        line_step(place_of(n_chip - 1 - r))
        pl.when(r == 0)(far_end)
        pl.when((r == n_chip - 2) & inner)(lambda: mate_service(1, 1))
        pl.when(r + 2 < n_chip)(lambda: pieces(y, place_of(jnp.maximum(n_chip - 3 - r, 0))))
        for at, listed in early.items():

            @pl.when(r == at)
            def _():
                for far, i, a in listed:
                    service(far, i, a)

        lax.fori_loop(
            jnp.minimum(r * share, rows), jnp.minimum((r + 1) * share, rows), own_row, 0
        )
        return carry

    lax.fori_loop(0, n_chip, line_loop, 0)

    def other_row(j, carry):
        grad_row(0, left_x[j], lambda col: oth_x[col], j, True)
        return carry

    for a in range(2):
        if a == 1:
            for far, i in far_near + [(1, 1)]:
                service(far, i, a)
        for far in range(2):
            for i in range(n_chip):
                o_copy(a, SIDE, shard_of(far, i, 1 - c), far * n_chip + i).wait_recv()
        l_copy(a).wait_recv()
        if a == 0:
            lax.fori_loop(0, rows, other_row, 0)

    def settle(n, carry):
        far, i, a = unit_of(n)
        own_ways(far, i, a, lambda d: d.wait_send())
        return carry

    lax.fori_loop(0, units, settle, 0)
    if n_chip > 2:
        cross_over().wait_send()
    late_ways(lambda d: d.wait_send())
    for a in range(2):
        for far in range(2):
            for i in range(n_chip):
                o_copy(a, SIDE, shard_of(far, i, c), far * n_chip + i).wait_send()
            o_copy(a, MATE, shard_of(far, 0, c), far * n_chip).wait_send()
        l_copy(a).wait_send()

    def settle_sum(place, carry):
        side_copy(1 - y, place).wait_send()
        side_copy(y, place).wait_send()
        for h in range(2):
            cross_act(place, h, lambda d: d.wait_send())

        @pl.when(between(place))
        def _():
            pl.when(z < place)(lambda: far_copy(ALONG_UP, place).wait_send())
            pl.when(z > place)(lambda: far_copy(ALONG_DOWN, place).wait_send())
            pl.when(z == place)(lambda: late_cross(place).wait_send())

        for h in range(2):
            pl.when(place > z)(lambda h=h: up_copy(place, h).wait_send())
            pl.when(place < z)(lambda h=h: down_copy(place, h).wait_send())
        return carry

    lax.fori_loop(0, n_chip, settle_sum, 0)


def finish_kernel(
    cols, in_held, up_held, down_held, other, left, in_out, up_out, down_out, sums, sems
):
    rows, count, _, width = sums.shape
    step = 4 if count % 4 == 0 else 1
    through = [
        pltpu.make_async_copy(in_held, in_out, sems.at[rows]),
        pltpu.make_async_copy(up_held, up_out, sems.at[rows + 1]),
    ]
    for m in through:
        m.start()

    def out_copy(j):
        return pltpu.make_async_copy(sums.at[j], down_out.at[j], sems.at[j])

    def row(j, carry):
        for first in range(0, count, step):
            picked = [other[cols[j, k]] for k in range(first, first + step)]
            value = jnp.dot(
                left[j], jnp.concatenate(picked, axis=1), preferred_element_type=jnp.float32
            )
            for i in range(step):
                block = value[:, i * width : (i + 1) * width]
                sums[j, first + i] = down_held[j, first + i] + block
        out_copy(j).start()
        return carry

    lax.fori_loop(0, rows, row, 0)
    for j in range(rows):
        out_copy(j).wait()
    for m in through:
        m.wait()


def fused_call(n_hst, n_chip, tokens, out_grad, up_blocks, up_cols, down_blocks, down_cols):
    rows, count, width, _ = up_blocks.shape
    tok, part = tokens.shape
    shards = n_hst * n_chip
    blocks = shards * part // width
    names = jnp.arange(blocks, dtype=jnp.int32)
    ranks = jnp.arange(count, dtype=jnp.int32)[None, None, :, None] - count
    cols = jnp.stack([up_cols, down_cols])
    hits = cols[:, :, :, None] == names
    inv = jnp.sum(jnp.where(hits, ranks, 0), axis=2, dtype=jnp.int32) + count
    hidden = rows * width
    bf, f32 = jnp.bfloat16, jnp.float32
    dma = pltpu.SemaphoreType.DMA
    whole = pl.BlockSpec(memory_space=pltpu.VMEM)
    smem = pl.BlockSpec(memory_space=pltpu.SMEM)
    anywhere = pl.BlockSpec(memory_space=pl.ANY)
    grads = jax.ShapeDtypeStruct((rows, count, width // 2, width), f32)

    def slots(amount):
        return pltpu.VMEM((amount, tok, part), bf)

    held = pl.pallas_call(
        functools.partial(fused_kernel, n_chip),
        in_specs=[smem] * 3 + [anywhere] * 4,
        out_specs=[whole] * 3 + [anywhere] * 2,
        out_shape=[
            pltpu.VMEM((tok, part), bf),
            pltpu.VMEM(grads.shape, f32),
            pltpu.VMEM(grads.shape, f32),
            pltpu.VMEM((blocks, tok, width), bf),
            pltpu.VMEM((rows, width // 2, tok), bf),
        ],
        scratch_shapes=[
            pltpu.VMEM((2, blocks, tok, width), bf),
            pltpu.VMEM((blocks, tok, width), bf),
            pltpu.VMEM((2, rows, count + 1, width, width), bf),
            pltpu.VMEM((hidden, part), bf),
            pltpu.VMEM((2, hidden, tok), f32),
            pltpu.VMEM((2, 2, rows, width // 2, tok), bf),
            pltpu.VMEM((rows, width // 2, tok), bf),
            pltpu.VMEM((tok, hidden), bf),
            slots(shards),
            slots(2 * n_chip),
        ]
        + [slots(n_chip)] * 5
        + [pltpu.VMEM((n_chip, tok // 4, part), bf)] * 2
        + [
            dma((2, 6, 2 * n_chip)),
            dma((2, shards)),
            dma((2, 3, 2 * n_chip)),
            dma((2, shards)),
            dma((2,)),
            dma((2,)),
            dma((4, 3 * n_chip)),
            dma((4, 3 * n_chip)),
            dma((2, part // width)),
            dma((2,)),
        ],
        compiler_params=pltpu.CompilerParams(
            collective_id=2, has_side_effects=True, vmem_limit_bytes=46 * 2**20
        ),
        cost_estimate=pl.CostEstimate(
            flops=22 * tok * hidden * shards * part // 4,
            bytes_accessed=20 * 2**20,
            transcendentals=hidden * tok,
        ),
    )(inv, up_cols, down_cols, tokens, out_grad, up_blocks, down_blocks)
    return pl.pallas_call(
        finish_kernel,
        in_specs=[smem] + [whole] * 5,
        out_specs=[anywhere] * 3,
        out_shape=[jax.ShapeDtypeStruct((tok, part), bf), grads, grads],
        scratch_shapes=[pltpu.VMEM(grads.shape, f32), dma((rows + 2,))],
        compiler_params=pltpu.CompilerParams(vmem_limit_bytes=24 * 2**20),
        cost_estimate=pl.CostEstimate(
            flops=2 * tok * hidden * count * width // 2,
            bytes_accessed=8 * 2**20,
            transcendentals=0,
        ),
    )(down_cols, *held)


def local(n_dp, n_hst, n_chip, tokens, out_grad, up_blocks, up_cols, down_blocks, down_cols):
    if n_dp == 2 and n_hst == 4 and n_chip >= 2 and n_chip % 2 == 0:
        return tuple(
            fused_call(
                n_hst, n_chip, tokens, out_grad, up_blocks, up_cols, down_blocks, down_cols
            )
        )
    whole_x, whole_dy = gather_call(n_hst, n_chip, tokens, out_grad)
    split = n_dp == 2
    partial_value, *grads = rows_call(
        split, whole_x, whole_dy, up_blocks, up_cols, down_blocks, down_cols
    )
    if split:
        swap = [(0, 1), (1, 0)]
        sums = [
            grads[i].astype(jnp.float32)
            + lax.ppermute(grads[i + 1], "dp", swap).astype(jnp.float32)
            for i in (0, 2)
        ]
    else:
        sums = [
            lax.psum_scatter(g, "dp", scatter_dimension=2, tiled=True).astype(jnp.float32)
            for g in grads
        ]
    summed = scatter_call(n_hst, n_chip, partial_value)
    return (summed, *sums)


def solution(mesh):
    placed = (
        P("dp", ("hst", "chip")),
        P("dp", ("hst", "chip")),
        P(("hst", "chip"), None, None, None),
        P(("hst", "chip"), None),
        P(("hst", "chip"), None, None, None),
        P(("hst", "chip"), None),
    )
    return jax.shard_map(
        functools.partial(local, mesh.shape["dp"], mesh.shape["hst"], mesh.shape["chip"]),
        mesh=mesh,
        in_specs=placed,
        out_specs=(
            P("dp", ("hst", "chip")),
            P(("hst", "chip"), None, "dp", None),
            P(("hst", "chip"), None, "dp", None),
        ),
        check_vma=False,
    )
```

```python
import functools

import jax
import jax.numpy as jnp
from jax import lax
from jax.experimental import pallas as pl
from jax.experimental.pallas import tpu as pltpu
from jax.sharding import PartitionSpec as P

NT = (((1,), (1,)), ((), ()))


def rows_kernel(
    split,
    up_cols,
    down_cols,
    me,
    x_ref,
    dy_ref,
    up_ref,
    down_ref,
    in_ref,
    *rest,
):
    outs, (acc, xs, dys, us, ds) = rest[:-5], rest[-5:]
    row = pl.program_id(0)
    width = up_ref.shape[-1]
    per_shard = x_ref.shape[2] // width
    count = up_ref.shape[1]

    @pl.when(row == 0)
    def _():
        acc[...] = jnp.zeros_like(acc)

    def place(col):
        return col // per_shard, pl.ds(pl.multiple_of((col % per_shard) * width, width), width)

    for k in range(count):
        lanes = pl.ds(k * width, width)
        shard, at = place(up_cols[row, k])
        xs[:, lanes] = x_ref[shard, :, at]
        shard, at = place(down_cols[row, k])
        dys[:, lanes] = dy_ref[shard, :, at]
        us[:, lanes] = up_ref[0, k]
        ds[:, lanes] = down_ref[0, k]
    pre = lax.dot_general(us[...], xs[...], NT, preferred_element_type=jnp.float32)
    hid = lax.dot_general(ds[...], dys[...], NT, preferred_element_type=jnp.float32)
    sig = 1.0 / (1.0 + jnp.exp(-pre))
    act = (pre * sig).astype(jnp.bfloat16)
    pre_grad_f = hid * sig * (1.0 + pre * (1.0 - sig))
    pre_grad = pre_grad_f.astype(jnp.bfloat16)
    pre_grad_t = pre_grad_f.T.astype(jnp.bfloat16)

    step = 4
    for base in range(0, count, step):
        lanes = pl.ds(base * width, step * width)
        up_part = jnp.dot(pre_grad, xs[:, lanes], preferred_element_type=jnp.float32)
        down_part = jnp.dot(act, dys[:, lanes], preferred_element_type=jnp.float32)
        back = jnp.dot(pre_grad_t, us[:, lanes], preferred_element_type=jnp.float32)
        for i in range(step):
            k = base + i
            cut = slice(i * width, (i + 1) * width)
            for part, out in ((up_part, outs[: len(outs) // 2]), (down_part, outs[len(outs) // 2 :])):
                block = part[:, cut].astype(jnp.bfloat16)
                if split:
                    half = width // 2
                    first = me[0] == 0
                    out[0][0, k] = jnp.where(first, block[:half], block[half:])
                    out[1][0, k] = jnp.where(first, block[half:], block[:half])
                else:
                    out[0][0, k] = block
            shard, at = place(up_cols[row, k])
            acc[shard, :, at] += back[:, cut]

    @pl.when(row == pl.num_programs(0) - 1)
    def _():
        for s in range(acc.shape[0]):
            in_ref[s] = acc[s].astype(jnp.bfloat16)


def rows_call(split, whole_x, whole_dy, up_blocks, up_cols, down_blocks, down_cols):
    rows, count, width, _ = up_blocks.shape
    shards, tok, part = whole_x.shape
    out_h = width // 2 if split else width
    n_out = 4 if split else 2
    whole = pl.BlockSpec(memory_space=pltpu.VMEM)
    smem = pl.BlockSpec(memory_space=pltpu.SMEM)

    def block(h):
        return pl.BlockSpec((1, count, h, width), lambda r: (r, 0, 0, 0))

    me = lax.axis_index("dp").astype(jnp.int32).reshape(1)
    flops = 10 * tok * rows * count * width * width
    return pl.pallas_call(
        functools.partial(rows_kernel, split),
        grid=(rows,),
        in_specs=[smem, smem, smem, whole, whole, block(width), block(width)],
        out_specs=[whole] + [block(out_h)] * n_out,
        out_shape=[jax.ShapeDtypeStruct(whole_x.shape, jnp.bfloat16)]
        + [jax.ShapeDtypeStruct((rows, count, out_h, width), jnp.bfloat16)] * n_out,
        scratch_shapes=[
            pltpu.VMEM(whole_x.shape, jnp.float32),
            pltpu.VMEM((tok, count * width), jnp.bfloat16),
            pltpu.VMEM((tok, count * width), jnp.bfloat16),
            pltpu.VMEM((width, count * width), jnp.bfloat16),
            pltpu.VMEM((width, count * width), jnp.bfloat16),
        ],
        compiler_params=pltpu.CompilerParams(
            dimension_semantics=("arbitrary",), vmem_limit_bytes=56 * 2**20
        ),
        cost_estimate=pl.CostEstimate(
            flops=flops, bytes_accessed=30 * 2**20, transcendentals=rows * width * tok
        ),
    )(up_cols, down_cols, me, whole_x, whole_dy, up_blocks, down_blocks)


MESH = pl.DeviceIdType.MESH
ALONG_UP, ALONG_DOWN, ACROSS, SIDE = range(4)


def gather_kernel(n_chip, x_ref, dy_ref, x_out, dy_out, send_sem, recv_sem, own_sem):
    hst, z = lax.axis_index("hst"), lax.axis_index("chip")
    far, c = hst // 2, hst % 2
    own = hst * n_chip + z
    ins, outs = (x_ref, dy_ref), (x_out, dy_out)
    not_last, not_first = z < n_chip - 1, z > 0
    peers = {
        ALONG_UP: {"hst": hst, "chip": (z + 1) % n_chip},
        ALONG_DOWN: {"hst": hst, "chip": (z + n_chip - 1) % n_chip},
        ACROSS: {"hst": (1 - far) * 2 + c, "chip": z},
        SIDE: {"hst": far * 2 + 1 - c, "chip": z},
    }

    barrier = pltpu.get_barrier_semaphore()

    def greet(way):
        pl.semaphore_signal(barrier, inc=1, device_id=peers[way], device_id_type=MESH)

    greet(ACROSS)
    greet(SIDE)
    pl.when(not_last)(lambda: greet(ALONG_UP))
    pl.when(not_first)(lambda: greet(ALONG_DOWN))
    inner = jnp.logical_and(not_last, not_first)
    pl.when(inner)(lambda: pl.semaphore_wait(barrier, 4))
    pl.when(jnp.logical_not(inner))(lambda: pl.semaphore_wait(barrier, 3))

    def copy(a, way, shard, source=None):
        return pltpu.make_async_remote_copy(
            src_ref=outs[a].at[shard] if source is None else source,
            dst_ref=outs[a].at[shard],
            send_sem=send_sem.at[a, way, shard],
            recv_sem=recv_sem.at[a, shard],
            device_id=peers[way],
            device_id_type=MESH,
        )

    def each(act):
        for t in range(n_chip + 1):
            for a in range(2):
                if t == 0:
                    act(a, (), own, None, True)
                elif t < n_chip:
                    below = z - t
                    act(a, (ALONG_UP,), hst * n_chip + below, below >= 0, False)
                    above = z + t
                    act(a, (ALONG_DOWN,), hst * n_chip + above, above < n_chip, False)
            for a in range(2):
                if t >= 1:
                    base = ((1 - far) * 2 + c) * n_chip
                    if t == 1:
                        act(a, None, base + z, None, False)
                    else:
                        act(a, None, base + z - (t - 1), z - (t - 1) >= 0, False)
                        act(a, None, base + z + (t - 1), z + (t - 1) < n_chip, False)

    def guarded(condition, run):
        if condition is None:
            run()
        else:
            pl.when(condition)(run)

    def forward(a, ways, shard, condition, is_own):
        def run():
            if not is_own:
                copy(a, SIDE, shard).wait_recv()
            source = ins[a] if is_own else None
            if ways is not None:
                if is_own or ALONG_UP in ways:
                    pl.when(not_last)(lambda: copy(a, ALONG_UP, shard, source).start())
                if is_own or ALONG_DOWN in ways:
                    pl.when(not_first)(lambda: copy(a, ALONG_DOWN, shard, source).start())
                copy(a, ACROSS, shard, source).start()
            copy(a, SIDE, shard, source).start()

        guarded(condition, run)

    def finish(a, ways, shard, condition, is_own):
        def run():
            source = ins[a] if is_own else None
            if ways is not None:
                if is_own or ALONG_UP in ways:
                    pl.when(not_last)(lambda: copy(a, ALONG_UP, shard, source).wait_send())
                if is_own or ALONG_DOWN in ways:
                    pl.when(not_first)(lambda: copy(a, ALONG_DOWN, shard, source).wait_send())
                copy(a, ACROSS, shard, source).wait_send()
            copy(a, SIDE, shard, source).wait_send()

        guarded(condition, run)

    each(forward)
    mine = [pltpu.make_async_copy(ins[a], outs[a].at[own], own_sem.at[a]) for a in range(2)]
    for m in mine:
        m.start()
    for half in range(2):
        for place in range(n_chip):
            for a in range(2):
                copy(a, SIDE, (half * 2 + 1 - c) * n_chip + place).wait_recv()
    each(finish)
    for m in mine:
        m.wait()


def gather_call(n_hst, n_chip, tokens, out_grad):
    if n_hst != 4:
        return [
            lax.all_gather(v, ("hst", "chip"), axis=0, tiled=False) for v in (tokens, out_grad)
        ]
    shards = n_hst * n_chip
    return pl.pallas_call(
        functools.partial(gather_kernel, n_chip),
        in_specs=[pl.BlockSpec(memory_space=pltpu.VMEM)] * 2,
        out_specs=[pl.BlockSpec(memory_space=pl.ANY)] * 2,
        out_shape=[jax.ShapeDtypeStruct((shards, *v.shape), v.dtype) for v in (tokens, out_grad)],
        scratch_shapes=[
            pltpu.SemaphoreType.DMA((2, 4, shards)),
            pltpu.SemaphoreType.DMA((2, shards)),
            pltpu.SemaphoreType.DMA((2,)),
        ],
        compiler_params=pltpu.CompilerParams(collective_id=0, has_side_effects=True),
    )(tokens, out_grad)


def scatter_kernel(n_chip, part, out, side, cross, up, down, cross_out, line_out, send_sem, recv_sem):
    hst, z = lax.axis_index("hst"), lax.axis_index("chip")
    far, c = hst // 2, hst % 2
    not_last, not_first = z < n_chip - 1, z > 0
    peers = {
        ALONG_UP: {"hst": hst, "chip": (z + 1) % n_chip},
        ALONG_DOWN: {"hst": hst, "chip": (z + n_chip - 1) % n_chip},
        ACROSS: {"hst": (1 - far) * 2 + c, "chip": z},
        SIDE: {"hst": far * 2 + 1 - c, "chip": z},
    }
    barrier = pltpu.get_barrier_semaphore()

    def greet(way):
        pl.semaphore_signal(barrier, inc=1, device_id=peers[way], device_id_type=MESH)

    greet(ACROSS)
    greet(SIDE)
    pl.when(not_last)(lambda: greet(ALONG_UP))
    pl.when(not_first)(lambda: greet(ALONG_DOWN))
    inner = jnp.logical_and(not_last, not_first)
    pl.when(inner)(lambda: pl.semaphore_wait(barrier, 4))
    pl.when(jnp.logical_not(inner))(lambda: pl.semaphore_wait(barrier, 3))

    def copy(way, source, target, slot):
        return pltpu.make_async_remote_copy(
            src_ref=source,
            dst_ref=target,
            send_sem=send_sem.at[way, slot],
            recv_sem=recv_sem.at[way, slot],
            device_id=peers[way],
            device_id_type=MESH,
        )

    def side_copy(half, place):
        slot = half * n_chip + place
        return copy(SIDE, part.at[(half * 2 + 1 - c) * n_chip + place], side.at[slot], slot)

    def cross_copy(place):
        return copy(ACROSS, cross_out.at[place], cross.at[place], place)

    def up_copy(place):
        return copy(ALONG_UP, line_out.at[place], up.at[place], place)

    def down_copy(place):
        return copy(ALONG_DOWN, line_out.at[place], down.at[place], place)

    def each(act):
        for t in range(n_chip - 1, 0, -1):
            pl.when(z + t < n_chip)(lambda t=t: act(z + t, 1))
            pl.when(z - t >= 0)(lambda t=t: act(z - t, -1))
        act(z, 0)

    rows = part.shape[1]
    chunk = 32 if rows % 32 == 0 else rows

    def total(store, terms):
        def body(i, carry):
            at = pl.ds(pl.multiple_of(i * chunk, chunk), chunk)
            value = None
            for ref, slot in terms:
                term = ref[slot, at, :].astype(jnp.float32)
                value = term if value is None else value + term
            store(at, value.astype(jnp.bfloat16))
            return carry

        lax.fori_loop(0, rows // chunk, body, 0)

    def to(ref, slot):
        def store(at, value):
            ref[slot, at, :] = value

        return store

    def to_out(at, value):
        out[at, :] = value

    each(lambda place, _: side_copy(1 - far, place).start())
    each(lambda place, _: side_copy(far, place).start())

    def cross_step(place, _):
        slot = (1 - far) * n_chip + place
        side_copy(1 - far, place).wait_recv()
        total(to(cross_out, place), [(part, ((1 - far) * 2 + c) * n_chip + place), (side, slot)])
        cross_copy(place).start()

    each(cross_step)

    def line_step(place, sign):
        slot = far * n_chip + place
        side_copy(far, place).wait_recv()
        cross_copy(place).wait_recv()
        base = [(part, (far * 2 + c) * n_chip + place), (side, slot), (cross, place)]
        if sign > 0:

            @pl.when(not_first)
            def _():
                up_copy(place).wait_recv()
                total(to(line_out, place), base + [(up, place)])

            @pl.when(jnp.logical_not(not_first))
            def _():
                total(to(line_out, place), base)

            up_copy(place).start()
        elif sign < 0:

            @pl.when(not_last)
            def _():
                down_copy(place).wait_recv()
                total(to(line_out, place), base + [(down, place)])

            @pl.when(jnp.logical_not(not_last))
            def _():
                total(to(line_out, place), base)

            down_copy(place).start()
        else:

            @pl.when(inner)
            def _():
                up_copy(place).wait_recv()
                down_copy(place).wait_recv()
                total(to_out, base + [(up, place), (down, place)])

            @pl.when(jnp.logical_not(not_first))
            def _():
                down_copy(place).wait_recv()
                total(to_out, base + [(down, place)])

            @pl.when(jnp.logical_not(not_last))
            def _():
                up_copy(place).wait_recv()
                total(to_out, base + [(up, place)])

    each(line_step)

    def finish(place, sign):
        side_copy(1 - far, place).wait_send()
        side_copy(far, place).wait_send()
        cross_copy(place).wait_send()
        if sign > 0:
            up_copy(place).wait_send()
        elif sign < 0:
            down_copy(place).wait_send()

    each(finish)


def scatter_call(n_hst, n_chip, part):
    if n_hst != 4 or n_chip < 2:
        return lax.psum_scatter(part, ("hst", "chip"), scatter_dimension=0, tiled=False)
    shards, rows, width = part.shape
    whole = pl.BlockSpec(memory_space=pltpu.VMEM)

    def slots(count):
        return pltpu.VMEM((count, rows, width), jnp.bfloat16)

    return pl.pallas_call(
        functools.partial(scatter_kernel, n_chip),
        in_specs=[whole],
        out_specs=whole,
        out_shape=jax.ShapeDtypeStruct((rows, width), jnp.bfloat16),
        scratch_shapes=[slots(2 * n_chip)]
        + [slots(n_chip)] * 5
        + [pltpu.SemaphoreType.DMA((4, 2 * n_chip))] * 2,
        compiler_params=pltpu.CompilerParams(
            collective_id=1, has_side_effects=True, vmem_limit_bytes=24 * 2**20
        ),
        cost_estimate=pl.CostEstimate(
            flops=shards * rows * width, bytes_accessed=120 * 2**20, transcendentals=0
        ),
    )(part)

PAIR, MATE = 4, 5


def fused_kernel(
    n_chip,
    inv,
    up_cols,
    down_cols,
    tokens,
    out_grad,
    up_hbm,
    down_hbm,
    in_ref,
    up_ref,
    down_ref,
    oth_dy,
    left_dy,
    own,
    oth_x,
    wts,
    dense,
    pre,
    lhs,
    left_x,
    back,
    part,
    side,
    cross,
    cross_out,
    up_in,
    down_in,
    line_out,
    far_up,
    far_down,
    g_send,
    g_recv,
    o_send,
    o_recv,
    l_send,
    l_recv,
    s_send,
    s_recv,
    own_sem,
    w_sem,
):
    dp, hst, z = lax.axis_index("dp"), lax.axis_index("hst"), lax.axis_index("chip")
    y, c = hst // 2, hst % 2
    _, rows, count_1, width, _ = wts.shape
    count = count_1 - 1
    tok = back.shape[0]
    per = dense.shape[1] // width
    half = width // 2
    events = 2 * n_chip
    not_last, not_first = z < n_chip - 1, z > 0
    inner = jnp.logical_and(not_last, not_first)
    toward = 1 - 2 * (z % 2)
    peers = {
        ALONG_UP: {"dp": dp, "hst": hst, "chip": (z + 1) % n_chip},
        ALONG_DOWN: {"dp": dp, "hst": hst, "chip": (z + n_chip - 1) % n_chip},
        ACROSS: {"dp": dp, "hst": (1 - y) * 2 + c, "chip": z},
        SIDE: {"dp": dp, "hst": y * 2 + 1 - c, "chip": z},
        PAIR: {"dp": 1 - dp, "hst": hst, "chip": z},
        MATE: {"dp": dp, "hst": hst, "chip": z + toward},
    }
    ins, oth = (tokens, out_grad), (oth_x, oth_dy)
    mine = hst * n_chip + z

    def blocks_of(shard):
        return pl.ds(shard * per, per)

    locals_ = [
        pltpu.make_async_copy(
            ins[a].at[:, pl.ds(b * width, width)], own.at[a, mine * per + b], own_sem.at[a, b]
        )
        for a in range(2)
        for b in range(per)
    ]
    weights = [
        pltpu.make_async_copy(w, wts.at[a, :, pl.ds(0, count)], w_sem.at[a])
        for a, w in enumerate((up_hbm, down_hbm))
    ]
    for m in locals_ + weights:
        m.start()

    barrier = pltpu.get_barrier_semaphore()

    def greet(way):
        pl.semaphore_signal(barrier, inc=1, device_id=peers[way], device_id_type=MESH)

    for way in (ACROSS, SIDE, PAIR):
        greet(way)
    pl.when(not_last)(lambda: greet(ALONG_UP))
    pl.when(not_first)(lambda: greet(ALONG_DOWN))
    pl.when(inner)(lambda: pl.semaphore_wait(barrier, 5))
    pl.when(jnp.logical_not(inner))(lambda: pl.semaphore_wait(barrier, 4))

    for m in locals_:
        m.wait()

    short = jnp.minimum(z, n_chip - 1 - z)

    def place_of(i):
        both = z + toward * (2 * (i % 2) - 1) * ((i + 1) // 2)
        return jnp.where(i <= 2 * short, both, jnp.where(2 * z < n_chip - 1, i, n_chip - 1 - i))

    last = n_chip - 1
    order = [(0, 0, 0), (0, 0, 1)]
    for i in range(1, n_chip):
        order += [(0, i, 0), (1, i - 1, 0), (0, i, 1), (1, i - 1, 1)]
    order += [(1, last, 1), (1, last, 0)]
    units = len(order)

    def pick(n, values):
        found = values[0]
        for m in range(1, len(values)):
            found = jnp.where(n == m, values[m], found)
        return found

    def unit_of(n):
        return tuple(pick(n, [u[m] for u in order]) for m in range(3))

    def shard_of(far, i, core):
        column = far * (1 - y) + (1 - far) * y
        return (column * 2 + core) * n_chip + place_of(i)

    def g_copy(a, way, shard, slot):
        return pltpu.make_async_remote_copy(
            src_ref=own.at[a, blocks_of(shard)],
            dst_ref=own.at[a, blocks_of(shard)],
            send_sem=g_send.at[a, way, slot],
            recv_sem=g_recv.at[a, shard],
            device_id=peers[way],
            device_id_type=MESH,
        )

    def x_copy(a, shard, slot):
        return pltpu.make_async_remote_copy(
            src_ref=own.at[a, blocks_of(shard)],
            dst_ref=oth[a].at[blocks_of(shard)],
            send_sem=g_send.at[a, PAIR, slot],
            recv_sem=o_recv.at[a, shard],
            device_id=peers[PAIR],
            device_id_type=MESH,
        )

    def o_copy(a, way, shard, slot):
        return pltpu.make_async_remote_copy(
            src_ref=oth[a].at[blocks_of(shard)],
            dst_ref=oth[a].at[blocks_of(shard)],
            send_sem=o_send.at[a, (SIDE, MATE, ACROSS).index(way), slot],
            recv_sem=o_recv.at[a, shard],
            device_id=peers[way],
            device_id_type=MESH,
        )

    def own_ways(far, i, a, act):
        place, shard, slot = place_of(i), shard_of(far, i, c), far * n_chip + i
        near = far == 0
        lined = (a == 1) & ((place == 0) | (place == last))
        along = near | lined
        act(g_copy(a, SIDE, shard, slot))
        pl.when(along & (place <= z) & not_last)(lambda: act(g_copy(a, ALONG_UP, shard, slot)))
        pl.when(along & (place >= z) & not_first)(lambda: act(g_copy(a, ALONG_DOWN, shard, slot)))
        across = near & (jnp.logical_not(lined) | (place == z))
        pl.when(across)(lambda: act(g_copy(a, ACROSS, shard, slot)))
        crossed = (far == 1) & (i == 2)
        pl.when((a == 0) & (i != 1) & jnp.logical_not(crossed))(lambda: act(x_copy(0, shard, slot)))
        pl.when((a == 1) & ((i == 0) | (i == 2)))(lambda: act(x_copy(1, shard, slot)))

    def assemble(a, shard):
        for j in range(rows):
            for b in range(per):
                dense[j * width : (j + 1) * width, b * width : (b + 1) * width] = wts[
                    a, j, inv[a, j, shard * per + b]
                ]

    def service(far, i, a):
        shard, slot = shard_of(far, i, c), far * n_chip + i
        o_copy(a, SIDE, shard, slot).wait_recv()
        o_copy(a, SIDE, shard, slot).start()

    def mate_service(far, a):
        o_copy(a, MATE, shard_of(far, 0, c), far * n_chip).start()

    def cross_over():
        return o_copy(0, ACROSS, shard_of(0, 2, c), 2)

    def end_over():
        return o_copy(1, ACROSS, shard_of(0, 1, c), 1)

    def gather_step(n, carry):
        far, i, a = unit_of(n)
        pl.when(n > 1)(lambda: g_copy(a, SIDE, shard_of(far, i, c), 0).wait_recv())
        own_ways(far, i, a, lambda d: d.start())

        for side_far, at in ((0, units // 2 - 1), (1, units - 5)):

            @pl.when(n == at)
            def _():
                for b in range(2):
                    service(side_far, 0, b)
                    if n_chip > 2 or side_far + b < 2:
                        pl.when(jnp.logical_not(inner))(lambda: mate_service(side_far, b))

        if n_chip > 2:

            @pl.when(n == units - 3)
            def _():
                service(0, 2, 0)
                cross_over().start()

        @pl.when(n == 0)
        def _():
            for m in weights:
                m.wait()
            for a in range(2):
                wts[a, :, count] = jnp.zeros((rows, width, width), wts.dtype)
            pre[...] = jnp.zeros_like(pre)

        def unit(q, carry):
            sib = jnp.where(q == 0, 0, 1)
            now = jnp.where(q == 1, n - 1, n)

            @pl.when((q == 0) | ((q == 1) & (n > 0) & (n < units - 1)) | ((q == 2) & (n > units - 3)))
            def _():
                far, i, a = unit_of(now)
                shard = shard_of(far, i, jnp.where(sib == 1, 1 - c, c))
                pl.when(sib == 1)(lambda: g_copy(a, SIDE, shard, 0).wait_recv())
                assemble(a, shard)
                taken = [own[a, shard * per + b] for b in range(per)]
                pre[a] += lax.dot_general(
                    dense[...],
                    jnp.concatenate(taken, axis=1),
                    NT,
                    preferred_element_type=jnp.float32,
                )

            return carry

        lax.fori_loop(0, 3, unit, 0)
        return carry

    lax.fori_loop(0, units, gather_step, 0)

    def gates(j, carry):
        at = pl.ds(pl.multiple_of(j * width, width), width)
        p, h = pre[0, at, :], pre[1, at, :]
        sig = 1.0 / (1.0 + jnp.exp(-p))
        act = (p * sig).astype(jnp.bfloat16)
        grad_f = h * sig * (1.0 + p * (1.0 - sig))
        grad = grad_f.astype(jnp.bfloat16)
        for f in range(2):
            lhs[0, f, j] = grad[f * half : (f + 1) * half]
            lhs[1, f, j] = act[f * half : (f + 1) * half]
        back[:, at] = grad_f.T.astype(jnp.bfloat16)
        return carry

    lax.fori_loop(0, rows, gates, 0)

    def l_copy(a):
        return pltpu.make_async_remote_copy(
            src_ref=lhs.at[a, 1 - dp],
            dst_ref=(left_x, left_dy)[a],
            send_sem=l_send.at[a],
            recv_sem=l_recv.at[a],
            device_id=peers[PAIR],
            device_id_type=MESH,
        )

    def late_ways(act):
        for i in range(3, n_chip):
            for far in range(2):
                act(x_copy(1, shard_of(far, i, c), far * n_chip + i))

    l_copy(0).start()
    l_copy(1).start()
    late_ways(lambda d: d.start())

    @pl.when(inner)
    def _():
        for a, far in ((0, 0), (0, 1), (1, 0)):
            mate_service(far, a)

    def copy(way, source, target, slot):
        return pltpu.make_async_remote_copy(
            src_ref=source,
            dst_ref=target,
            send_sem=s_send.at[way, slot],
            recv_sem=s_recv.at[way, slot],
            device_id=peers[way],
            device_id_type=MESH,
        )

    def side_copy(column, place):
        slot = column * n_chip + place
        return copy(SIDE, part.at[(column * 2 + 1 - c) * n_chip + place], side.at[slot], slot)

    def between(place):
        return (place > 0) & (place < last)

    half_tok, quarter = tok // 2, tok // 4
    halves = (pl.ds(0, half_tok), pl.ds(half_tok, half_tok))
    third, top = pl.ds(half_tok, quarter), pl.ds(3 * quarter, quarter)

    def cross_act(place, h, act):
        def send(at):
            return copy(
                ACROSS, cross_out.at[place, at], cross.at[place, at], h * n_chip + place
            )

        if h == 0:
            act(send(halves[0]))
        else:
            pl.when(between(place))(lambda: act(send(third)))
            pl.when(jnp.logical_not(between(place)))(lambda: act(send(halves[1])))

    def late_cross(place):
        return copy(
            ACROSS, cross_out.at[place, top], cross.at[place, top], 2 * n_chip + place
        )

    def far_copy(way, place):
        target = far_up if way == ALONG_UP else far_down
        return copy(way, cross_out.at[place, top], target.at[place], 2 * n_chip + place)

    def up_copy(place, h):
        at = halves[h]
        return copy(
            ALONG_UP, line_out.at[place, at], up_in.at[place, at], h * n_chip + place
        )

    def down_copy(place, h):
        at = halves[h]
        return copy(
            ALONG_DOWN, line_out.at[place, at], down_in.at[place, at], h * n_chip + place
        )

    chunk = 32 if quarter % 32 == 0 else quarter

    def total(store, terms, start=0, stop=tok // chunk):
        def body(i, carry):
            at = pl.ds(pl.multiple_of(i * chunk, chunk), chunk)
            value = None
            for ref, slot, above in terms:
                rows_at = pl.ds(pl.multiple_of(i * chunk - above, chunk), chunk)
                term = ref[slot, rows_at, :].astype(jnp.float32)
                value = term if value is None else value + term
            store(at, value.astype(jnp.bfloat16))
            return carry

        lax.fori_loop(start, stop, body, 0)

    def to(ref, slot):
        def store(at, value):
            ref[slot, at, :] = value

        return store

    def to_out(at, value):
        in_ref[at, :] = value

    def pieces(column, place):
        def body(q, carry):
            core = jnp.where(q == 0, 1 - c, c)
            shard = (column * 2 + core) * n_chip + place
            assemble(0, shard)
            part[shard] = jnp.dot(
                back[...], dense[...], preferred_element_type=jnp.float32
            ).astype(jnp.bfloat16)
            pl.when(q == 0)(lambda: side_copy(column, place).start())
            return carry

        lax.fori_loop(0, 2, body, 0)

    def far_send(place):
        pl.when(z < place)(lambda: far_copy(ALONG_UP, place).start())
        pl.when(z > place)(lambda: far_copy(ALONG_DOWN, place).start())

    per_quarter = quarter // chunk

    def far_step(place):
        terms = [(cross_out, place, 0)]
        upper, middle = (far_up, place, 3 * quarter), (far_down, place, 3 * quarter)

        @pl.when((z < place) & not_first)
        def _():
            far_copy(ALONG_UP, place).wait_recv()
            total(to(cross_out, place), terms + [upper], 3 * per_quarter, 4 * per_quarter)
            far_send(place)

        @pl.when((z > place) & not_last)
        def _():
            far_copy(ALONG_DOWN, place).wait_recv()
            total(to(cross_out, place), terms + [middle], 3 * per_quarter, 4 * per_quarter)
            far_send(place)

    def far_end():
        @pl.when(between(z))
        def _():
            far_copy(ALONG_UP, z).wait_recv()
            far_copy(ALONG_DOWN, z).wait_recv()
            terms = [(cross_out, z, 0), (far_up, z, 3 * quarter), (far_down, z, 3 * quarter)]
            total(to(cross_out, z), terms, 3 * per_quarter, 4 * per_quarter)
            late_cross(z).start()

    def cross_step(place):
        slot = (1 - y) * n_chip + place
        side_copy(1 - y, place).wait_recv()
        total(
            to(cross_out, place),
            [(part, ((1 - y) * 2 + c) * n_chip + place, 0), (side, slot, 0)],
        )
        for h in range(2):
            cross_act(place, h, lambda d: d.start())
        ends = ((z < place) & jnp.logical_not(not_first)) | (
            (z > place) & jnp.logical_not(not_last)
        )
        pl.when(between(place) & ends)(lambda: far_send(place))

    turn = min(2, last)

    def piece_step(q, carry):
        pl.when((q > 0) & (q != turn + 1))(
            lambda: cross_step(place_of(last - jnp.where(q > turn, q - 2, q - 1)))
        )
        column = jnp.where(q == turn, y, 1 - y)
        m = jnp.where(q == turn, 0, jnp.where(q > turn, q - 1, q))
        pieces(column, place_of(last - m))
        return carry

    lax.fori_loop(0, n_chip, piece_step, 0)
    if turn != last:
        cross_step(place_of(1))

    def line_half(place, h):
        slot = y * n_chip + place
        cross_act(place, h, lambda d: d.wait_recv())
        begin, end = h * 2 * per_quarter, (h + 1) * 2 * per_quarter
        full = end
        if h == 1:
            pl.when((place == z) & between(place))(lambda: late_cross(place).wait_recv())
            full = jnp.where(between(place) & (place != z), end - per_quarter, end)
        base = [(part, (y * 2 + c) * n_chip + place, 0), (side, slot, 0)]

        def sums(store, more):
            total(store, base + more + [(cross, place, 0)], begin, full)
            if h == 1:
                total(store, base + more, full, end)

        @pl.when(place > z)
        def _():
            @pl.when(not_first)
            def _():
                up_copy(place, h).wait_recv()
                sums(to(line_out, place), [(up_in, place, 0)])

            @pl.when(jnp.logical_not(not_first))
            def _():
                sums(to(line_out, place), [])

            up_copy(place, h).start()

        @pl.when(place < z)
        def _():
            @pl.when(not_last)
            def _():
                down_copy(place, h).wait_recv()
                sums(to(line_out, place), [(down_in, place, 0)])

            @pl.when(jnp.logical_not(not_last))
            def _():
                sums(to(line_out, place), [])

            down_copy(place, h).start()

        @pl.when(place == z)
        def _():
            @pl.when(inner)
            def _():
                up_copy(place, h).wait_recv()
                down_copy(place, h).wait_recv()
                sums(to_out, [(up_in, place, 0), (down_in, place, 0)])

            @pl.when(jnp.logical_not(not_first))
            def _():
                down_copy(place, h).wait_recv()
                sums(to_out, [(down_in, place, 0)])

            @pl.when(jnp.logical_not(not_last))
            def _():
                up_copy(place, h).wait_recv()
                sums(to_out, [(up_in, place, 0)])

    def line_step(place):
        side_copy(y, place).wait_recv()
        for h in range(2):
            line_half(place, h)

    cols, outs = (up_cols, down_cols), (up_ref, down_ref)
    step = 4 if count % 4 == 0 else 1

    def grad_row(a, left, source, j, add):
        for first in range(0, count, step):
            picked = [source(cols[a][j, k]) for k in range(first, first + step)]
            value = jnp.dot(
                left, jnp.concatenate(picked, axis=1), preferred_element_type=jnp.float32
            )
            for i in range(step):
                block = value[:, i * width : (i + 1) * width]
                if add:
                    outs[a][j, first + i] += block
                else:
                    outs[a][j, first + i] = block

    share = -(-rows // (n_chip - 1))

    def own_row(j, carry):
        for a in range(2):
            grad_row(a, lhs[a, dp, j], lambda col, a=a: own[a, col], j, False)
        return carry

    far_near = [(far, i) for i in range(3, n_chip) for far in range(2)]
    early = {0: [(far, i, 0) for far, i in far_near], 1: [(0, 1, 0), (1, 1, 0)]}
    if n_chip > 2:
        early[0] += [(1, 2, 0), (0, 2, 1), (1, 2, 1)]
    def line_loop(r, carry):
        line_step(place_of(last - r))
        pl.when(r == 0)(lambda: pieces(1 - y, place_of(0)))
        pl.when(r < last)(lambda: pieces(y, place_of(jnp.maximum(last - 1 - r, 0))))

        @pl.when(r == 0)
        def _():
            cross_step(place_of(0))
            for place in range(1, last):
                far_step(place)
            far_end()

        for at, listed in early.items():

            @pl.when(r == at)
            def _():
                for far, i, a in listed:
                    service(far, i, a)

        lax.fori_loop(
            jnp.minimum(r * share, rows), jnp.minimum((r + 1) * share, rows), own_row, 0
        )

        @pl.when(r == n_chip - 2)
        def _():
            service(0, 1, 1)
            pl.when(jnp.logical_not(inner))(lambda: end_over().start())

        return carry

    lax.fori_loop(0, n_chip, line_loop, 0)

    def other_row(j, carry):
        grad_row(0, left_x[j], lambda col: oth_x[col], j, True)
        return carry

    for a in range(2):
        if a == 1:
            for far, i in far_near + [(1, 1)]:
                service(far, i, a)
        for far in range(2):
            for i in range(n_chip):
                o_copy(a, SIDE, shard_of(far, i, 1 - c), far * n_chip + i).wait_recv()
        l_copy(a).wait_recv()
        if a == 0:
            lax.fori_loop(0, rows, other_row, 0)

    def settle(n, carry):
        far, i, a = unit_of(n)
        own_ways(far, i, a, lambda d: d.wait_send())
        return carry

    lax.fori_loop(0, units, settle, 0)
    if n_chip > 2:
        cross_over().wait_send()
    pl.when(jnp.logical_not(inner))(lambda: end_over().wait_send())
    late_ways(lambda d: d.wait_send())
    for a in range(2):
        for far in range(2):
            for i in range(n_chip):
                o_copy(a, SIDE, shard_of(far, i, c), far * n_chip + i).wait_send()
            mated = o_copy(a, MATE, shard_of(far, 0, c), far * n_chip)
            if a + far < 2:
                mated.wait_send()
            elif n_chip > 2:
                pl.when(jnp.logical_not(inner))(mated.wait_send)
        l_copy(a).wait_send()

    def settle_sum(place, carry):
        side_copy(1 - y, place).wait_send()
        side_copy(y, place).wait_send()
        for h in range(2):
            cross_act(place, h, lambda d: d.wait_send())

        @pl.when(between(place))
        def _():
            pl.when(z < place)(lambda: far_copy(ALONG_UP, place).wait_send())
            pl.when(z > place)(lambda: far_copy(ALONG_DOWN, place).wait_send())
            pl.when(z == place)(lambda: late_cross(place).wait_send())

        for h in range(2):
            pl.when(place > z)(lambda h=h: up_copy(place, h).wait_send())
            pl.when(place < z)(lambda h=h: down_copy(place, h).wait_send())
        return carry

    lax.fori_loop(0, n_chip, settle_sum, 0)


def finish_kernel(
    cols, in_held, up_held, down_held, other, left, in_out, up_out, down_out, sums, sems
):
    rows, count, _, width = sums.shape
    step = 4 if count % 4 == 0 else 1
    through = [
        pltpu.make_async_copy(in_held, in_out, sems.at[rows]),
        pltpu.make_async_copy(up_held, up_out, sems.at[rows + 1]),
    ]
    for m in through:
        m.start()

    def out_copy(j):
        return pltpu.make_async_copy(sums.at[j], down_out.at[j], sems.at[j])

    def row(j, carry):
        for first in range(0, count, step):
            picked = [other[cols[j, k]] for k in range(first, first + step)]
            value = jnp.dot(
                left[j], jnp.concatenate(picked, axis=1), preferred_element_type=jnp.float32
            )
            for i in range(step):
                block = value[:, i * width : (i + 1) * width]
                sums[j, first + i] = down_held[j, first + i] + block
        out_copy(j).start()
        return carry

    lax.fori_loop(0, rows, row, 0)
    for j in range(rows):
        out_copy(j).wait()
    for m in through:
        m.wait()


def fused_call(n_hst, n_chip, tokens, out_grad, up_blocks, up_cols, down_blocks, down_cols):
    rows, count, width, _ = up_blocks.shape
    tok, part = tokens.shape
    shards = n_hst * n_chip
    blocks = shards * part // width
    names = jnp.arange(blocks, dtype=jnp.int32)
    ranks = jnp.arange(count, dtype=jnp.int32)[None, None, :, None] - count
    cols = jnp.stack([up_cols, down_cols])
    hits = cols[:, :, :, None] == names
    inv = jnp.sum(jnp.where(hits, ranks, 0), axis=2, dtype=jnp.int32) + count
    hidden = rows * width
    bf, f32 = jnp.bfloat16, jnp.float32
    dma = pltpu.SemaphoreType.DMA
    whole = pl.BlockSpec(memory_space=pltpu.VMEM)
    smem = pl.BlockSpec(memory_space=pltpu.SMEM)
    anywhere = pl.BlockSpec(memory_space=pl.ANY)
    grads = jax.ShapeDtypeStruct((rows, count, width // 2, width), f32)

    def slots(amount):
        return pltpu.VMEM((amount, tok, part), bf)

    held = pl.pallas_call(
        functools.partial(fused_kernel, n_chip),
        in_specs=[smem] * 3 + [anywhere] * 4,
        out_specs=[whole] * 3 + [anywhere] * 2,
        out_shape=[
            pltpu.VMEM((tok, part), bf),
            pltpu.VMEM(grads.shape, f32),
            pltpu.VMEM(grads.shape, f32),
            pltpu.VMEM((blocks, tok, width), bf),
            pltpu.VMEM((rows, width // 2, tok), bf),
        ],
        scratch_shapes=[
            pltpu.VMEM((2, blocks, tok, width), bf),
            pltpu.VMEM((blocks, tok, width), bf),
            pltpu.VMEM((2, rows, count + 1, width, width), bf),
            pltpu.VMEM((hidden, part), bf),
            pltpu.VMEM((2, hidden, tok), f32),
            pltpu.VMEM((2, 2, rows, width // 2, tok), bf),
            pltpu.VMEM((rows, width // 2, tok), bf),
            pltpu.VMEM((tok, hidden), bf),
            slots(shards),
            slots(2 * n_chip),
        ]
        + [slots(n_chip)] * 5
        + [pltpu.VMEM((n_chip, tok // 4, part), bf)] * 2
        + [
            dma((2, 6, 2 * n_chip)),
            dma((2, shards)),
            dma((2, 3, 2 * n_chip)),
            dma((2, shards)),
            dma((2,)),
            dma((2,)),
            dma((4, 3 * n_chip)),
            dma((4, 3 * n_chip)),
            dma((2, part // width)),
            dma((2,)),
        ],
        compiler_params=pltpu.CompilerParams(
            collective_id=2, has_side_effects=True, vmem_limit_bytes=46 * 2**20
        ),
        cost_estimate=pl.CostEstimate(
            flops=22 * tok * hidden * shards * part // 4,
            bytes_accessed=20 * 2**20,
            transcendentals=hidden * tok,
        ),
    )(inv, up_cols, down_cols, tokens, out_grad, up_blocks, down_blocks)
    return pl.pallas_call(
        finish_kernel,
        in_specs=[smem] + [whole] * 5,
        out_specs=[anywhere] * 3,
        out_shape=[jax.ShapeDtypeStruct((tok, part), bf), grads, grads],
        scratch_shapes=[pltpu.VMEM(grads.shape, f32), dma((rows + 2,))],
        compiler_params=pltpu.CompilerParams(vmem_limit_bytes=24 * 2**20),
        cost_estimate=pl.CostEstimate(
            flops=2 * tok * hidden * count * width // 2,
            bytes_accessed=8 * 2**20,
            transcendentals=0,
        ),
    )(down_cols, *held)


def local(n_dp, n_hst, n_chip, tokens, out_grad, up_blocks, up_cols, down_blocks, down_cols):
    if n_dp == 2 and n_hst == 4 and n_chip == 4:
        return tuple(
            fused_call(
                n_hst, n_chip, tokens, out_grad, up_blocks, up_cols, down_blocks, down_cols
            )
        )
    whole_x, whole_dy = gather_call(n_hst, n_chip, tokens, out_grad)
    split = n_dp == 2
    partial_value, *grads = rows_call(
        split, whole_x, whole_dy, up_blocks, up_cols, down_blocks, down_cols
    )
    if split:
        swap = [(0, 1), (1, 0)]
        sums = [
            grads[i].astype(jnp.float32)
            + lax.ppermute(grads[i + 1], "dp", swap).astype(jnp.float32)
            for i in (0, 2)
        ]
    else:
        sums = [
            lax.psum_scatter(g, "dp", scatter_dimension=2, tiled=True).astype(jnp.float32)
            for g in grads
        ]
    summed = scatter_call(n_hst, n_chip, partial_value)
    return (summed, *sums)


def solution(mesh):
    placed = (
        P("dp", ("hst", "chip")),
        P("dp", ("hst", "chip")),
        P(("hst", "chip"), None, None, None),
        P(("hst", "chip"), None),
        P(("hst", "chip"), None, None, None),
        P(("hst", "chip"), None),
    )
    return jax.shard_map(
        functools.partial(local, mesh.shape["dp"], mesh.shape["hst"], mesh.shape["chip"]),
        mesh=mesh,
        in_specs=placed,
        out_specs=(
            P("dp", ("hst", "chip")),
            P(("hst", "chip"), None, "dp", None),
            P(("hst", "chip"), None, "dp", None),
        ),
        check_vma=False,
    )
```

```python
import functools

import jax
import jax.numpy as jnp
from jax import lax
from jax.experimental import pallas as pl
from jax.experimental.pallas import tpu as pltpu
from jax.sharding import PartitionSpec as P

NT = (((1,), (1,)), ((), ()))


def rows_kernel(
    split,
    up_cols,
    down_cols,
    me,
    x_ref,
    dy_ref,
    up_ref,
    down_ref,
    in_ref,
    *rest,
):
    outs, (acc, xs, dys, us, ds) = rest[:-5], rest[-5:]
    row = pl.program_id(0)
    width = up_ref.shape[-1]
    per_shard = x_ref.shape[2] // width
    count = up_ref.shape[1]

    @pl.when(row == 0)
    def _():
        acc[...] = jnp.zeros_like(acc)

    def place(col):
        return col // per_shard, pl.ds(pl.multiple_of((col % per_shard) * width, width), width)

    for k in range(count):
        lanes = pl.ds(k * width, width)
        shard, at = place(up_cols[row, k])
        xs[:, lanes] = x_ref[shard, :, at]
        shard, at = place(down_cols[row, k])
        dys[:, lanes] = dy_ref[shard, :, at]
        us[:, lanes] = up_ref[0, k]
        ds[:, lanes] = down_ref[0, k]
    pre = lax.dot_general(us[...], xs[...], NT, preferred_element_type=jnp.float32)
    hid = lax.dot_general(ds[...], dys[...], NT, preferred_element_type=jnp.float32)
    sig = 1.0 / (1.0 + jnp.exp(-pre))
    act = (pre * sig).astype(jnp.bfloat16)
    pre_grad_f = hid * sig * (1.0 + pre * (1.0 - sig))
    pre_grad = pre_grad_f.astype(jnp.bfloat16)
    pre_grad_t = pre_grad_f.T.astype(jnp.bfloat16)

    step = 4
    for base in range(0, count, step):
        lanes = pl.ds(base * width, step * width)
        up_part = jnp.dot(pre_grad, xs[:, lanes], preferred_element_type=jnp.float32)
        down_part = jnp.dot(act, dys[:, lanes], preferred_element_type=jnp.float32)
        back = jnp.dot(pre_grad_t, us[:, lanes], preferred_element_type=jnp.float32)
        for i in range(step):
            k = base + i
            cut = slice(i * width, (i + 1) * width)
            for part, out in ((up_part, outs[: len(outs) // 2]), (down_part, outs[len(outs) // 2 :])):
                block = part[:, cut].astype(jnp.bfloat16)
                if split:
                    half = width // 2
                    first = me[0] == 0
                    out[0][0, k] = jnp.where(first, block[:half], block[half:])
                    out[1][0, k] = jnp.where(first, block[half:], block[:half])
                else:
                    out[0][0, k] = block
            shard, at = place(up_cols[row, k])
            acc[shard, :, at] += back[:, cut]

    @pl.when(row == pl.num_programs(0) - 1)
    def _():
        for s in range(acc.shape[0]):
            in_ref[s] = acc[s].astype(jnp.bfloat16)


def rows_call(split, whole_x, whole_dy, up_blocks, up_cols, down_blocks, down_cols):
    rows, count, width, _ = up_blocks.shape
    shards, tok, part = whole_x.shape
    out_h = width // 2 if split else width
    n_out = 4 if split else 2
    whole = pl.BlockSpec(memory_space=pltpu.VMEM)
    smem = pl.BlockSpec(memory_space=pltpu.SMEM)

    def block(h):
        return pl.BlockSpec((1, count, h, width), lambda r: (r, 0, 0, 0))

    me = lax.axis_index("dp").astype(jnp.int32).reshape(1)
    flops = 10 * tok * rows * count * width * width
    return pl.pallas_call(
        functools.partial(rows_kernel, split),
        grid=(rows,),
        in_specs=[smem, smem, smem, whole, whole, block(width), block(width)],
        out_specs=[whole] + [block(out_h)] * n_out,
        out_shape=[jax.ShapeDtypeStruct(whole_x.shape, jnp.bfloat16)]
        + [jax.ShapeDtypeStruct((rows, count, out_h, width), jnp.bfloat16)] * n_out,
        scratch_shapes=[
            pltpu.VMEM(whole_x.shape, jnp.float32),
            pltpu.VMEM((tok, count * width), jnp.bfloat16),
            pltpu.VMEM((tok, count * width), jnp.bfloat16),
            pltpu.VMEM((width, count * width), jnp.bfloat16),
            pltpu.VMEM((width, count * width), jnp.bfloat16),
        ],
        compiler_params=pltpu.CompilerParams(
            dimension_semantics=("arbitrary",), vmem_limit_bytes=56 * 2**20
        ),
        cost_estimate=pl.CostEstimate(
            flops=flops, bytes_accessed=30 * 2**20, transcendentals=rows * width * tok
        ),
    )(up_cols, down_cols, me, whole_x, whole_dy, up_blocks, down_blocks)


MESH = pl.DeviceIdType.MESH
ALONG_UP, ALONG_DOWN, ACROSS, SIDE = range(4)


def gather_kernel(n_chip, x_ref, dy_ref, x_out, dy_out, send_sem, recv_sem, own_sem):
    hst, z = lax.axis_index("hst"), lax.axis_index("chip")
    far, c = hst // 2, hst % 2
    own = hst * n_chip + z
    ins, outs = (x_ref, dy_ref), (x_out, dy_out)
    not_last, not_first = z < n_chip - 1, z > 0
    peers = {
        ALONG_UP: {"hst": hst, "chip": (z + 1) % n_chip},
        ALONG_DOWN: {"hst": hst, "chip": (z + n_chip - 1) % n_chip},
        ACROSS: {"hst": (1 - far) * 2 + c, "chip": z},
        SIDE: {"hst": far * 2 + 1 - c, "chip": z},
    }

    barrier = pltpu.get_barrier_semaphore()

    def greet(way):
        pl.semaphore_signal(barrier, inc=1, device_id=peers[way], device_id_type=MESH)

    greet(ACROSS)
    greet(SIDE)
    pl.when(not_last)(lambda: greet(ALONG_UP))
    pl.when(not_first)(lambda: greet(ALONG_DOWN))
    inner = jnp.logical_and(not_last, not_first)
    pl.when(inner)(lambda: pl.semaphore_wait(barrier, 4))
    pl.when(jnp.logical_not(inner))(lambda: pl.semaphore_wait(barrier, 3))

    def copy(a, way, shard, source=None):
        return pltpu.make_async_remote_copy(
            src_ref=outs[a].at[shard] if source is None else source,
            dst_ref=outs[a].at[shard],
            send_sem=send_sem.at[a, way, shard],
            recv_sem=recv_sem.at[a, shard],
            device_id=peers[way],
            device_id_type=MESH,
        )

    def each(act):
        for t in range(n_chip + 1):
            for a in range(2):
                if t == 0:
                    act(a, (), own, None, True)
                elif t < n_chip:
                    below = z - t
                    act(a, (ALONG_UP,), hst * n_chip + below, below >= 0, False)
                    above = z + t
                    act(a, (ALONG_DOWN,), hst * n_chip + above, above < n_chip, False)
            for a in range(2):
                if t >= 1:
                    base = ((1 - far) * 2 + c) * n_chip
                    if t == 1:
                        act(a, None, base + z, None, False)
                    else:
                        act(a, None, base + z - (t - 1), z - (t - 1) >= 0, False)
                        act(a, None, base + z + (t - 1), z + (t - 1) < n_chip, False)

    def guarded(condition, run):
        if condition is None:
            run()
        else:
            pl.when(condition)(run)

    def forward(a, ways, shard, condition, is_own):
        def run():
            if not is_own:
                copy(a, SIDE, shard).wait_recv()
            source = ins[a] if is_own else None
            if ways is not None:
                if is_own or ALONG_UP in ways:
                    pl.when(not_last)(lambda: copy(a, ALONG_UP, shard, source).start())
                if is_own or ALONG_DOWN in ways:
                    pl.when(not_first)(lambda: copy(a, ALONG_DOWN, shard, source).start())
                copy(a, ACROSS, shard, source).start()
            copy(a, SIDE, shard, source).start()

        guarded(condition, run)

    def finish(a, ways, shard, condition, is_own):
        def run():
            source = ins[a] if is_own else None
            if ways is not None:
                if is_own or ALONG_UP in ways:
                    pl.when(not_last)(lambda: copy(a, ALONG_UP, shard, source).wait_send())
                if is_own or ALONG_DOWN in ways:
                    pl.when(not_first)(lambda: copy(a, ALONG_DOWN, shard, source).wait_send())
                copy(a, ACROSS, shard, source).wait_send()
            copy(a, SIDE, shard, source).wait_send()

        guarded(condition, run)

    each(forward)
    mine = [pltpu.make_async_copy(ins[a], outs[a].at[own], own_sem.at[a]) for a in range(2)]
    for m in mine:
        m.start()
    for half in range(2):
        for place in range(n_chip):
            for a in range(2):
                copy(a, SIDE, (half * 2 + 1 - c) * n_chip + place).wait_recv()
    each(finish)
    for m in mine:
        m.wait()


def gather_call(n_hst, n_chip, tokens, out_grad):
    if n_hst != 4:
        return [
            lax.all_gather(v, ("hst", "chip"), axis=0, tiled=False) for v in (tokens, out_grad)
        ]
    shards = n_hst * n_chip
    return pl.pallas_call(
        functools.partial(gather_kernel, n_chip),
        in_specs=[pl.BlockSpec(memory_space=pltpu.VMEM)] * 2,
        out_specs=[pl.BlockSpec(memory_space=pl.ANY)] * 2,
        out_shape=[jax.ShapeDtypeStruct((shards, *v.shape), v.dtype) for v in (tokens, out_grad)],
        scratch_shapes=[
            pltpu.SemaphoreType.DMA((2, 4, shards)),
            pltpu.SemaphoreType.DMA((2, shards)),
            pltpu.SemaphoreType.DMA((2,)),
        ],
        compiler_params=pltpu.CompilerParams(collective_id=0, has_side_effects=True),
    )(tokens, out_grad)


def scatter_kernel(n_chip, part, out, side, cross, up, down, cross_out, line_out, send_sem, recv_sem):
    hst, z = lax.axis_index("hst"), lax.axis_index("chip")
    far, c = hst // 2, hst % 2
    not_last, not_first = z < n_chip - 1, z > 0
    peers = {
        ALONG_UP: {"hst": hst, "chip": (z + 1) % n_chip},
        ALONG_DOWN: {"hst": hst, "chip": (z + n_chip - 1) % n_chip},
        ACROSS: {"hst": (1 - far) * 2 + c, "chip": z},
        SIDE: {"hst": far * 2 + 1 - c, "chip": z},
    }
    barrier = pltpu.get_barrier_semaphore()

    def greet(way):
        pl.semaphore_signal(barrier, inc=1, device_id=peers[way], device_id_type=MESH)

    greet(ACROSS)
    greet(SIDE)
    pl.when(not_last)(lambda: greet(ALONG_UP))
    pl.when(not_first)(lambda: greet(ALONG_DOWN))
    inner = jnp.logical_and(not_last, not_first)
    pl.when(inner)(lambda: pl.semaphore_wait(barrier, 4))
    pl.when(jnp.logical_not(inner))(lambda: pl.semaphore_wait(barrier, 3))

    def copy(way, source, target, slot):
        return pltpu.make_async_remote_copy(
            src_ref=source,
            dst_ref=target,
            send_sem=send_sem.at[way, slot],
            recv_sem=recv_sem.at[way, slot],
            device_id=peers[way],
            device_id_type=MESH,
        )

    def side_copy(half, place):
        slot = half * n_chip + place
        return copy(SIDE, part.at[(half * 2 + 1 - c) * n_chip + place], side.at[slot], slot)

    def cross_copy(place):
        return copy(ACROSS, cross_out.at[place], cross.at[place], place)

    def up_copy(place):
        return copy(ALONG_UP, line_out.at[place], up.at[place], place)

    def down_copy(place):
        return copy(ALONG_DOWN, line_out.at[place], down.at[place], place)

    def each(act):
        for t in range(n_chip - 1, 0, -1):
            pl.when(z + t < n_chip)(lambda t=t: act(z + t, 1))
            pl.when(z - t >= 0)(lambda t=t: act(z - t, -1))
        act(z, 0)

    rows = part.shape[1]
    chunk = 32 if rows % 32 == 0 else rows

    def total(store, terms):
        def body(i, carry):
            at = pl.ds(pl.multiple_of(i * chunk, chunk), chunk)
            value = None
            for ref, slot in terms:
                term = ref[slot, at, :].astype(jnp.float32)
                value = term if value is None else value + term
            store(at, value.astype(jnp.bfloat16))
            return carry

        lax.fori_loop(0, rows // chunk, body, 0)

    def to(ref, slot):
        def store(at, value):
            ref[slot, at, :] = value

        return store

    def to_out(at, value):
        out[at, :] = value

    each(lambda place, _: side_copy(1 - far, place).start())
    each(lambda place, _: side_copy(far, place).start())

    def cross_step(place, _):
        slot = (1 - far) * n_chip + place
        side_copy(1 - far, place).wait_recv()
        total(to(cross_out, place), [(part, ((1 - far) * 2 + c) * n_chip + place), (side, slot)])
        cross_copy(place).start()

    each(cross_step)

    def line_step(place, sign):
        slot = far * n_chip + place
        side_copy(far, place).wait_recv()
        cross_copy(place).wait_recv()
        base = [(part, (far * 2 + c) * n_chip + place), (side, slot), (cross, place)]
        if sign > 0:

            @pl.when(not_first)
            def _():
                up_copy(place).wait_recv()
                total(to(line_out, place), base + [(up, place)])

            @pl.when(jnp.logical_not(not_first))
            def _():
                total(to(line_out, place), base)

            up_copy(place).start()
        elif sign < 0:

            @pl.when(not_last)
            def _():
                down_copy(place).wait_recv()
                total(to(line_out, place), base + [(down, place)])

            @pl.when(jnp.logical_not(not_last))
            def _():
                total(to(line_out, place), base)

            down_copy(place).start()
        else:

            @pl.when(inner)
            def _():
                up_copy(place).wait_recv()
                down_copy(place).wait_recv()
                total(to_out, base + [(up, place), (down, place)])

            @pl.when(jnp.logical_not(not_first))
            def _():
                down_copy(place).wait_recv()
                total(to_out, base + [(down, place)])

            @pl.when(jnp.logical_not(not_last))
            def _():
                up_copy(place).wait_recv()
                total(to_out, base + [(up, place)])

    each(line_step)

    def finish(place, sign):
        side_copy(1 - far, place).wait_send()
        side_copy(far, place).wait_send()
        cross_copy(place).wait_send()
        if sign > 0:
            up_copy(place).wait_send()
        elif sign < 0:
            down_copy(place).wait_send()

    each(finish)


def scatter_call(n_hst, n_chip, part):
    if n_hst != 4 or n_chip < 2:
        return lax.psum_scatter(part, ("hst", "chip"), scatter_dimension=0, tiled=False)
    shards, rows, width = part.shape
    whole = pl.BlockSpec(memory_space=pltpu.VMEM)

    def slots(count):
        return pltpu.VMEM((count, rows, width), jnp.bfloat16)

    return pl.pallas_call(
        functools.partial(scatter_kernel, n_chip),
        in_specs=[whole],
        out_specs=whole,
        out_shape=jax.ShapeDtypeStruct((rows, width), jnp.bfloat16),
        scratch_shapes=[slots(2 * n_chip)]
        + [slots(n_chip)] * 5
        + [pltpu.SemaphoreType.DMA((4, 2 * n_chip))] * 2,
        compiler_params=pltpu.CompilerParams(
            collective_id=1, has_side_effects=True, vmem_limit_bytes=24 * 2**20
        ),
        cost_estimate=pl.CostEstimate(
            flops=shards * rows * width, bytes_accessed=120 * 2**20, transcendentals=0
        ),
    )(part)

PAIR, MATE = 4, 5


def fused_kernel(
    n_chip,
    inv,
    up_cols,
    down_cols,
    tokens,
    out_grad,
    up_hbm,
    down_hbm,
    in_ref,
    up_ref,
    down_ref,
    oth_dy,
    left_dy,
    own,
    oth_x,
    wts,
    dense,
    pre,
    lhs,
    left_x,
    back,
    part,
    side,
    cross,
    cross_out,
    up_in,
    down_in,
    line_out,
    far_up,
    far_down,
    g_send,
    g_recv,
    o_send,
    o_recv,
    l_send,
    l_recv,
    s_send,
    s_recv,
    own_sem,
    w_sem,
):
    dp, hst, z = lax.axis_index("dp"), lax.axis_index("hst"), lax.axis_index("chip")
    y, c = hst // 2, hst % 2
    _, rows, count_1, width, _ = wts.shape
    count = count_1 - 1
    tok = back.shape[0]
    shards = dense.shape[0] - 1
    per = dense.shape[2] // width
    half = width // 2
    events = 2 * n_chip
    not_last, not_first = z < n_chip - 1, z > 0
    inner = jnp.logical_and(not_last, not_first)
    toward = 1 - 2 * (z % 2)
    peers = {
        ALONG_UP: {"dp": dp, "hst": hst, "chip": (z + 1) % n_chip},
        ALONG_DOWN: {"dp": dp, "hst": hst, "chip": (z + n_chip - 1) % n_chip},
        ACROSS: {"dp": dp, "hst": (1 - y) * 2 + c, "chip": z},
        SIDE: {"dp": dp, "hst": y * 2 + 1 - c, "chip": z},
        PAIR: {"dp": 1 - dp, "hst": hst, "chip": z},
        MATE: {"dp": dp, "hst": hst, "chip": z + toward},
    }
    ins, oth = (tokens, out_grad), (oth_x, oth_dy)
    mine = hst * n_chip + z

    def blocks_of(shard):
        return pl.ds(shard * per, per)

    locals_ = [
        pltpu.make_async_copy(
            ins[a].at[:, pl.ds(b * width, width)], own.at[a, mine * per + b], own_sem.at[a, b]
        )
        for a in range(2)
        for b in range(per)
    ]
    weights = [
        pltpu.make_async_copy(w, wts.at[a, :, pl.ds(0, count)], w_sem.at[a])
        for a, w in enumerate((up_hbm, down_hbm))
    ]
    for m in locals_ + weights:
        m.start()

    barrier = pltpu.get_barrier_semaphore()

    def greet(way):
        pl.semaphore_signal(barrier, inc=1, device_id=peers[way], device_id_type=MESH)

    for way in (ACROSS, SIDE, PAIR):
        greet(way)
    pl.when(not_last)(lambda: greet(ALONG_UP))
    pl.when(not_first)(lambda: greet(ALONG_DOWN))
    pl.when(inner)(lambda: pl.semaphore_wait(barrier, 5))
    pl.when(jnp.logical_not(inner))(lambda: pl.semaphore_wait(barrier, 4))

    for m in locals_:
        m.wait()

    short = jnp.minimum(z, n_chip - 1 - z)

    def place_of(i):
        both = z + toward * (2 * (i % 2) - 1) * ((i + 1) // 2)
        return jnp.where(i <= 2 * short, both, jnp.where(2 * z < n_chip - 1, i, n_chip - 1 - i))

    last = n_chip - 1
    order = [(0, 0, 0), (0, 0, 1)]
    for i in range(1, n_chip):
        order += [(0, i, 0), (1, i - 1, 0), (0, i, 1), (1, i - 1, 1)]
    order += [(1, last, 1), (1, last, 0)]
    units = len(order)

    def pick(n, values):
        found = values[0]
        for m in range(1, len(values)):
            found = jnp.where(n == m, values[m], found)
        return found

    def unit_of(n):
        return tuple(pick(n, [u[m] for u in order]) for m in range(3))

    def shard_of(far, i, core):
        column = far * (1 - y) + (1 - far) * y
        return (column * 2 + core) * n_chip + place_of(i)

    def g_copy(a, way, shard, slot):
        return pltpu.make_async_remote_copy(
            src_ref=own.at[a, blocks_of(shard)],
            dst_ref=own.at[a, blocks_of(shard)],
            send_sem=g_send.at[a, way, slot],
            recv_sem=g_recv.at[a, shard],
            device_id=peers[way],
            device_id_type=MESH,
        )

    def x_copy(a, shard, slot):
        return pltpu.make_async_remote_copy(
            src_ref=own.at[a, blocks_of(shard)],
            dst_ref=oth[a].at[blocks_of(shard)],
            send_sem=g_send.at[a, PAIR, slot],
            recv_sem=o_recv.at[a, shard],
            device_id=peers[PAIR],
            device_id_type=MESH,
        )

    def o_copy(a, way, shard, slot):
        return pltpu.make_async_remote_copy(
            src_ref=oth[a].at[blocks_of(shard)],
            dst_ref=oth[a].at[blocks_of(shard)],
            send_sem=o_send.at[a, (SIDE, MATE, ACROSS).index(way), slot],
            recv_sem=o_recv.at[a, shard],
            device_id=peers[way],
            device_id_type=MESH,
        )

    def own_ways(far, i, a, act):
        place, shard, slot = place_of(i), shard_of(far, i, c), far * n_chip + i
        near = far == 0
        lined = (a == 1) & ((place == 0) | (place == last))
        along = near | lined
        act(g_copy(a, SIDE, shard, slot))
        pl.when(along & (place <= z) & not_last)(lambda: act(g_copy(a, ALONG_UP, shard, slot)))
        pl.when(along & (place >= z) & not_first)(lambda: act(g_copy(a, ALONG_DOWN, shard, slot)))
        across = near & (jnp.logical_not(lined) | (place == z))
        pl.when(across)(lambda: act(g_copy(a, ACROSS, shard, slot)))
        crossed = (far == 1) & (i == 2)
        pl.when((a == 0) & (i != 1) & jnp.logical_not(crossed))(lambda: act(x_copy(0, shard, slot)))
        pl.when((a == 1) & ((i == 0) | (i == 2)))(lambda: act(x_copy(1, shard, slot)))

    def assemble(a, shard, to):
        for j in range(rows):
            for b in range(per):
                dense[to, j * width : (j + 1) * width, b * width : (b + 1) * width] = wts[
                    a, j, inv[a, j, shard * per + b]
                ]

    def service(far, i, a):
        shard, slot = shard_of(far, i, c), far * n_chip + i
        o_copy(a, SIDE, shard, slot).wait_recv()
        o_copy(a, SIDE, shard, slot).start()

    def mate_service(far, a):
        o_copy(a, MATE, shard_of(far, 0, c), far * n_chip).start()

    def cross_over():
        return o_copy(0, ACROSS, shard_of(0, 2, c), 2)

    def gather_step(n, carry):
        @pl.when(n < units)
        def _():
            far, i, a = unit_of(n)
            pl.when(n > 1)(lambda: g_copy(a, SIDE, shard_of(far, i, c), 0).wait_recv())
            own_ways(far, i, a, lambda d: d.start())

        for far, at in ((0, units // 2 - 1), (1, units - 5)):

            @pl.when(n == at)
            def _():
                for a in range(2):
                    service(far, 0, a)
                    pl.when(jnp.logical_not(inner))(lambda: mate_service(far, a))

        if n_chip > 2:

            @pl.when(n == units - 3)
            def _():
                service(0, 2, 0)
                cross_over().start()

        @pl.when(n == 0)
        def _():
            for m in weights:
                m.wait()
            for a in range(2):
                wts[a, :, count] = jnp.zeros((rows, width, width), wts.dtype)
            pre[...] = jnp.zeros_like(pre)

        def unit(sib, carry):
            now = n - sib

            @pl.when((now >= 0) & (now < units))
            def _():
                far, i, a = unit_of(now)
                shard = shard_of(far, i, jnp.where(sib == 1, 1 - c, c))
                pl.when(sib == 1)(lambda: g_copy(a, SIDE, shard, 0).wait_recv())
                to = jnp.where(a == 0, shard, shards)
                assemble(a, shard, to)
                taken = [own[a, shard * per + b] for b in range(per)]
                pre[a] += lax.dot_general(
                    dense[to],
                    jnp.concatenate(taken, axis=1),
                    NT,
                    preferred_element_type=jnp.float32,
                )

            return carry

        lax.fori_loop(0, 2, unit, 0)
        return carry

    lax.fori_loop(0, units + 1, gather_step, 0)

    def gates(j, carry):
        at = pl.ds(pl.multiple_of(j * width, width), width)
        p, h = pre[0, at, :], pre[1, at, :]
        sig = 1.0 / (1.0 + jnp.exp(-p))
        act = (p * sig).astype(jnp.bfloat16)
        grad_f = h * sig * (1.0 + p * (1.0 - sig))
        grad = grad_f.astype(jnp.bfloat16)
        for f in range(2):
            lhs[0, f, j] = grad[f * half : (f + 1) * half]
            lhs[1, f, j] = act[f * half : (f + 1) * half]
        back[:, at] = grad_f.T.astype(jnp.bfloat16)
        return carry

    lax.fori_loop(0, rows, gates, 0)

    def l_copy(a):
        return pltpu.make_async_remote_copy(
            src_ref=lhs.at[a, 1 - dp],
            dst_ref=(left_x, left_dy)[a],
            send_sem=l_send.at[a],
            recv_sem=l_recv.at[a],
            device_id=peers[PAIR],
            device_id_type=MESH,
        )

    def late_ways(act):
        for i in range(3, n_chip):
            for far in range(2):
                act(x_copy(1, shard_of(far, i, c), far * n_chip + i))

    l_copy(0).start()
    l_copy(1).start()
    late_ways(lambda d: d.start())

    @pl.when(inner)
    def _():
        for a in range(2):
            for far in range(2):
                mate_service(far, a)

    def copy(way, source, target, slot):
        return pltpu.make_async_remote_copy(
            src_ref=source,
            dst_ref=target,
            send_sem=s_send.at[way, slot],
            recv_sem=s_recv.at[way, slot],
            device_id=peers[way],
            device_id_type=MESH,
        )

    def side_copy(column, place):
        slot = column * n_chip + place
        return copy(SIDE, part.at[(column * 2 + 1 - c) * n_chip + place], side.at[slot], slot)

    def between(place):
        return (place > 0) & (place < last)

    low, high = pl.ds(0, tok // 2), pl.ds(tok // 2, tok // 2)

    def cross_act(place, act):
        def send(at, slot):
            return copy(ACROSS, cross_out.at[place, at], cross.at[place, at], slot)

        pl.when(between(place))(lambda: act(send(low, place)))
        pl.when(jnp.logical_not(between(place)))(lambda: act(send(pl.ds(0, tok), place)))

    def late_cross(place):
        return copy(
            ACROSS, cross_out.at[place, high], cross.at[place, high], n_chip + place
        )

    def far_copy(way, place):
        target = far_up if way == ALONG_UP else far_down
        return copy(way, cross_out.at[place, high], target.at[place], n_chip + place)

    def up_copy(place):
        return copy(ALONG_UP, line_out.at[place], up_in.at[place], place)

    def down_copy(place):
        return copy(ALONG_DOWN, line_out.at[place], down_in.at[place], place)

    chunk = 32 if tok % 32 == 0 else tok

    def total(store, terms, start=0, stop=tok // chunk):
        def body(i, carry):
            at = pl.ds(pl.multiple_of(i * chunk, chunk), chunk)
            value = None
            for ref, slot, above in terms:
                rows_at = pl.ds(pl.multiple_of(i * chunk - above, chunk), chunk)
                term = ref[slot, rows_at, :].astype(jnp.float32)
                value = term if value is None else value + term
            store(at, value.astype(jnp.bfloat16))
            return carry

        lax.fori_loop(start, stop, body, 0)

    def to(ref, slot):
        def store(at, value):
            ref[slot, at, :] = value

        return store

    def to_out(at, value):
        in_ref[at, :] = value

    def pieces(column, place):
        def body(q, carry):
            core = jnp.where(q == 0, 1 - c, c)
            shard = (column * 2 + core) * n_chip + place
            part[shard] = jnp.dot(
                back[...], dense[shard], preferred_element_type=jnp.float32
            ).astype(jnp.bfloat16)
            pl.when(q == 0)(lambda: side_copy(column, place).start())
            return carry

        lax.fori_loop(0, 2, body, 0)

    def far_send(place):
        pl.when(z < place)(lambda: far_copy(ALONG_UP, place).start())
        pl.when(z > place)(lambda: far_copy(ALONG_DOWN, place).start())

    half_chunks = tok // 2 // chunk

    def far_step(place):
        terms = [(cross_out, place, 0)]
        upper, middle = (far_up, place, tok // 2), (far_down, place, tok // 2)

        @pl.when((z < place) & not_first)
        def _():
            far_copy(ALONG_UP, place).wait_recv()
            total(to(cross_out, place), terms + [upper], half_chunks, 2 * half_chunks)
            far_send(place)

        @pl.when((z > place) & not_last)
        def _():
            far_copy(ALONG_DOWN, place).wait_recv()
            total(to(cross_out, place), terms + [middle], half_chunks, 2 * half_chunks)
            far_send(place)

    def far_end():
        @pl.when(between(z))
        def _():
            far_copy(ALONG_UP, z).wait_recv()
            far_copy(ALONG_DOWN, z).wait_recv()
            terms = [(cross_out, z, 0), (far_up, z, tok // 2), (far_down, z, tok // 2)]
            total(to(cross_out, z), terms, half_chunks, 2 * half_chunks)
            late_cross(z).start()

    def piece_step(r, carry):
        @pl.when((r > 0) & (r <= n_chip))
        def _():
            place = place_of(n_chip - r)
            slot = (1 - y) * n_chip + place
            side_copy(1 - y, place).wait_recv()
            total(
                to(cross_out, place),
                [(part, ((1 - y) * 2 + c) * n_chip + place, 0), (side, slot, 0)],
            )
            cross_act(place, lambda d: d.start())
            ends = jnp.logical_or(
                (z < place) & jnp.logical_not(not_first), (z > place) & jnp.logical_not(not_last)
            )
            pl.when(between(place) & ends)(lambda: far_send(place))

        column = jnp.where(r < n_chip, 1 - y, y)
        pieces(column, place_of(n_chip - 1 - r % n_chip))
        return carry

    lax.fori_loop(0, n_chip + 2, piece_step, 0)

    for place in range(1, last):
        far_step(place)

    def line_step(place):
        slot = y * n_chip + place
        side_copy(y, place).wait_recv()
        cross_act(place, lambda d: d.wait_recv())
        pl.when((place == z) & between(place))(lambda: late_cross(place).wait_recv())
        full = jnp.where(between(place) & (place != z), half_chunks, tok // chunk)
        base = [(part, (y * 2 + c) * n_chip + place, 0), (side, slot, 0)]

        def sums(store, more):
            total(store, base + more + [(cross, place, 0)], 0, full)
            total(store, base + more, full, tok // chunk)

        @pl.when(place > z)
        def _():
            @pl.when(not_first)
            def _():
                up_copy(place).wait_recv()
                sums(to(line_out, place), [(up_in, place, 0)])

            @pl.when(jnp.logical_not(not_first))
            def _():
                sums(to(line_out, place), [])

            up_copy(place).start()

        @pl.when(place < z)
        def _():
            @pl.when(not_last)
            def _():
                down_copy(place).wait_recv()
                sums(to(line_out, place), [(down_in, place, 0)])

            @pl.when(jnp.logical_not(not_last))
            def _():
                sums(to(line_out, place), [])

            down_copy(place).start()

        @pl.when(place == z)
        def _():
            @pl.when(inner)
            def _():
                up_copy(place).wait_recv()
                down_copy(place).wait_recv()
                sums(to_out, [(up_in, place, 0), (down_in, place, 0)])

            @pl.when(jnp.logical_not(not_first))
            def _():
                down_copy(place).wait_recv()
                sums(to_out, [(down_in, place, 0)])

            @pl.when(jnp.logical_not(not_last))
            def _():
                up_copy(place).wait_recv()
                sums(to_out, [(up_in, place, 0)])

    cols, outs = (up_cols, down_cols), (up_ref, down_ref)
    step = 4 if count % 4 == 0 else 1

    def grad_row(a, left, source, j, add):
        for first in range(0, count, step):
            picked = [source(cols[a][j, k]) for k in range(first, first + step)]
            value = jnp.dot(
                left, jnp.concatenate(picked, axis=1), preferred_element_type=jnp.float32
            )
            for i in range(step):
                block = value[:, i * width : (i + 1) * width]
                if add:
                    outs[a][j, first + i] += block
                else:
                    outs[a][j, first + i] = block

    share = -(-rows // (n_chip - 1))

    def own_row(j, carry):
        for a in range(2):
            grad_row(a, lhs[a, dp, j], lambda col, a=a: own[a, col], j, False)
        return carry

    far_near = [(far, i) for i in range(3, n_chip) for far in range(2)]
    early = {0: [(far, i, 0) for far, i in far_near], 1: [(0, 1, 0), (1, 1, 0)]}
    if n_chip > 2:
        early[0] += [(1, 2, 0), (0, 2, 1), (1, 2, 1)]
    early[n_chip - 2] = early.get(n_chip - 2, []) + [(0, 1, 1), (1, 1, 1)]
    def line_loop(r, carry):
        line_step(place_of(n_chip - 1 - r))
        pl.when(r == 0)(far_end)
        pl.when(r + 2 < n_chip)(lambda: pieces(y, place_of(jnp.maximum(n_chip - 3 - r, 0))))
        for at, listed in early.items():

            @pl.when(r == at)
            def _():
                for far, i, a in listed:
                    service(far, i, a)

        lax.fori_loop(
            jnp.minimum(r * share, rows), jnp.minimum((r + 1) * share, rows), own_row, 0
        )
        return carry

    lax.fori_loop(0, n_chip, line_loop, 0)

    def other_row(j, carry):
        grad_row(0, left_x[j], lambda col: oth_x[col], j, True)
        return carry

    for a in range(2):
        if a == 1:
            for far, i in far_near:
                service(far, i, a)
        for far in range(2):
            for i in range(n_chip):
                o_copy(a, SIDE, shard_of(far, i, 1 - c), far * n_chip + i).wait_recv()
        l_copy(a).wait_recv()
        if a == 0:
            lax.fori_loop(0, rows, other_row, 0)

    def settle(n, carry):
        far, i, a = unit_of(n)
        own_ways(far, i, a, lambda d: d.wait_send())
        return carry

    lax.fori_loop(0, units, settle, 0)
    if n_chip > 2:
        cross_over().wait_send()
    late_ways(lambda d: d.wait_send())
    for a in range(2):
        for far in range(2):
            for i in range(n_chip):
                o_copy(a, SIDE, shard_of(far, i, c), far * n_chip + i).wait_send()
            o_copy(a, MATE, shard_of(far, 0, c), far * n_chip).wait_send()
        l_copy(a).wait_send()

    def settle_sum(place, carry):
        side_copy(1 - y, place).wait_send()
        side_copy(y, place).wait_send()
        cross_act(place, lambda d: d.wait_send())

        @pl.when(between(place))
        def _():
            pl.when(z < place)(lambda: far_copy(ALONG_UP, place).wait_send())
            pl.when(z > place)(lambda: far_copy(ALONG_DOWN, place).wait_send())
            pl.when(z == place)(lambda: late_cross(place).wait_send())

        pl.when(place > z)(lambda: up_copy(place).wait_send())
        pl.when(place < z)(lambda: down_copy(place).wait_send())
        return carry

    lax.fori_loop(0, n_chip, settle_sum, 0)


def finish_kernel(
    cols, in_held, up_held, down_held, other, left, in_out, up_out, down_out, sums, sems
):
    rows, count, _, width = sums.shape
    step = 4 if count % 4 == 0 else 1
    through = [
        pltpu.make_async_copy(in_held, in_out, sems.at[rows]),
        pltpu.make_async_copy(up_held, up_out, sems.at[rows + 1]),
    ]
    for m in through:
        m.start()

    def out_copy(j):
        return pltpu.make_async_copy(sums.at[j], down_out.at[j], sems.at[j])

    def row(j, carry):
        for first in range(0, count, step):
            picked = [other[cols[j, k]] for k in range(first, first + step)]
            value = jnp.dot(
                left[j], jnp.concatenate(picked, axis=1), preferred_element_type=jnp.float32
            )
            for i in range(step):
                block = value[:, i * width : (i + 1) * width]
                sums[j, first + i] = down_held[j, first + i] + block
        out_copy(j).start()
        return carry

    lax.fori_loop(0, rows, row, 0)
    for j in range(rows):
        out_copy(j).wait()
    for m in through:
        m.wait()


def fused_call(n_hst, n_chip, tokens, out_grad, up_blocks, up_cols, down_blocks, down_cols):
    rows, count, width, _ = up_blocks.shape
    tok, part = tokens.shape
    shards = n_hst * n_chip
    blocks = shards * part // width
    names = jnp.arange(blocks, dtype=jnp.int32)
    ranks = jnp.arange(count, dtype=jnp.int32)[None, None, :, None] - count
    cols = jnp.stack([up_cols, down_cols])
    hits = cols[:, :, :, None] == names
    inv = jnp.sum(jnp.where(hits, ranks, 0), axis=2, dtype=jnp.int32) + count
    hidden = rows * width
    bf, f32 = jnp.bfloat16, jnp.float32
    dma = pltpu.SemaphoreType.DMA
    whole = pl.BlockSpec(memory_space=pltpu.VMEM)
    smem = pl.BlockSpec(memory_space=pltpu.SMEM)
    anywhere = pl.BlockSpec(memory_space=pl.ANY)
    grads = jax.ShapeDtypeStruct((rows, count, width // 2, width), f32)

    def slots(amount):
        return pltpu.VMEM((amount, tok, part), bf)

    held = pl.pallas_call(
        functools.partial(fused_kernel, n_chip),
        in_specs=[smem] * 3 + [anywhere] * 4,
        out_specs=[whole] * 3 + [anywhere] * 2,
        out_shape=[
            pltpu.VMEM((tok, part), bf),
            pltpu.VMEM(grads.shape, f32),
            pltpu.VMEM(grads.shape, f32),
            pltpu.VMEM((blocks, tok, width), bf),
            pltpu.VMEM((rows, width // 2, tok), bf),
        ],
        scratch_shapes=[
            pltpu.VMEM((2, blocks, tok, width), bf),
            pltpu.VMEM((blocks, tok, width), bf),
            pltpu.VMEM((2, rows, count + 1, width, width), bf),
            pltpu.VMEM((shards + 1, hidden, part), bf),
            pltpu.VMEM((2, hidden, tok), f32),
            pltpu.VMEM((2, 2, rows, width // 2, tok), bf),
            pltpu.VMEM((rows, width // 2, tok), bf),
            pltpu.VMEM((tok, hidden), bf),
            slots(shards),
            slots(2 * n_chip),
        ]
        + [slots(n_chip)] * 5
        + [pltpu.VMEM((n_chip, tok // 2, part), bf)] * 2
        + [
            dma((2, 6, 2 * n_chip)),
            dma((2, shards)),
            dma((2, 3, 2 * n_chip)),
            dma((2, shards)),
            dma((2,)),
            dma((2,)),
            dma((4, 2 * n_chip)),
            dma((4, 2 * n_chip)),
            dma((2, part // width)),
            dma((2,)),
        ],
        compiler_params=pltpu.CompilerParams(
            collective_id=2, has_side_effects=True, vmem_limit_bytes=51 * 2**20
        ),
        cost_estimate=pl.CostEstimate(
            flops=22 * tok * hidden * shards * part // 4,
            bytes_accessed=20 * 2**20,
            transcendentals=hidden * tok,
        ),
    )(inv, up_cols, down_cols, tokens, out_grad, up_blocks, down_blocks)
    return pl.pallas_call(
        finish_kernel,
        in_specs=[smem] + [whole] * 5,
        out_specs=[anywhere] * 3,
        out_shape=[jax.ShapeDtypeStruct((tok, part), bf), grads, grads],
        scratch_shapes=[pltpu.VMEM(grads.shape, f32), dma((rows + 2,))],
        compiler_params=pltpu.CompilerParams(vmem_limit_bytes=24 * 2**20),
        cost_estimate=pl.CostEstimate(
            flops=2 * tok * hidden * count * width // 2,
            bytes_accessed=8 * 2**20,
            transcendentals=0,
        ),
    )(down_cols, *held)


def local(n_dp, n_hst, n_chip, tokens, out_grad, up_blocks, up_cols, down_blocks, down_cols):
    if n_dp == 2 and n_hst == 4 and n_chip >= 2 and n_chip % 2 == 0:
        return tuple(
            fused_call(
                n_hst, n_chip, tokens, out_grad, up_blocks, up_cols, down_blocks, down_cols
            )
        )
    whole_x, whole_dy = gather_call(n_hst, n_chip, tokens, out_grad)
    split = n_dp == 2
    partial_value, *grads = rows_call(
        split, whole_x, whole_dy, up_blocks, up_cols, down_blocks, down_cols
    )
    if split:
        swap = [(0, 1), (1, 0)]
        sums = [
            grads[i].astype(jnp.float32)
            + lax.ppermute(grads[i + 1], "dp", swap).astype(jnp.float32)
            for i in (0, 2)
        ]
    else:
        sums = [
            lax.psum_scatter(g, "dp", scatter_dimension=2, tiled=True).astype(jnp.float32)
            for g in grads
        ]
    summed = scatter_call(n_hst, n_chip, partial_value)
    return (summed, *sums)


def solution(mesh):
    placed = (
        P("dp", ("hst", "chip")),
        P("dp", ("hst", "chip")),
        P(("hst", "chip"), None, None, None),
        P(("hst", "chip"), None),
        P(("hst", "chip"), None, None, None),
        P(("hst", "chip"), None),
    )
    return jax.shard_map(
        functools.partial(local, mesh.shape["dp"], mesh.shape["hst"], mesh.shape["chip"]),
        mesh=mesh,
        in_specs=placed,
        out_specs=(
            P("dp", ("hst", "chip")),
            P(("hst", "chip"), None, "dp", None),
            P(("hst", "chip"), None, "dp", None),
        ),
        check_vma=False,
    )
```

```python
import functools

import jax
import jax.numpy as jnp
from jax import lax
from jax.experimental import pallas as pl
from jax.experimental.pallas import tpu as pltpu
from jax.sharding import PartitionSpec as P

NT = (((1,), (1,)), ((), ()))


def rows_kernel(
    split,
    up_cols,
    down_cols,
    me,
    x_ref,
    dy_ref,
    up_ref,
    down_ref,
    in_ref,
    *rest,
):
    outs, (acc, xs, dys, us, ds) = rest[:-5], rest[-5:]
    row = pl.program_id(0)
    width = up_ref.shape[-1]
    per_shard = x_ref.shape[2] // width
    count = up_ref.shape[1]

    @pl.when(row == 0)
    def _():
        acc[...] = jnp.zeros_like(acc)

    def place(col):
        return col // per_shard, pl.ds(pl.multiple_of((col % per_shard) * width, width), width)

    for k in range(count):
        lanes = pl.ds(k * width, width)
        shard, at = place(up_cols[row, k])
        xs[:, lanes] = x_ref[shard, :, at]
        shard, at = place(down_cols[row, k])
        dys[:, lanes] = dy_ref[shard, :, at]
        us[:, lanes] = up_ref[0, k]
        ds[:, lanes] = down_ref[0, k]
    pre = lax.dot_general(us[...], xs[...], NT, preferred_element_type=jnp.float32)
    hid = lax.dot_general(ds[...], dys[...], NT, preferred_element_type=jnp.float32)
    sig = 1.0 / (1.0 + jnp.exp(-pre))
    act = (pre * sig).astype(jnp.bfloat16)
    pre_grad_f = hid * sig * (1.0 + pre * (1.0 - sig))
    pre_grad = pre_grad_f.astype(jnp.bfloat16)
    pre_grad_t = pre_grad_f.T.astype(jnp.bfloat16)

    step = 4
    for base in range(0, count, step):
        lanes = pl.ds(base * width, step * width)
        up_part = jnp.dot(pre_grad, xs[:, lanes], preferred_element_type=jnp.float32)
        down_part = jnp.dot(act, dys[:, lanes], preferred_element_type=jnp.float32)
        back = jnp.dot(pre_grad_t, us[:, lanes], preferred_element_type=jnp.float32)
        for i in range(step):
            k = base + i
            cut = slice(i * width, (i + 1) * width)
            for part, out in ((up_part, outs[: len(outs) // 2]), (down_part, outs[len(outs) // 2 :])):
                block = part[:, cut].astype(jnp.bfloat16)
                if split:
                    half = width // 2
                    first = me[0] == 0
                    out[0][0, k] = jnp.where(first, block[:half], block[half:])
                    out[1][0, k] = jnp.where(first, block[half:], block[:half])
                else:
                    out[0][0, k] = block
            shard, at = place(up_cols[row, k])
            acc[shard, :, at] += back[:, cut]

    @pl.when(row == pl.num_programs(0) - 1)
    def _():
        for s in range(acc.shape[0]):
            in_ref[s] = acc[s].astype(jnp.bfloat16)


def rows_call(split, whole_x, whole_dy, up_blocks, up_cols, down_blocks, down_cols):
    rows, count, width, _ = up_blocks.shape
    shards, tok, part = whole_x.shape
    out_h = width // 2 if split else width
    n_out = 4 if split else 2
    whole = pl.BlockSpec(memory_space=pltpu.VMEM)
    smem = pl.BlockSpec(memory_space=pltpu.SMEM)

    def block(h):
        return pl.BlockSpec((1, count, h, width), lambda r: (r, 0, 0, 0))

    me = lax.axis_index("dp").astype(jnp.int32).reshape(1)
    flops = 10 * tok * rows * count * width * width
    return pl.pallas_call(
        functools.partial(rows_kernel, split),
        grid=(rows,),
        in_specs=[smem, smem, smem, whole, whole, block(width), block(width)],
        out_specs=[whole] + [block(out_h)] * n_out,
        out_shape=[jax.ShapeDtypeStruct(whole_x.shape, jnp.bfloat16)]
        + [jax.ShapeDtypeStruct((rows, count, out_h, width), jnp.bfloat16)] * n_out,
        scratch_shapes=[
            pltpu.VMEM(whole_x.shape, jnp.float32),
            pltpu.VMEM((tok, count * width), jnp.bfloat16),
            pltpu.VMEM((tok, count * width), jnp.bfloat16),
            pltpu.VMEM((width, count * width), jnp.bfloat16),
            pltpu.VMEM((width, count * width), jnp.bfloat16),
        ],
        compiler_params=pltpu.CompilerParams(
            dimension_semantics=("arbitrary",), vmem_limit_bytes=56 * 2**20
        ),
        cost_estimate=pl.CostEstimate(
            flops=flops, bytes_accessed=30 * 2**20, transcendentals=rows * width * tok
        ),
    )(up_cols, down_cols, me, whole_x, whole_dy, up_blocks, down_blocks)


MESH = pl.DeviceIdType.MESH
ALONG_UP, ALONG_DOWN, ACROSS, SIDE = range(4)


def gather_kernel(n_chip, x_ref, dy_ref, x_out, dy_out, send_sem, recv_sem, own_sem):
    hst, z = lax.axis_index("hst"), lax.axis_index("chip")
    far, c = hst // 2, hst % 2
    own = hst * n_chip + z
    ins, outs = (x_ref, dy_ref), (x_out, dy_out)
    not_last, not_first = z < n_chip - 1, z > 0
    peers = {
        ALONG_UP: {"hst": hst, "chip": (z + 1) % n_chip},
        ALONG_DOWN: {"hst": hst, "chip": (z + n_chip - 1) % n_chip},
        ACROSS: {"hst": (1 - far) * 2 + c, "chip": z},
        SIDE: {"hst": far * 2 + 1 - c, "chip": z},
    }

    barrier = pltpu.get_barrier_semaphore()

    def greet(way):
        pl.semaphore_signal(barrier, inc=1, device_id=peers[way], device_id_type=MESH)

    greet(ACROSS)
    greet(SIDE)
    pl.when(not_last)(lambda: greet(ALONG_UP))
    pl.when(not_first)(lambda: greet(ALONG_DOWN))
    inner = jnp.logical_and(not_last, not_first)
    pl.when(inner)(lambda: pl.semaphore_wait(barrier, 4))
    pl.when(jnp.logical_not(inner))(lambda: pl.semaphore_wait(barrier, 3))

    def copy(a, way, shard, source=None):
        return pltpu.make_async_remote_copy(
            src_ref=outs[a].at[shard] if source is None else source,
            dst_ref=outs[a].at[shard],
            send_sem=send_sem.at[a, way, shard],
            recv_sem=recv_sem.at[a, shard],
            device_id=peers[way],
            device_id_type=MESH,
        )

    def each(act):
        for t in range(n_chip + 1):
            for a in range(2):
                if t == 0:
                    act(a, (), own, None, True)
                elif t < n_chip:
                    below = z - t
                    act(a, (ALONG_UP,), hst * n_chip + below, below >= 0, False)
                    above = z + t
                    act(a, (ALONG_DOWN,), hst * n_chip + above, above < n_chip, False)
            for a in range(2):
                if t >= 1:
                    base = ((1 - far) * 2 + c) * n_chip
                    if t == 1:
                        act(a, None, base + z, None, False)
                    else:
                        act(a, None, base + z - (t - 1), z - (t - 1) >= 0, False)
                        act(a, None, base + z + (t - 1), z + (t - 1) < n_chip, False)

    def guarded(condition, run):
        if condition is None:
            run()
        else:
            pl.when(condition)(run)

    def forward(a, ways, shard, condition, is_own):
        def run():
            if not is_own:
                copy(a, SIDE, shard).wait_recv()
            source = ins[a] if is_own else None
            if ways is not None:
                if is_own or ALONG_UP in ways:
                    pl.when(not_last)(lambda: copy(a, ALONG_UP, shard, source).start())
                if is_own or ALONG_DOWN in ways:
                    pl.when(not_first)(lambda: copy(a, ALONG_DOWN, shard, source).start())
                copy(a, ACROSS, shard, source).start()
            copy(a, SIDE, shard, source).start()

        guarded(condition, run)

    def finish(a, ways, shard, condition, is_own):
        def run():
            source = ins[a] if is_own else None
            if ways is not None:
                if is_own or ALONG_UP in ways:
                    pl.when(not_last)(lambda: copy(a, ALONG_UP, shard, source).wait_send())
                if is_own or ALONG_DOWN in ways:
                    pl.when(not_first)(lambda: copy(a, ALONG_DOWN, shard, source).wait_send())
                copy(a, ACROSS, shard, source).wait_send()
            copy(a, SIDE, shard, source).wait_send()

        guarded(condition, run)

    each(forward)
    mine = [pltpu.make_async_copy(ins[a], outs[a].at[own], own_sem.at[a]) for a in range(2)]
    for m in mine:
        m.start()
    for half in range(2):
        for place in range(n_chip):
            for a in range(2):
                copy(a, SIDE, (half * 2 + 1 - c) * n_chip + place).wait_recv()
    each(finish)
    for m in mine:
        m.wait()


def gather_call(n_hst, n_chip, tokens, out_grad):
    if n_hst != 4:
        return [
            lax.all_gather(v, ("hst", "chip"), axis=0, tiled=False) for v in (tokens, out_grad)
        ]
    shards = n_hst * n_chip
    return pl.pallas_call(
        functools.partial(gather_kernel, n_chip),
        in_specs=[pl.BlockSpec(memory_space=pltpu.VMEM)] * 2,
        out_specs=[pl.BlockSpec(memory_space=pl.ANY)] * 2,
        out_shape=[jax.ShapeDtypeStruct((shards, *v.shape), v.dtype) for v in (tokens, out_grad)],
        scratch_shapes=[
            pltpu.SemaphoreType.DMA((2, 4, shards)),
            pltpu.SemaphoreType.DMA((2, shards)),
            pltpu.SemaphoreType.DMA((2,)),
        ],
        compiler_params=pltpu.CompilerParams(collective_id=0, has_side_effects=True),
    )(tokens, out_grad)


def scatter_kernel(n_chip, part, out, side, cross, up, down, cross_out, line_out, send_sem, recv_sem):
    hst, z = lax.axis_index("hst"), lax.axis_index("chip")
    far, c = hst // 2, hst % 2
    not_last, not_first = z < n_chip - 1, z > 0
    peers = {
        ALONG_UP: {"hst": hst, "chip": (z + 1) % n_chip},
        ALONG_DOWN: {"hst": hst, "chip": (z + n_chip - 1) % n_chip},
        ACROSS: {"hst": (1 - far) * 2 + c, "chip": z},
        SIDE: {"hst": far * 2 + 1 - c, "chip": z},
    }
    barrier = pltpu.get_barrier_semaphore()

    def greet(way):
        pl.semaphore_signal(barrier, inc=1, device_id=peers[way], device_id_type=MESH)

    greet(ACROSS)
    greet(SIDE)
    pl.when(not_last)(lambda: greet(ALONG_UP))
    pl.when(not_first)(lambda: greet(ALONG_DOWN))
    inner = jnp.logical_and(not_last, not_first)
    pl.when(inner)(lambda: pl.semaphore_wait(barrier, 4))
    pl.when(jnp.logical_not(inner))(lambda: pl.semaphore_wait(barrier, 3))

    def copy(way, source, target, slot):
        return pltpu.make_async_remote_copy(
            src_ref=source,
            dst_ref=target,
            send_sem=send_sem.at[way, slot],
            recv_sem=recv_sem.at[way, slot],
            device_id=peers[way],
            device_id_type=MESH,
        )

    def side_copy(half, place):
        slot = half * n_chip + place
        return copy(SIDE, part.at[(half * 2 + 1 - c) * n_chip + place], side.at[slot], slot)

    def cross_copy(place):
        return copy(ACROSS, cross_out.at[place], cross.at[place], place)

    def up_copy(place):
        return copy(ALONG_UP, line_out.at[place], up.at[place], place)

    def down_copy(place):
        return copy(ALONG_DOWN, line_out.at[place], down.at[place], place)

    def each(act):
        for t in range(n_chip - 1, 0, -1):
            pl.when(z + t < n_chip)(lambda t=t: act(z + t, 1))
            pl.when(z - t >= 0)(lambda t=t: act(z - t, -1))
        act(z, 0)

    rows = part.shape[1]
    chunk = 32 if rows % 32 == 0 else rows

    def total(store, terms):
        def body(i, carry):
            at = pl.ds(pl.multiple_of(i * chunk, chunk), chunk)
            value = None
            for ref, slot in terms:
                term = ref[slot, at, :].astype(jnp.float32)
                value = term if value is None else value + term
            store(at, value.astype(jnp.bfloat16))
            return carry

        lax.fori_loop(0, rows // chunk, body, 0)

    def to(ref, slot):
        def store(at, value):
            ref[slot, at, :] = value

        return store

    def to_out(at, value):
        out[at, :] = value

    each(lambda place, _: side_copy(1 - far, place).start())
    each(lambda place, _: side_copy(far, place).start())

    def cross_step(place, _):
        slot = (1 - far) * n_chip + place
        side_copy(1 - far, place).wait_recv()
        total(to(cross_out, place), [(part, ((1 - far) * 2 + c) * n_chip + place), (side, slot)])
        cross_copy(place).start()

    each(cross_step)

    def line_step(place, sign):
        slot = far * n_chip + place
        side_copy(far, place).wait_recv()
        cross_copy(place).wait_recv()
        base = [(part, (far * 2 + c) * n_chip + place), (side, slot), (cross, place)]
        if sign > 0:

            @pl.when(not_first)
            def _():
                up_copy(place).wait_recv()
                total(to(line_out, place), base + [(up, place)])

            @pl.when(jnp.logical_not(not_first))
            def _():
                total(to(line_out, place), base)

            up_copy(place).start()
        elif sign < 0:

            @pl.when(not_last)
            def _():
                down_copy(place).wait_recv()
                total(to(line_out, place), base + [(down, place)])

            @pl.when(jnp.logical_not(not_last))
            def _():
                total(to(line_out, place), base)

            down_copy(place).start()
        else:

            @pl.when(inner)
            def _():
                up_copy(place).wait_recv()
                down_copy(place).wait_recv()
                total(to_out, base + [(up, place), (down, place)])

            @pl.when(jnp.logical_not(not_first))
            def _():
                down_copy(place).wait_recv()
                total(to_out, base + [(down, place)])

            @pl.when(jnp.logical_not(not_last))
            def _():
                up_copy(place).wait_recv()
                total(to_out, base + [(up, place)])

    each(line_step)

    def finish(place, sign):
        side_copy(1 - far, place).wait_send()
        side_copy(far, place).wait_send()
        cross_copy(place).wait_send()
        if sign > 0:
            up_copy(place).wait_send()
        elif sign < 0:
            down_copy(place).wait_send()

    each(finish)


def scatter_call(n_hst, n_chip, part):
    if n_hst != 4 or n_chip < 2:
        return lax.psum_scatter(part, ("hst", "chip"), scatter_dimension=0, tiled=False)
    shards, rows, width = part.shape
    whole = pl.BlockSpec(memory_space=pltpu.VMEM)

    def slots(count):
        return pltpu.VMEM((count, rows, width), jnp.bfloat16)

    return pl.pallas_call(
        functools.partial(scatter_kernel, n_chip),
        in_specs=[whole],
        out_specs=whole,
        out_shape=jax.ShapeDtypeStruct((rows, width), jnp.bfloat16),
        scratch_shapes=[slots(2 * n_chip)]
        + [slots(n_chip)] * 5
        + [pltpu.SemaphoreType.DMA((4, 2 * n_chip))] * 2,
        compiler_params=pltpu.CompilerParams(
            collective_id=1, has_side_effects=True, vmem_limit_bytes=24 * 2**20
        ),
        cost_estimate=pl.CostEstimate(
            flops=shards * rows * width, bytes_accessed=120 * 2**20, transcendentals=0
        ),
    )(part)

PAIR, MATE = 4, 5


def fused_kernel(
    n_chip,
    inv,
    up_cols,
    down_cols,
    tokens,
    out_grad,
    up_hbm,
    down_hbm,
    in_ref,
    up_ref,
    down_ref,
    oth_dy,
    left_dy,
    own,
    oth_x,
    wts,
    dense,
    pre,
    lhs,
    left_x,
    back,
    part,
    side,
    cross,
    cross_out,
    up_in,
    down_in,
    line_out,
    far_up,
    far_down,
    g_send,
    g_recv,
    o_send,
    o_recv,
    l_send,
    l_recv,
    s_send,
    s_recv,
    own_sem,
    w_sem,
):
    dp, hst, z = lax.axis_index("dp"), lax.axis_index("hst"), lax.axis_index("chip")
    y, c = hst // 2, hst % 2
    _, rows, count_1, width, _ = wts.shape
    count = count_1 - 1
    tok = back.shape[0]
    shards = dense.shape[0] - 1
    per = dense.shape[2] // width
    half = width // 2
    events = 2 * n_chip
    not_last, not_first = z < n_chip - 1, z > 0
    inner = jnp.logical_and(not_last, not_first)
    toward = 1 - 2 * (z % 2)
    peers = {
        ALONG_UP: {"dp": dp, "hst": hst, "chip": (z + 1) % n_chip},
        ALONG_DOWN: {"dp": dp, "hst": hst, "chip": (z + n_chip - 1) % n_chip},
        ACROSS: {"dp": dp, "hst": (1 - y) * 2 + c, "chip": z},
        SIDE: {"dp": dp, "hst": y * 2 + 1 - c, "chip": z},
        PAIR: {"dp": 1 - dp, "hst": hst, "chip": z},
        MATE: {"dp": dp, "hst": hst, "chip": z + toward},
    }
    ins, oth = (tokens, out_grad), (oth_x, oth_dy)
    mine = hst * n_chip + z

    def blocks_of(shard):
        return pl.ds(shard * per, per)

    locals_ = [
        pltpu.make_async_copy(
            ins[a].at[:, pl.ds(b * width, width)], own.at[a, mine * per + b], own_sem.at[a, b]
        )
        for a in range(2)
        for b in range(per)
    ]
    weights = [
        pltpu.make_async_copy(w, wts.at[a, :, pl.ds(0, count)], w_sem.at[a])
        for a, w in enumerate((up_hbm, down_hbm))
    ]
    for m in locals_ + weights:
        m.start()

    barrier = pltpu.get_barrier_semaphore()

    def greet(way):
        pl.semaphore_signal(barrier, inc=1, device_id=peers[way], device_id_type=MESH)

    for way in (ACROSS, SIDE, PAIR):
        greet(way)
    pl.when(not_last)(lambda: greet(ALONG_UP))
    pl.when(not_first)(lambda: greet(ALONG_DOWN))
    pl.when(inner)(lambda: pl.semaphore_wait(barrier, 5))
    pl.when(jnp.logical_not(inner))(lambda: pl.semaphore_wait(barrier, 4))

    for m in locals_:
        m.wait()

    short = jnp.minimum(z, n_chip - 1 - z)

    def place_of(i):
        both = z + toward * (2 * (i % 2) - 1) * ((i + 1) // 2)
        return jnp.where(i <= 2 * short, both, jnp.where(2 * z < n_chip - 1, i, n_chip - 1 - i))

    last = n_chip - 1
    order = [(0, 0, 0), (0, 0, 1)]
    for i in range(1, n_chip):
        order += [(0, i, 0), (1, i - 1, 0), (0, i, 1), (1, i - 1, 1)]
    order += [(1, last, 1), (1, last, 0)]
    units = len(order)

    def pick(n, values):
        found = values[0]
        for m in range(1, len(values)):
            found = jnp.where(n == m, values[m], found)
        return found

    def unit_of(n):
        return tuple(pick(n, [u[m] for u in order]) for m in range(3))

    def shard_of(far, i, core):
        column = far * (1 - y) + (1 - far) * y
        return (column * 2 + core) * n_chip + place_of(i)

    def g_copy(a, way, shard, slot):
        return pltpu.make_async_remote_copy(
            src_ref=own.at[a, blocks_of(shard)],
            dst_ref=own.at[a, blocks_of(shard)],
            send_sem=g_send.at[a, way, slot],
            recv_sem=g_recv.at[a, shard],
            device_id=peers[way],
            device_id_type=MESH,
        )

    def x_copy(a, shard, slot):
        return pltpu.make_async_remote_copy(
            src_ref=own.at[a, blocks_of(shard)],
            dst_ref=oth[a].at[blocks_of(shard)],
            send_sem=g_send.at[a, PAIR, slot],
            recv_sem=o_recv.at[a, shard],
            device_id=peers[PAIR],
            device_id_type=MESH,
        )

    def o_copy(a, way, shard, slot):
        return pltpu.make_async_remote_copy(
            src_ref=oth[a].at[blocks_of(shard)],
            dst_ref=oth[a].at[blocks_of(shard)],
            send_sem=o_send.at[a, (SIDE, MATE, ACROSS).index(way), slot],
            recv_sem=o_recv.at[a, shard],
            device_id=peers[way],
            device_id_type=MESH,
        )

    def own_ways(far, i, a, act):
        place, shard, slot = place_of(i), shard_of(far, i, c), far * n_chip + i
        near = far == 0
        lined = (a == 1) & ((place == 0) | (place == last))
        along = near | lined
        act(g_copy(a, SIDE, shard, slot))
        pl.when(along & (place <= z) & not_last)(lambda: act(g_copy(a, ALONG_UP, shard, slot)))
        pl.when(along & (place >= z) & not_first)(lambda: act(g_copy(a, ALONG_DOWN, shard, slot)))
        across = near & (jnp.logical_not(lined) | (place == z))
        pl.when(across)(lambda: act(g_copy(a, ACROSS, shard, slot)))
        crossed = (far == 1) & (i == 2)
        pl.when((a == 0) & (i != 1) & jnp.logical_not(crossed))(lambda: act(x_copy(0, shard, slot)))
        pl.when((a == 1) & ((i == 0) | (i == 2)))(lambda: act(x_copy(1, shard, slot)))

    def assemble(a, shard, to):
        for j in range(rows):
            for b in range(per):
                dense[to, j * width : (j + 1) * width, b * width : (b + 1) * width] = wts[
                    a, j, inv[a, j, shard * per + b] + count
                ]

    def service(far, i, a):
        shard, slot = shard_of(far, i, c), far * n_chip + i
        o_copy(a, SIDE, shard, slot).wait_recv()
        o_copy(a, SIDE, shard, slot).start()

    def mate_service(far, a):
        o_copy(a, MATE, shard_of(far, 0, c), far * n_chip).start()

    def cross_over():
        return o_copy(0, ACROSS, shard_of(0, 2, c), 2)

    def gather_step(n, carry):
        @pl.when(n < units)
        def _():
            far, i, a = unit_of(n)
            pl.when(n > 1)(lambda: g_copy(a, SIDE, shard_of(far, i, c), 0).wait_recv())
            own_ways(far, i, a, lambda d: d.start())

        for far, at in ((0, units // 2 - 1), (1, units - 5)):

            @pl.when(n == at)
            def _():
                for a in range(2):
                    service(far, 0, a)
                    pl.when(jnp.logical_not(inner))(lambda: mate_service(far, a))

        if n_chip > 2:

            @pl.when(n == units - 1)
            def _():
                service(0, 2, 0)
                cross_over().start()

        @pl.when(n == 0)
        def _():
            for m in weights:
                m.wait()
            for a in range(2):
                wts[a, :, count] = jnp.zeros((rows, width, width), wts.dtype)
            pre[...] = jnp.zeros_like(pre)

        def unit(sib, carry):
            now = n - sib

            @pl.when((now >= 0) & (now < units))
            def _():
                far, i, a = unit_of(now)
                shard = shard_of(far, i, jnp.where(sib == 1, 1 - c, c))
                pl.when(sib == 1)(lambda: g_copy(a, SIDE, shard, 0).wait_recv())
                to = jnp.where(a == 0, shard, shards)
                assemble(a, shard, to)
                taken = [own[a, shard * per + b] for b in range(per)]
                pre[a] += lax.dot_general(
                    dense[to],
                    jnp.concatenate(taken, axis=1),
                    NT,
                    preferred_element_type=jnp.float32,
                )

            return carry

        lax.fori_loop(0, 2, unit, 0)
        return carry

    lax.fori_loop(0, units + 1, gather_step, 0)

    def gates(j, carry):
        at = pl.ds(pl.multiple_of(j * width, width), width)
        p, h = pre[0, at, :], pre[1, at, :]
        sig = 1.0 / (1.0 + jnp.exp(-p))
        act = (p * sig).astype(jnp.bfloat16)
        grad_f = h * sig * (1.0 + p * (1.0 - sig))
        grad = grad_f.astype(jnp.bfloat16)
        for f in range(2):
            lhs[0, f, j] = grad[f * half : (f + 1) * half]
            lhs[1, f, j] = act[f * half : (f + 1) * half]
        back[:, at] = grad_f.T.astype(jnp.bfloat16)
        return carry

    lax.fori_loop(0, rows, gates, 0)

    def l_copy(a):
        return pltpu.make_async_remote_copy(
            src_ref=lhs.at[a, 1 - dp],
            dst_ref=(left_x, left_dy)[a],
            send_sem=l_send.at[a],
            recv_sem=l_recv.at[a],
            device_id=peers[PAIR],
            device_id_type=MESH,
        )

    def late_ways(act):
        for i in range(3, n_chip):
            for far in range(2):
                act(x_copy(1, shard_of(far, i, c), far * n_chip + i))

    l_copy(0).start()
    l_copy(1).start()
    late_ways(lambda d: d.start())

    @pl.when(inner)
    def _():
        for a in range(2):
            for far in range(2):
                mate_service(far, a)

    def copy(way, source, target, slot):
        return pltpu.make_async_remote_copy(
            src_ref=source,
            dst_ref=target,
            send_sem=s_send.at[way, slot],
            recv_sem=s_recv.at[way, slot],
            device_id=peers[way],
            device_id_type=MESH,
        )

    def side_copy(column, place):
        slot = column * n_chip + place
        return copy(SIDE, part.at[(column * 2 + 1 - c) * n_chip + place], side.at[slot], slot)

    def between(place):
        return (place > 0) & (place < last)

    low, high = pl.ds(0, tok // 2), pl.ds(tok // 2, tok // 2)

    def cross_act(place, act):
        def send(at, slot):
            return copy(ACROSS, cross_out.at[place, at], cross.at[place, at], slot)

        pl.when(between(place))(lambda: act(send(low, place)))
        pl.when(jnp.logical_not(between(place)))(lambda: act(send(pl.ds(0, tok), place)))

    def late_cross(place):
        return copy(
            ACROSS, cross_out.at[place, high], cross.at[place, high], n_chip + place
        )

    def far_copy(way, place):
        target = far_up if way == ALONG_UP else far_down
        return copy(way, cross_out.at[place, high], target.at[place], n_chip + place)

    def up_copy(place):
        return copy(ALONG_UP, line_out.at[place], up_in.at[place], place)

    def down_copy(place):
        return copy(ALONG_DOWN, line_out.at[place], down_in.at[place], place)

    chunk = 32 if tok % 32 == 0 else tok

    def total(store, terms, start=0, stop=tok // chunk):
        def body(i, carry):
            at = pl.ds(pl.multiple_of(i * chunk, chunk), chunk)
            value = None
            for ref, slot, above in terms:
                rows_at = pl.ds(pl.multiple_of(i * chunk - above, chunk), chunk)
                term = ref[slot, rows_at, :].astype(jnp.float32)
                value = term if value is None else value + term
            store(at, value.astype(jnp.bfloat16))
            return carry

        lax.fori_loop(start, stop, body, 0)

    def to(ref, slot):
        def store(at, value):
            ref[slot, at, :] = value

        return store

    def to_out(at, value):
        in_ref[at, :] = value

    def pieces(column, place):
        def body(q, carry):
            core = jnp.where(q == 0, 1 - c, c)
            shard = (column * 2 + core) * n_chip + place
            part[shard] = jnp.dot(
                back[...], dense[shard], preferred_element_type=jnp.float32
            ).astype(jnp.bfloat16)
            pl.when(q == 0)(lambda: side_copy(column, place).start())
            return carry

        lax.fori_loop(0, 2, body, 0)

    def far_send(place):
        pl.when(z < place)(lambda: far_copy(ALONG_UP, place).start())
        pl.when(z > place)(lambda: far_copy(ALONG_DOWN, place).start())

    half_chunks = tok // 2 // chunk

    def far_step(place):
        terms = [(cross_out, place, 0)]
        upper, middle = (far_up, place, tok // 2), (far_down, place, tok // 2)

        @pl.when((z < place) & not_first)
        def _():
            far_copy(ALONG_UP, place).wait_recv()
            total(to(cross_out, place), terms + [upper], half_chunks, 2 * half_chunks)
            far_send(place)

        @pl.when((z > place) & not_last)
        def _():
            far_copy(ALONG_DOWN, place).wait_recv()
            total(to(cross_out, place), terms + [middle], half_chunks, 2 * half_chunks)
            far_send(place)

    def far_end():
        @pl.when(between(z))
        def _():
            far_copy(ALONG_UP, z).wait_recv()
            far_copy(ALONG_DOWN, z).wait_recv()
            terms = [(cross_out, z, 0), (far_up, z, tok // 2), (far_down, z, tok // 2)]
            total(to(cross_out, z), terms, half_chunks, 2 * half_chunks)
            late_cross(z).start()

    def piece_step(r, carry):
        @pl.when((r > 0) & (r <= n_chip))
        def _():
            place = place_of(n_chip - r)
            slot = (1 - y) * n_chip + place
            side_copy(1 - y, place).wait_recv()
            total(
                to(cross_out, place),
                [(part, ((1 - y) * 2 + c) * n_chip + place, 0), (side, slot, 0)],
            )
            cross_act(place, lambda d: d.start())
            ends = jnp.logical_or(
                (z < place) & jnp.logical_not(not_first), (z > place) & jnp.logical_not(not_last)
            )
            pl.when(between(place) & ends)(lambda: far_send(place))

        column = jnp.where(r < n_chip, 1 - y, y)
        pieces(column, place_of(n_chip - 1 - r % n_chip))
        return carry

    lax.fori_loop(0, n_chip + 2, piece_step, 0)

    for place in range(1, last):
        far_step(place)

    def line_step(place):
        slot = y * n_chip + place
        side_copy(y, place).wait_recv()
        cross_act(place, lambda d: d.wait_recv())
        pl.when((place == z) & between(place))(lambda: late_cross(place).wait_recv())
        full = jnp.where(between(place) & (place != z), half_chunks, tok // chunk)
        base = [(part, (y * 2 + c) * n_chip + place, 0), (side, slot, 0)]

        def sums(store, more):
            total(store, base + more + [(cross, place, 0)], 0, full)
            total(store, base + more, full, tok // chunk)

        @pl.when(place > z)
        def _():
            @pl.when(not_first)
            def _():
                up_copy(place).wait_recv()
                sums(to(line_out, place), [(up_in, place, 0)])

            @pl.when(jnp.logical_not(not_first))
            def _():
                sums(to(line_out, place), [])

            up_copy(place).start()

        @pl.when(place < z)
        def _():
            @pl.when(not_last)
            def _():
                down_copy(place).wait_recv()
                sums(to(line_out, place), [(down_in, place, 0)])

            @pl.when(jnp.logical_not(not_last))
            def _():
                sums(to(line_out, place), [])

            down_copy(place).start()

        @pl.when(place == z)
        def _():
            @pl.when(inner)
            def _():
                up_copy(place).wait_recv()
                down_copy(place).wait_recv()
                sums(to_out, [(up_in, place, 0), (down_in, place, 0)])

            @pl.when(jnp.logical_not(not_first))
            def _():
                down_copy(place).wait_recv()
                sums(to_out, [(down_in, place, 0)])

            @pl.when(jnp.logical_not(not_last))
            def _():
                up_copy(place).wait_recv()
                sums(to_out, [(up_in, place, 0)])

    cols, outs = (up_cols, down_cols), (up_ref, down_ref)
    step = 4 if count % 4 == 0 else 1

    def grad_row(a, left, source, j, add):
        for first in range(0, count, step):
            picked = [source(cols[a][j, k]) for k in range(first, first + step)]
            value = jnp.dot(
                left, jnp.concatenate(picked, axis=1), preferred_element_type=jnp.float32
            )
            for i in range(step):
                block = value[:, i * width : (i + 1) * width]
                if add:
                    outs[a][j, first + i] += block
                else:
                    outs[a][j, first + i] = block

    share = -(-rows // (n_chip - 1))

    def own_row(j, carry):
        for a in range(2):
            grad_row(a, lhs[a, dp, j], lambda col, a=a: own[a, col], j, False)
        return carry

    far_near = [(far, i) for i in range(3, n_chip) for far in range(2)]
    early = {0: [(far, i, 0) for far, i in far_near], 1: [(0, 1, 0), (1, 1, 0)]}
    if n_chip > 2:
        early[0] += [(1, 2, 0), (0, 2, 1), (1, 2, 1)]
    early[n_chip - 2] = early.get(n_chip - 2, []) + [(0, 1, 1), (1, 1, 1)]
    def line_loop(r, carry):
        line_step(place_of(n_chip - 1 - r))
        pl.when(r == 0)(far_end)
        pl.when(r + 2 < n_chip)(lambda: pieces(y, place_of(jnp.maximum(n_chip - 3 - r, 0))))
        for at, listed in early.items():

            @pl.when(r == at)
            def _():
                for far, i, a in listed:
                    service(far, i, a)

        lax.fori_loop(
            jnp.minimum(r * share, rows), jnp.minimum((r + 1) * share, rows), own_row, 0
        )
        return carry

    lax.fori_loop(0, n_chip, line_loop, 0)

    def other_row(j, carry):
        grad_row(0, left_x[j], lambda col: oth_x[col], j, True)
        return carry

    for a in range(2):
        if a == 1:
            for far, i in far_near:
                service(far, i, a)
        for far in range(2):
            for i in range(n_chip):
                o_copy(a, SIDE, shard_of(far, i, 1 - c), far * n_chip + i).wait_recv()
        l_copy(a).wait_recv()
        if a == 0:
            lax.fori_loop(0, rows, other_row, 0)

    def settle(n, carry):
        far, i, a = unit_of(n)
        own_ways(far, i, a, lambda d: d.wait_send())
        return carry

    lax.fori_loop(0, units, settle, 0)
    if n_chip > 2:
        cross_over().wait_send()
    late_ways(lambda d: d.wait_send())
    for a in range(2):
        for far in range(2):
            for i in range(n_chip):
                o_copy(a, SIDE, shard_of(far, i, c), far * n_chip + i).wait_send()
            o_copy(a, MATE, shard_of(far, 0, c), far * n_chip).wait_send()
        l_copy(a).wait_send()

    def settle_sum(place, carry):
        side_copy(1 - y, place).wait_send()
        side_copy(y, place).wait_send()
        cross_act(place, lambda d: d.wait_send())

        @pl.when(between(place))
        def _():
            pl.when(z < place)(lambda: far_copy(ALONG_UP, place).wait_send())
            pl.when(z > place)(lambda: far_copy(ALONG_DOWN, place).wait_send())
            pl.when(z == place)(lambda: late_cross(place).wait_send())

        pl.when(place > z)(lambda: up_copy(place).wait_send())
        pl.when(place < z)(lambda: down_copy(place).wait_send())
        return carry

    lax.fori_loop(0, n_chip, settle_sum, 0)


def finish_kernel(
    cols, in_held, up_held, down_held, other, left, in_out, up_out, down_out, sums, sems
):
    rows, count, _, width = sums.shape
    step = 4 if count % 4 == 0 else 1
    through = [
        pltpu.make_async_copy(in_held, in_out, sems.at[rows]),
        pltpu.make_async_copy(up_held, up_out, sems.at[rows + 1]),
    ]
    for m in through:
        m.start()

    def out_copy(j):
        return pltpu.make_async_copy(sums.at[j], down_out.at[j], sems.at[j])

    def row(j, carry):
        for first in range(0, count, step):
            picked = [other[cols[j, k]] for k in range(first, first + step)]
            value = jnp.dot(
                left[j], jnp.concatenate(picked, axis=1), preferred_element_type=jnp.float32
            )
            for i in range(step):
                block = value[:, i * width : (i + 1) * width]
                sums[j, first + i] = down_held[j, first + i] + block
        out_copy(j).start()
        return carry

    lax.fori_loop(0, rows, row, 0)
    for j in range(rows):
        out_copy(j).wait()
    for m in through:
        m.wait()


def fused_call(n_hst, n_chip, tokens, out_grad, up_blocks, up_cols, down_blocks, down_cols):
    rows, count, width, _ = up_blocks.shape
    tok, part = tokens.shape
    shards = n_hst * n_chip
    blocks = shards * part // width
    names = jnp.arange(blocks, dtype=jnp.int32)
    ranks = jnp.arange(count, dtype=jnp.int32)[None, None, :, None] - count
    cols = jnp.stack([up_cols, down_cols])
    hits = cols[:, :, :, None] == names
    inv = jnp.sum(jnp.where(hits, ranks, 0), axis=2, dtype=jnp.int32)
    hidden = rows * width
    bf, f32 = jnp.bfloat16, jnp.float32
    dma = pltpu.SemaphoreType.DMA
    whole = pl.BlockSpec(memory_space=pltpu.VMEM)
    smem = pl.BlockSpec(memory_space=pltpu.SMEM)
    anywhere = pl.BlockSpec(memory_space=pl.ANY)
    grads = jax.ShapeDtypeStruct((rows, count, width // 2, width), f32)

    def slots(amount):
        return pltpu.VMEM((amount, tok, part), bf)

    held = pl.pallas_call(
        functools.partial(fused_kernel, n_chip),
        in_specs=[smem] * 3 + [anywhere] * 4,
        out_specs=[whole] * 3 + [anywhere] * 2,
        out_shape=[
            pltpu.VMEM((tok, part), bf),
            pltpu.VMEM(grads.shape, f32),
            pltpu.VMEM(grads.shape, f32),
            pltpu.VMEM((blocks, tok, width), bf),
            pltpu.VMEM((rows, width // 2, tok), bf),
        ],
        scratch_shapes=[
            pltpu.VMEM((2, blocks, tok, width), bf),
            pltpu.VMEM((blocks, tok, width), bf),
            pltpu.VMEM((2, rows, count + 1, width, width), bf),
            pltpu.VMEM((shards + 1, hidden, part), bf),
            pltpu.VMEM((2, hidden, tok), f32),
            pltpu.VMEM((2, 2, rows, width // 2, tok), bf),
            pltpu.VMEM((rows, width // 2, tok), bf),
            pltpu.VMEM((tok, hidden), bf),
            slots(shards),
            slots(2 * n_chip),
        ]
        + [slots(n_chip)] * 5
        + [pltpu.VMEM((n_chip, tok // 2, part), bf)] * 2
        + [
            dma((2, 6, 2 * n_chip)),
            dma((2, shards)),
            dma((2, 3, 2 * n_chip)),
            dma((2, shards)),
            dma((2,)),
            dma((2,)),
            dma((4, 2 * n_chip)),
            dma((4, 2 * n_chip)),
            dma((2, part // width)),
            dma((2,)),
        ],
        compiler_params=pltpu.CompilerParams(
            collective_id=2, has_side_effects=True, vmem_limit_bytes=51 * 2**20
        ),
        cost_estimate=pl.CostEstimate(
            flops=22 * tok * hidden * shards * part // 4,
            bytes_accessed=20 * 2**20,
            transcendentals=hidden * tok,
        ),
    )(inv, up_cols, down_cols, tokens, out_grad, up_blocks, down_blocks)
    return pl.pallas_call(
        finish_kernel,
        in_specs=[smem] + [whole] * 5,
        out_specs=[anywhere] * 3,
        out_shape=[jax.ShapeDtypeStruct((tok, part), bf), grads, grads],
        scratch_shapes=[pltpu.VMEM(grads.shape, f32), dma((rows + 2,))],
        compiler_params=pltpu.CompilerParams(vmem_limit_bytes=24 * 2**20),
        cost_estimate=pl.CostEstimate(
            flops=2 * tok * hidden * count * width // 2,
            bytes_accessed=8 * 2**20,
            transcendentals=0,
        ),
    )(down_cols, *held)


def local(n_dp, n_hst, n_chip, tokens, out_grad, up_blocks, up_cols, down_blocks, down_cols):
    if n_dp == 2 and n_hst == 4 and n_chip >= 2 and n_chip % 2 == 0:
        return tuple(
            fused_call(
                n_hst, n_chip, tokens, out_grad, up_blocks, up_cols, down_blocks, down_cols
            )
        )
    whole_x, whole_dy = gather_call(n_hst, n_chip, tokens, out_grad)
    split = n_dp == 2
    partial_value, *grads = rows_call(
        split, whole_x, whole_dy, up_blocks, up_cols, down_blocks, down_cols
    )
    if split:
        swap = [(0, 1), (1, 0)]
        sums = [
            grads[i].astype(jnp.float32)
            + lax.ppermute(grads[i + 1], "dp", swap).astype(jnp.float32)
            for i in (0, 2)
        ]
    else:
        sums = [
            lax.psum_scatter(g, "dp", scatter_dimension=2, tiled=True).astype(jnp.float32)
            for g in grads
        ]
    summed = scatter_call(n_hst, n_chip, partial_value)
    return (summed, *sums)


def solution(mesh):
    placed = (
        P("dp", ("hst", "chip")),
        P("dp", ("hst", "chip")),
        P(("hst", "chip"), None, None, None),
        P(("hst", "chip"), None),
        P(("hst", "chip"), None, None, None),
        P(("hst", "chip"), None),
    )
    return jax.shard_map(
        functools.partial(local, mesh.shape["dp"], mesh.shape["hst"], mesh.shape["chip"]),
        mesh=mesh,
        in_specs=placed,
        out_specs=(
            P("dp", ("hst", "chip")),
            P(("hst", "chip"), None, "dp", None),
            P(("hst", "chip"), None, "dp", None),
        ),
        check_vma=False,
    )
```
